32 devices in a mesh: dp: 4 (over z), seq: 4 (over x, core), mp: 2 (over y).
Axes of the slice: x: 2, y: 2, z: 4, core: 2. Of those that a mesh axis runs over, the one named last changes fastest.
Arguments:
- hidden: bfloat16 [2, 4, 2048, 2048], P(None, 'dp', 'seq'), may hold values from -6 to 6
- w_query: bfloat16 [2048, 2048], P(('dp', 'seq'), 'mp'), may hold values from -0.125 to 0.125
- w_key: bfloat16 [2048, 1024], P(('dp', 'seq'), 'mp'), may hold values from -0.125 to 0.125
- w_value: bfloat16 [2048, 1024], P(('dp', 'seq'), 'mp'), may hold values from -0.125 to 0.125
- w_out: bfloat16 [2048, 2048], P('mp', ('dp', 'seq')), may hold values from -0.75 to 0.75
- w_gate: bfloat16 [2048, 6144], P(('dp', 'seq'), 'mp'), may hold values from -0.125 to 0.125
- w_up: bfloat16 [2048, 6144], P(('dp', 'seq'), 'mp'), may hold values from -0.125 to 0.125
- w_down: bfloat16 [6144, 2048], P('mp', ('dp', 'seq')), may hold values from -0.078125 to 0.078125
- norm_attn: bfloat16 [2048], P(('dp', 'seq')), may hold values from 0.25 to 1.75
- norm_ffn: bfloat16 [2048], P(('dp', 'seq')), may hold values from 0.25 to 1.75
- norm_query: bfloat16 [128], replicated, may hold values from 0.25 to 1.75
- norm_key: bfloat16 [128], replicated, may hold values from 0.25 to 1.75
- segments: int32 [2, 4, 2048], P(None, 'dp', 'seq'), may hold values from 0 to 7, as said below
- positions: int32 [2, 4, 2048], P(None, 'dp', 'seq'), may hold values from 0 to 2047, as said below
- cotangent: bfloat16 [2, 4, 2048, 2048], P(None, 'dp', 'seq'), may hold values from -6 to 6
Outputs:
- layer_out: bfloat16 [2, 4, 2048, 2048], P(None, 'dp', 'seq')
- grad_hidden: bfloat16 [2, 4, 2048, 2048], P(None, 'dp', 'seq')
- grad_query: float32 [2048, 2048], P(('dp', 'seq'), 'mp')
- grad_key: float32 [2048, 1024], P(('dp', 'seq'), 'mp')
- grad_value: float32 [2048, 1024], P(('dp', 'seq'), 'mp')
- grad_out: float32 [2048, 2048], P('mp', ('dp', 'seq'))
- grad_gate: float32 [2048, 6144], P(('dp', 'seq'), 'mp')
- grad_up: float32 [2048, 6144], P(('dp', 'seq'), 'mp')
- grad_down: float32 [6144, 2048], P('mp', ('dp', 'seq'))
- grad_norm_attn: float32 [2048], P(('dp', 'seq'))
- grad_norm_ffn: float32 [2048], P(('dp', 'seq'))
- grad_norm_query: float32 [128], replicated
- grad_norm_key: float32 [128], replicated
The draws below stay inside these ranges and needn't reach their ends.
Inputs may be any that keep to these rules, and one draw needn't show every extreme that they name: `segments`: along each sequence the segment numbers never fall and start at 0; a document is a run of equal numbers, and document lengths are heavy-tailed. One sequence is a single document. `positions`: each token's position counts up by one from 0 at the first token of its document.
All inputs are finite; a program needn't handle non-finite values.
Results may differ from the reference program's by a relative error of at most 0.025.
Values may be sent and summed in bfloat16 or wider, within the bound.
No kernel may reach another device: no remote copies, remote signals or barrier semaphores. Data moves between devices by JAX's collectives and lax.ppermute only.
A program may use at most 384 MiB of HBM per device.

```python
import jax
import jax.numpy as jnp
from jax import lax

D = 2048
HEADS = 16
KV_HEADS = 8
HEAD = 128
FF = 6144
MICRO = 2
NDOC = 8
BATCH = 4
LEN = 2048


def doc_layout(key):
    count = MICRO * BATCH
    picks = jax.random.randint(jax.random.fold_in(key, 7), (count, NDOC), 0, 64)
    weights_doc = 4096 // (picks + 1)
    ends = jnp.cumsum(weights_doc, axis=1) * LEN // jnp.sum(weights_doc, axis=1, keepdims=True)
    token_ids = jnp.arange(LEN, dtype=jnp.int32)
    seg_ids = jnp.sum((token_ids[None, :, None] >= ends[:, None, :]).astype(jnp.int32), axis=2)
    row_ids = jnp.arange(count, dtype=jnp.int32)
    seg_ids = jnp.where(row_ids[:, None] == 0, 0, seg_ids)
    starts = jnp.concatenate([jnp.zeros((count, 1), jnp.int32), ends[:, :-1]], axis=1)
    starts = jnp.where(row_ids[:, None] == 0, 0, starts)
    slot_ids = jnp.arange(NDOC, dtype=jnp.int32)
    start_of = jnp.sum(jnp.where(seg_ids[:, :, None] == slot_ids[None, None, :], starts[:, None, :], 0), axis=2)
    pos_ids = token_ids[None, :] - start_of
    return (seg_ids.astype(jnp.int32).reshape(MICRO, BATCH, LEN), pos_ids.astype(jnp.int32).reshape(MICRO, BATCH, LEN))


def draw_segments(key, part):
    return doc_layout(key)[0]


def draw_positions(key, part):
    return doc_layout(key)[1]


def block_levels(key, dims, pieces, low, high):
    factor_of = 1.0
    for dim, shards_of in pieces:
        heights = jax.random.uniform(jax.random.fold_in(jax.random.fold_in(key, 6), dim), (shards_of,), jnp.float32, low / len(pieces), high / len(pieces))
        factor_of = factor_of * jnp.repeat(jnp.exp(heights), dims[dim] // shards_of).reshape((-1,) + (1,) * (len(dims) - 1 - dim))
    return factor_of


def noise(rng, extent, deviation, limit, shards=(), held_as=jnp.bfloat16):
    array = deviation * jax.random.normal(rng, extent, jnp.float32)
    if shards:
        array = array * block_levels(rng, extent, shards, -0.22, 0.18)
    return jnp.clip(array, -limit, limit).astype(held_as)


def setup_inputs(seed: int = 0) -> dict:
    key_list = jax.random.split(jax.random.key(seed), 16)
    hidden = noise(key_list[0], (MICRO, BATCH, LEN, D), 1.0, 6.0, ((1, 4), (2, 4)))
    w_query = noise(key_list[1], (D, HEADS * HEAD), D ** -0.5, 0.125, ((0, 16), (1, 2)))
    w_key = noise(key_list[2], (D, KV_HEADS * HEAD), D ** -0.5, 0.125, ((0, 16), (1, 2)))
    w_value = noise(key_list[3], (D, KV_HEADS * HEAD), D ** -0.5, 0.125, ((0, 16), (1, 2)))
    w_out = noise(key_list[4], (HEADS * HEAD, D), 64 ** -0.5, 0.75, ((0, 2), (1, 16)))
    w_gate = noise(key_list[5], (D, FF), D ** -0.5, 0.125, ((0, 16), (1, 2)))
    w_up = noise(key_list[6], (D, FF), D ** -0.5, 0.125, ((0, 16), (1, 2)))
    w_down = noise(key_list[7], (FF, D), FF ** -0.5, 0.078125, ((0, 2), (1, 16)))
    norm_attn = jnp.clip(1.0 + 0.15 * jax.random.normal(key_list[8], (D,), jnp.float32), 0.25, 1.75).astype(jnp.bfloat16)
    norm_ffn = jnp.clip(1.0 + 0.15 * jax.random.normal(key_list[9], (D,), jnp.float32), 0.25, 1.75).astype(jnp.bfloat16)
    norm_query = jnp.clip(1.0 + 0.15 * jax.random.normal(key_list[10], (HEAD,), jnp.float32), 0.25, 1.75).astype(jnp.bfloat16)
    norm_key = jnp.clip(1.0 + 0.15 * jax.random.normal(key_list[11], (HEAD,), jnp.float32), 0.25, 1.75).astype(jnp.bfloat16)
    segments = draw_segments(jax.random.fold_in(key_list[15], 71), 0)
    positions = draw_positions(jax.random.fold_in(key_list[15], 71), 0)
    cotangent = noise(key_list[14], (MICRO, BATCH, LEN, D), 1.0, 6.0, ((1, 4), (2, 4)))
    return {"hidden": hidden, "w_query": w_query, "w_key": w_key, "w_value": w_value, "w_out": w_out, "w_gate": w_gate, "w_up": w_up, "w_down": w_down, "norm_attn": norm_attn, "norm_ffn": norm_ffn, "norm_query": norm_query, "norm_key": norm_key, "segments": segments, "positions": positions, "cotangent": cotangent}


EPS = 1e-06
ROPE_BASE = 1000000.0

@jax.custom_vjp
def low(v):
    return lax.optimization_barrier(v.astype(jnp.bfloat16)).astype(jnp.float32)

@jax.custom_vjp
def low_back(v):
    return v

def low_keep(v):
    return (low(v), None)

def low_pass(kept, grad):
    return (grad,)

def back_keep(v):
    return (v, None)

def back_low(kept, grad):
    return (low(grad),)
low.defvjp(low_keep, low_pass)
low_back.defvjp(back_keep, back_low)

def rms_scale(values, gain):
    inverse = lax.rsqrt(lax.optimization_barrier(jnp.mean(values * values, axis=-1, keepdims=True)) + EPS)
    return values * inverse * gain

def rotate(values, cosine, sine):
    half_size = values.shape[-1] // 2
    turned = jnp.concatenate([-values[..., half_size:], values[..., :half_size]], axis=-1)
    return values * cosine + turned * sine

def matmul(left, right):
    return jnp.dot(left, right, precision=lax.Precision.HIGHEST)

def sequence_layer(params, tokens, seg_ids, pos_ids):
    w_query, w_key, w_value, w_out, w_gate, w_up, w_down, norm_attn, norm_ffn, norm_query, norm_key = params
    length = tokens.shape[0]
    normed_attn = low(rms_scale(tokens, norm_attn))
    query_raw = low_back(matmul(normed_attn, w_query)).reshape(length, HEADS, HEAD)
    key_raw = low_back(matmul(normed_attn, w_key)).reshape(length, KV_HEADS, HEAD)
    values_all = low(low_back(matmul(normed_attn, w_value))).reshape(length, KV_HEADS, HEAD)
    frequency = ROPE_BASE ** (-(jnp.arange(HEAD // 2, dtype=jnp.float32) * 2.0) / HEAD)
    angles = pos_ids.astype(jnp.float32)[:, None] * frequency[None, :]
    angles = jnp.concatenate([angles, angles], axis=-1)[:, None, :]
    cosine = jnp.cos(angles)
    sine = jnp.sin(angles)
    queries = low(rotate(rms_scale(query_raw, norm_query), cosine, sine))
    keys_rot = low(rotate(rms_scale(key_raw, norm_key), cosine, sine))
    group_size = HEADS // KV_HEADS
    grouped = queries.reshape(length, KV_HEADS, group_size, HEAD)
    block_rows = min(512, length)
    score_scale = HEAD ** (-0.5)
    key_ids = jnp.arange(length, dtype=jnp.int32)

    def attend(start_row):
        q_block = lax.dynamic_slice_in_dim(grouped, start_row, block_rows, 0)
        seg_block = lax.dynamic_slice_in_dim(seg_ids, start_row, block_rows, 0)
        row_ids = start_row + jnp.arange(block_rows, dtype=jnp.int32)
        scores = low_back(jnp.einsum('qkgd,tkd->kgqt', q_block, keys_rot, precision=lax.Precision.HIGHEST) * score_scale)
        allowed = (seg_block[:, None] == seg_ids[None, :]) & (row_ids[:, None] >= key_ids[None, :])
        scores = jnp.where(allowed[None, None], scores, -1e+30)
        weights_p = jax.nn.softmax(scores, axis=-1)
        mixed = jnp.einsum('kgqt,tkd->qkgd', low(weights_p), values_all, precision=lax.Precision.HIGHEST)
        return mixed.reshape(block_rows, HEADS * HEAD)
    block_starts = jnp.arange(length // block_rows, dtype=jnp.int32) * block_rows
    mixed_all = lax.map(jax.checkpoint(attend), block_starts).reshape(length, HEADS * HEAD)
    attn_heads = low(low_back(mixed_all))
    middle = tokens + low_back(matmul(attn_heads, w_out))
    normed_ffn = low(rms_scale(middle, norm_ffn))
    gate = low_back(matmul(normed_ffn, w_gate))
    upward = low_back(matmul(normed_ffn, w_up))
    act = low(jax.nn.silu(gate) * upward)
    return middle + matmul(act, w_down)

def reference(hidden, w_query, w_key, w_value, w_out, w_gate, w_up, w_down, norm_attn, norm_ffn, norm_query, norm_key, segments, positions, cotangent):
    params = tuple((weight_arr.astype(jnp.float32) for weight_arr in (w_query, w_key, w_value, w_out, w_gate, w_up, w_down, norm_attn, norm_ffn, norm_query, norm_key)))
    count = MICRO * BATCH
    tokens = hidden.reshape(count, LEN, D).astype(jnp.float32)
    seg_all = segments.reshape(count, LEN)
    pos_all = positions.reshape(count, LEN)
    cot_all = cotangent.reshape(count, LEN, D).astype(jnp.float32)

    def one_sequence(carried, inputs_at):
        tok_seq, seg_seq, pos_seq, cot_seq = inputs_at

        def layer_fn(weights_all, tok_in):
            return sequence_layer(weights_all, tok_in, seg_seq, pos_seq)
        result, pull_back = jax.vjp(layer_fn, params, tok_seq)
        grad_params, grad_tokens = pull_back(cot_seq)
        carried = jax.tree.map(jnp.add, carried, grad_params)
        return (carried, (result.astype(jnp.bfloat16), grad_tokens.astype(jnp.bfloat16)))
    zero_grads = jax.tree.map(jnp.zeros_like, params)
    grads, (outs_all, grads_in) = lax.scan(one_sequence, zero_grads, (tokens, seg_all, pos_all, cot_all))
    return (outs_all.reshape(MICRO, BATCH, LEN, D), grads_in.reshape(MICRO, BATCH, LEN, D), grads[0], grads[1], grads[2], grads[3], grads[4], grads[5], grads[6], grads[7], grads[8], grads[9], grads[10])
```

```python
import jax
import jax.numpy as jnp
from jax import lax
from jax.sharding import PartitionSpec as P

HEADS = 16
KV_HEADS = 8
HEAD = 128
MICRO = 2

EPS = 1e-06
ROPE_BASE = 1000000.0
F32 = jnp.float32
BF16 = jnp.bfloat16


def dot(left, right):
    return jnp.dot(left, right, preferred_element_type=F32)


def tdot(left, right):
    return lax.dot_general(left, right, (((0,), (0,)), ((), ())), preferred_element_type=F32)


def rdot(left, right):
    return lax.dot_general(left, right, (((1,), (1,)), ((), ())), preferred_element_type=F32)


def rotate(values, cosine, sine):
    half_size = values.shape[-1] // 2
    turned = jnp.concatenate([-values[..., half_size:], values[..., :half_size]], axis=-1)
    return values * cosine + turned * sine


def rotate_back(grads, cosine, sine):
    half_size = grads.shape[-1] // 2
    scaled = grads * sine
    back_part = jnp.concatenate([scaled[..., half_size:], -scaled[..., :half_size]], axis=-1)
    return grads * cosine + back_part


def norm_back(grads, values, inverse, gain):
    scaled = grads * gain
    return inverse * scaled - values * inverse**3 * jnp.mean(
        scaled * values, axis=-1, keepdims=True
    )


def inv_rms(values):
    return lax.rsqrt(jnp.mean(values * values, axis=-1, keepdims=True) + EPS)


def make_local(mp_size, seq_size, dp_size):
    data_axes = ("dp", "seq")
    pair = [(i, i ^ 1) for i in range(seq_size)]
    up_pairs = [(i, i + 2) for i in range(seq_size - 2)]
    down_pairs = [(i + 2, i) for i in range(seq_size - 2)]

    def mp_sum(part):
        part = lax.optimization_barrier(part.astype(BF16))
        if mp_size == 2:
            other = lax.ppermute(part, "mp", [(0, 1), (1, 0)])
            return part.astype(F32) + other.astype(F32)
        return lax.psum(part, "mp").astype(F32)

    def local(
        hidden,
        w_query,
        w_key,
        w_value,
        w_out,
        w_gate,
        w_up,
        w_down,
        norm_attn,
        norm_ffn,
        norm_query,
        norm_key,
        segments,
        positions,
        cotangent,
    ):
        rows = hidden.shape[2]
        width = hidden.shape[3]
        total = MICRO * rows
        q_cols = w_query.shape[1]
        k_cols = w_key.shape[1]
        kv_heads = k_cols // HEAD
        group = HEADS // KV_HEADS
        score_scale = HEAD ** (-0.5)
        rank = lax.axis_index("seq")
        own_rows = w_query.shape[0]

        gains = jnp.concatenate(
            [
                jnp.broadcast_to(norm_attn[:, None], (own_rows, 64)),
                jnp.broadcast_to(norm_ffn[:, None], (own_rows, 64)),
            ],
            axis=1,
        )
        first = jnp.concatenate([w_query, w_key, w_value, w_out.T, gains], axis=1)
        first = lax.all_gather(first, data_axes, axis=0, tiled=True)
        second = jnp.stack([w_gate, w_up, w_down.T])
        second, first = lax.optimization_barrier((second, first))
        second = lax.all_gather(second, data_axes, axis=1, tiled=True)
        qkv_cols = q_cols + 2 * k_cols
        w_qkv = first[:, :qkv_cols]
        w_out_t = first[:, qkv_cols : qkv_cols + q_cols]
        gain_attn = first[:, qkv_cols + q_cols].astype(F32)
        gain_ffn = first[:, qkv_cols + q_cols + 64].astype(F32)
        gate_full, up_full, down_t = second[0], second[1], second[2]
        gain_query = norm_query.astype(F32)
        gain_key = norm_key.astype(F32)

        tokens = hidden.reshape(total, width).astype(F32)
        cot = cotangent.reshape(total, width)

        seg_own = segments[:, 0]
        seg_pair = lax.ppermute(seg_own, "seq", pair)
        both = jnp.stack([seg_own, seg_pair])
        both_x = lax.ppermute(both, "seq", up_pairs)
        seg_all = jnp.zeros((MICRO, rows * seq_size), jnp.int32)

        def place(buffer, parts, axis):
            for flip, part in enumerate(parts):
                buffer = lax.dynamic_update_slice_in_dim(
                    buffer, part, jnp.bitwise_xor(rank, flip) * rows, axis
                )
            return buffer

        seg_all = place(seg_all, [both[0], both[1], both_x[0], both_x[1]], 1)

        frequency = ROPE_BASE ** (-(jnp.arange(HEAD // 2, dtype=F32) * 2.0) / HEAD)
        angles = positions.reshape(total).astype(F32)[:, None] * frequency[None, :]
        angles = jnp.concatenate([angles, angles], axis=-1)[:, None, :]
        cosine = jnp.cos(angles)
        sine = jnp.sin(angles)

        inv_attn = inv_rms(tokens)
        normed_attn = (tokens * inv_attn * gain_attn).astype(BF16)
        raw = dot(normed_attn, w_qkv)
        query_raw = raw[:, :q_cols].reshape(total, -1, HEAD)
        key_raw = raw[:, q_cols : q_cols + k_cols].reshape(total, -1, HEAD)
        values = raw[:, q_cols + k_cols :].astype(BF16)
        query_inv = inv_rms(query_raw)
        key_inv = inv_rms(key_raw)
        queries = rotate(query_raw * query_inv * gain_query, cosine, sine).astype(BF16)
        keys = rotate(key_raw * key_inv * gain_key, cosine, sine).astype(BF16)
        keys = keys.reshape(total, k_cols)
        key_ids = jnp.arange(rows * seq_size, dtype=jnp.int32)
        row_ids = rank * rows + jnp.arange(rows, dtype=jnp.int32)

        kept = []
        middles = []
        heads_out = []
        for step in range(MICRO):
            cut = slice(step * rows, (step + 1) * rows)
            own = jnp.concatenate([keys[cut], values[cut]], axis=1)
            near = lax.ppermute(own, "seq", pair)
            far = lax.ppermute(own, "seq", up_pairs)
            far_near = lax.ppermute(far, "seq", pair)
            wide = place(
                jnp.zeros((rows * seq_size, 2 * k_cols), BF16), [own, near, far, far_near], 0
            )
            keys_all = wide[:, :k_cols].reshape(-1, kv_heads, HEAD)
            values_all = wide[:, k_cols:].reshape(-1, kv_heads, HEAD)
            q_block = queries[cut].reshape(rows, kv_heads, group, HEAD)
            allowed = (seg_own[step][:, None] == seg_all[step][None, :]) & (
                row_ids[:, None] >= key_ids[None, :]
            )
            scores = (
                jnp.einsum("qkgd,tkd->kgqt", q_block, keys_all, preferred_element_type=F32)
                * score_scale
            )
            scores = jnp.where(allowed[None, None], scores, -1e30)
            row_max = jnp.max(scores, axis=-1, keepdims=True)
            expo = jnp.exp(scores - row_max)
            row_sum = jnp.sum(expo, axis=-1, keepdims=True)
            probs = (expo / row_sum).astype(BF16)
            mixed = jnp.einsum("kgqt,tkd->qkgd", probs, values_all, preferred_element_type=F32)
            attn_heads = mixed.reshape(rows, -1).astype(BF16)
            heads_out.append(attn_heads)
            kept.append((q_block, keys_all, values_all, allowed, row_max + jnp.log(row_sum)))
            attn_part = rdot(attn_heads, w_out_t)
            middles.append(tokens[cut] + mp_sum(attn_part))
        middle = jnp.concatenate(middles, axis=0)
        attn_heads = jnp.concatenate(heads_out, axis=0)

        inv_ffn = inv_rms(middle)
        normed_ffn = (middle * inv_ffn * gain_ffn).astype(BF16)
        gate = dot(normed_ffn, gate_full)
        upward = dot(normed_ffn, up_full)
        sigma = jax.nn.sigmoid(gate)
        silu = gate * sigma
        act = (silu * upward).astype(BF16)
        grad_act = dot(cot, down_t)
        grad_gate_in = (grad_act * upward * sigma * (1.0 + gate * (1.0 - sigma))).astype(BF16)
        grad_up_in = (grad_act * silu).astype(BF16)

        def scatter(grad):
            return lax.psum_scatter(
                grad.astype(BF16), data_axes, scatter_dimension=0, tiled=True
            )

        down_owned = scatter(tdot(cot, act))
        backs = []
        for step in range(MICRO):
            cut = slice(step * rows, (step + 1) * rows)
            backs.append(
                mp_sum(rdot(grad_gate_in[cut], gate_full) + rdot(grad_up_in[cut], up_full))
            )
        gate_owned = scatter(tdot(normed_ffn, grad_gate_in))
        up_owned = scatter(tdot(normed_ffn, grad_up_in))
        down_part = rdot(act, down_t)
        layer_out = (middle + mp_sum(down_part)).astype(BF16)
        grad_normed_ffn = jnp.concatenate(backs, axis=0)
        gain_ffn_grad = jnp.sum(grad_normed_ffn * middle * inv_ffn, axis=0)
        grad_middle = cot.astype(F32) + norm_back(grad_normed_ffn, middle, inv_ffn, gain_ffn)
        grad_middle_b = grad_middle.astype(BF16)
        grad_heads = dot(grad_middle_b, w_out_t).astype(BF16)
        out_owned = scatter(tdot(grad_middle_b, attn_heads))

        grad_queries = []
        grad_keys = []
        grad_values = []
        for step in range(MICRO):
            cut = slice(step * rows, (step + 1) * rows)
            q_block, keys_all, values_all, allowed, log_sum = kept[step]
            g_block = grad_heads[cut].reshape(rows, kv_heads, group, HEAD)
            scores = (
                jnp.einsum("qkgd,tkd->kgqt", q_block, keys_all, preferred_element_type=F32)
                * score_scale
            )
            probs = jnp.where(allowed[None, None], jnp.exp(scores - log_sum), 0.0)
            grad_probs = jnp.einsum(
                "qkgd,tkd->kgqt", g_block, values_all, preferred_element_type=F32
            )
            row_dot = jnp.sum(grad_probs * probs, axis=-1, keepdims=True)
            grad_scores = (probs * (grad_probs - row_dot)).astype(BF16)
            grad_queries.append(
                jnp.einsum("kgqt,tkd->qkgd", grad_scores, keys_all, preferred_element_type=F32)
                * score_scale
            )
            grad_k = (
                jnp.einsum("kgqt,qkgd->tkd", grad_scores, q_block, preferred_element_type=F32)
                * score_scale
            )
            grad_v = jnp.einsum(
                "kgqt,qkgd->tkd", probs.astype(BF16), g_block, preferred_element_type=F32
            )
            wide = jnp.concatenate(
                [grad_k.reshape(-1, k_cols), grad_v.reshape(-1, k_cols)], axis=1
            )

            def part(flip):
                return lax.dynamic_slice_in_dim(
                    wide, jnp.bitwise_xor(rank, flip) * rows, rows, 0
                )

            sent = jnp.stack([part(1), part(3)]).astype(BF16)
            got = lax.ppermute(sent, "seq", pair).astype(F32)
            far = lax.ppermute((part(2) + got[1]).astype(BF16), "seq", down_pairs).astype(F32)
            owned = part(0) + got[0] + far
            grad_keys.append(owned[:, :k_cols])
            grad_values.append(owned[:, k_cols:])
        grad_query_rot = jnp.concatenate(grad_queries, axis=0).reshape(total, -1, HEAD)
        grad_key_rot = jnp.concatenate(grad_keys, axis=0).reshape(total, -1, HEAD)
        grad_value_in = jnp.concatenate(grad_values, axis=0).astype(BF16)
        query_turn = rotate_back(grad_query_rot, cosine, sine)
        key_turn = rotate_back(grad_key_rot, cosine, sine)
        query_gain = jnp.sum(query_turn * query_raw * query_inv, axis=(0, 1))
        key_gain = jnp.sum(key_turn * key_raw * key_inv, axis=(0, 1))
        grad_query_in = norm_back(query_turn, query_raw, query_inv, gain_query)
        grad_key_in = norm_back(key_turn, key_raw, key_inv, gain_key)
        grad_qkv_in = jnp.concatenate(
            [
                grad_query_in.astype(BF16).reshape(total, -1),
                grad_key_in.astype(BF16).reshape(total, -1),
                grad_value_in,
            ],
            axis=1,
        )
        qkv_owned = scatter(tdot(normed_attn, grad_qkv_in))
        backs = []
        for step in range(MICRO):
            cut = slice(step * rows, (step + 1) * rows)
            backs.append(mp_sum(rdot(grad_qkv_in[cut], w_qkv)))
        grad_normed_attn = jnp.concatenate(backs, axis=0)
        gain_attn_grad = jnp.sum(grad_normed_attn * tokens * inv_attn, axis=0)
        grad_tokens = (
            grad_middle + norm_back(grad_normed_attn, tokens, inv_attn, gain_attn)
        ).astype(BF16)

        small = jnp.concatenate([gain_attn_grad, gain_ffn_grad, query_gain, key_gain])
        small = lax.all_gather(small, ("dp", "seq", "mp"), axis=0, tiled=False)
        small = small.reshape(dp_size * seq_size, mp_size, -1)
        head_sum = jnp.sum(small[:, :, 2 * width :], axis=(0, 1))
        owner = (lax.axis_index("dp") * seq_size + rank) * own_rows
        wide_sum = jnp.sum(small[:, 0, : 2 * width], axis=0).reshape(2, width)
        wide_sum = lax.dynamic_slice_in_dim(wide_sum, owner, own_rows, 1)

        qkv_owned = qkv_owned.astype(F32)
        return (
            layer_out.reshape(MICRO, 1, rows, width),
            grad_tokens.reshape(MICRO, 1, rows, width),
            qkv_owned[:, :q_cols],
            qkv_owned[:, q_cols : q_cols + k_cols],
            qkv_owned[:, q_cols + k_cols :],
            out_owned.T.astype(F32),
            gate_owned.astype(F32),
            up_owned.astype(F32),
            down_owned.T.astype(F32),
            wide_sum[0],
            wide_sum[1],
            head_sum[:HEAD],
            head_sum[HEAD:],
        )

    return local


def solution(mesh):
    return jax.shard_map(
        make_local(mesh.shape["mp"], mesh.shape["seq"], mesh.shape["dp"]),
        mesh=mesh,
        in_specs=(
            P(None, "dp", "seq", None),
            P(("dp", "seq"), "mp"),
            P(("dp", "seq"), "mp"),
            P(("dp", "seq"), "mp"),
            P("mp", ("dp", "seq")),
            P(("dp", "seq"), "mp"),
            P(("dp", "seq"), "mp"),
            P("mp", ("dp", "seq")),
            P(("dp", "seq")),
            P(("dp", "seq")),
            P(),
            P(),
            P(None, "dp", "seq"),
            P(None, "dp", "seq"),
            P(None, "dp", "seq", None),
        ),
        out_specs=(
            P(None, "dp", "seq", None),
            P(None, "dp", "seq", None),
            P(("dp", "seq"), "mp"),
            P(("dp", "seq"), "mp"),
            P(("dp", "seq"), "mp"),
            P("mp", ("dp", "seq")),
            P(("dp", "seq"), "mp"),
            P(("dp", "seq"), "mp"),
            P("mp", ("dp", "seq")),
            P(("dp", "seq")),
            P(("dp", "seq")),
            P(),
            P(),
        ),
        check_vma=False,
    )
```

```python
import functools

import jax
import jax.numpy as jnp
from jax import lax
from jax.experimental import pallas as pl
from jax.experimental.pallas import tpu as pltpu
from jax.sharding import PartitionSpec as P

HEADS = 16
KV_HEADS = 8
HEAD = 128
MICRO = 2

EPS = 1e-06
ROPE_BASE = 1000000.0
F32 = jnp.float32
BF16 = jnp.bfloat16
SCALE = HEAD ** (-0.5)
EXP2_SCALE = SCALE * 1.4426950408889634


def dot(left, right):
    return jnp.dot(left, right, preferred_element_type=F32)


def tdot(left, right):
    return lax.dot_general(left, right, (((0,), (0,)), ((), ())), preferred_element_type=F32)


def rdot(left, right):
    return lax.dot_general(left, right, (((1,), (1,)), ((), ())), preferred_element_type=F32)


def rotate(values, cosine, sine):
    half_size = values.shape[-1] // 2
    turned = jnp.concatenate([-values[..., half_size:], values[..., :half_size]], axis=-1)
    return values * cosine + turned * sine


def rotate_back(grads, cosine, sine):
    half_size = grads.shape[-1] // 2
    scaled = grads * sine
    back_part = jnp.concatenate([scaled[..., half_size:], -scaled[..., :half_size]], axis=-1)
    return grads * cosine + back_part


def norm_back(grads, values, inverse, gain):
    scaled = grads * gain
    return inverse * scaled - values * inverse**3 * jnp.mean(
        scaled * values, axis=-1, keepdims=True
    )


def inv_rms(values):
    return lax.rsqrt(jnp.mean(values * values, axis=-1, keepdims=True) + EPS)


def forward_kernel(tile, group, need, q, k0,v0,k1,v1,k2,v2,k3,v3, seg_q, seg_k, out, log_sum, acc, den):
    rows=q.shape[0]
    tiles=[(g,t) for g in range(group) for t in range(rows//tile)]
    def run(flip, k, v):
        for g,t in tiles:
            cut=slice(t*tile,(t+1)*tile)
            n=(t+1)*tile if flip==0 else rows
            s=rdot(q[cut,g*HEAD:(g+1)*HEAD], k[:n,:])
            ok=seg_q[cut,:]==seg_k[flip:flip+1,:n]
            if flip==0:
                ok&=(lax.broadcasted_iota(jnp.int32,(tile,n),0)+t*tile)>=lax.broadcasted_iota(jnp.int32,(tile,n),1)
            e=jnp.where(ok,jnp.exp2(s*EXP2_SCALE),0.0)
            mixed=dot(e.astype(BF16),v[:n,:])
            total=jnp.sum(e,axis=1,keepdims=True)
            at=slice(g*rows+t*tile,g*rows+(t+1)*tile)
            if flip==0:
                acc[at,:]=mixed; den[at,:]=total
            else:
                acc[at,:]+=mixed; den[at,:]+=total
    run(0,k0,v0)
    for flip,(k,v) in ((1,(k1,v1)),(2,(k2,v2)),(3,(k3,v3))):
        pl.when(need[flip]>0)(functools.partial(run,flip,k,v))
    for g in range(group):
        at=slice(g*rows,(g+1)*rows)
        out[:,g*HEAD:(g+1)*HEAD]=(acc[at,:]/den[at,:]).astype(out.dtype)
    log_sum[0]=jnp.log2(den[...])

def attend(need, queries, step, parts, seg_q, seg_k, k_cols, group, tile=256):
    rows=parts[0].shape[0]; kv=k_cols//HEAD
    kspec=pl.BlockSpec((rows,HEAD),lambda h,n:(0,h))
    vspec=pl.BlockSpec((rows,HEAD),lambda h,n:(0,h+kv))
    return pl.pallas_call(
        functools.partial(forward_kernel,tile,group),
        grid_spec=pltpu.PrefetchScalarGridSpec(
            num_scalar_prefetch=1, grid=(kv,),
            in_specs=[pl.BlockSpec((rows,group*HEAD),lambda h,n:(step,h))]+[kspec,vspec]*4+[
                pl.BlockSpec((rows,1),lambda h,n:(0,0)), pl.BlockSpec((4,rows),lambda h,n:(0,0))],
            out_specs=[pl.BlockSpec((rows,group*HEAD),lambda h,n:(0,h)), pl.BlockSpec((1,group*rows,1),lambda h,n:(h,0,0))],
            scratch_shapes=[pltpu.VMEM((group*rows,HEAD),F32),pltpu.VMEM((group*rows,1),F32)]),
        out_shape=[jax.ShapeDtypeStruct((rows,kv*group*HEAD),BF16),jax.ShapeDtypeStruct((kv,group*rows,1),F32)],
        name="attend",
    )(need,queries,*[p for part in parts for p in (part,part)],seg_q,seg_k)

def backward_kernel(tile, group, need, q, g_out, k0,v0,k1,v1,k2,v2,k3,v3, seg_q, seg_k, stats, dq, d0,d1,d2,d3, acc):
    rows=q.shape[0]
    tiles=[(g,t) for g in range(group) for t in range(rows//tile)]
    def run(flip,k,v,d,dk_acc,dv_acc):
        for idx,(g,t) in enumerate(tiles):
            cut=slice(t*tile,(t+1)*tile)
            at=slice(g*rows+t*tile,g*rows+(t+1)*tile)
            n=(t+1)*tile if flip==0 else rows
            qt=q[cut,g*HEAD:(g+1)*HEAD]; dt=g_out[cut,g*HEAD:(g+1)*HEAD]
            kn=k[:n,:]
            s=rdot(kn,qt)
            ok=seg_k[:n,flip:flip+1]==seg_q[:,cut]
            if flip==0:
                ok&=(lax.broadcasted_iota(jnp.int32,(n,tile),1)+t*tile)>=lax.broadcasted_iota(jnp.int32,(n,tile),0)
            p=jnp.where(ok,jnp.exp2(s*EXP2_SCALE-stats[0,0:1,at]),0.0)
            dp=rdot(v[:n,:],dt)
            ds=(p*(dp-stats[0,1:2,at])).astype(BF16)
            dv=dot(p.astype(BF16),dt)
            dk=dot(ds,qt)
            if idx==0:
                dk_acc[...]=jnp.zeros_like(dk_acc); dv_acc[...]=jnp.zeros_like(dv_acc)
            dk_acc[:n,:]+=dk
            dv_acc[:n,:]+=dv
            back=tdot(ds,kn)*SCALE
            o=(cut,slice(g*HEAD,(g+1)*HEAD))
            if flip==0: dq[o]=back
            else: dq[o]+=back
        d[0]=(dk_acc[...]*SCALE).astype(d.dtype)
        d[1]=dv_acc[...].astype(d.dtype)
    run(0,k0,v0,d0,acc.at[0],acc.at[1])
    for flip,(k,v,d) in ((1,(k1,v1,d1)),(2,(k2,v2,d2)),(3,(k3,v3,d3))):
        pl.when(need[flip]>0)(functools.partial(run,flip,k,v,d,acc.at[0],acc.at[1]))
        def clear(d=d): d[...]=jnp.zeros_like(d)
        pl.when(need[flip]<=0)(clear)

def attend_back(need, queries, grad_heads, step, parts, seg_q, seg_k, stats, k_cols, group, tile=256):
    rows=parts[0].shape[0]; kv=k_cols//HEAD
    kspec=pl.BlockSpec((rows,HEAD),lambda h,n:(0,h))
    vspec=pl.BlockSpec((rows,HEAD),lambda h,n:(0,h+kv))
    qspec=pl.BlockSpec((rows,group*HEAD),lambda h,n:(step,h))
    dspec=pl.BlockSpec((2,rows,HEAD),lambda h,n:(0,0,h))
    types=(F32,BF16,F32,BF16)
    return pl.pallas_call(
        functools.partial(backward_kernel,tile,group),
        grid_spec=pltpu.PrefetchScalarGridSpec(
            num_scalar_prefetch=1, grid=(kv,),
            in_specs=[qspec,qspec]+[kspec,vspec]*4+[
                pl.BlockSpec((1,rows),lambda h,n:(0,0)), pl.BlockSpec((rows,4),lambda h,n:(0,0)),
                pl.BlockSpec((1,2,group*rows),lambda h,n:(h,0,0))],
            out_specs=[pl.BlockSpec((rows,group*HEAD),lambda h,n:(0,h))]+[dspec]*4,
            scratch_shapes=[pltpu.VMEM((2,rows,HEAD),F32)]),
        out_shape=[jax.ShapeDtypeStruct((rows,kv*group*HEAD),F32)]+[jax.ShapeDtypeStruct((2,rows,k_cols),t) for t in types],
        name="attend_back",
    )(need,queries,grad_heads,*[p for part in parts for p in (part,part)],seg_q,seg_k,stats)


def make_local(mp_size, seq_size, dp_size):
    data_axes = ("dp", "seq")
    pair = [(i, i ^ 1) for i in range(seq_size)]
    up_pairs = [(i, i + 2) for i in range(seq_size - 2)]
    down_pairs = [(i + 2, i) for i in range(seq_size - 2)]

    def scatter(grad):
        return lax.psum_scatter(grad, data_axes, scatter_dimension=0, tiled=True)

    def mp_part(part):
        part = lax.optimization_barrier(part.astype(BF16))
        if mp_size == 2:
            return part, lax.ppermute(part, "mp", [(0, 1), (1, 0)])
        return lax.psum(part, "mp"), jnp.zeros(part.shape, BF16)

    def mp_sum(part):
        mine, other = mp_part(part)
        return mine.astype(F32) + other.astype(F32)

    def local(
        hidden,
        w_query,
        w_key,
        w_value,
        w_out,
        w_gate,
        w_up,
        w_down,
        norm_attn,
        norm_ffn,
        norm_query,
        norm_key,
        segments,
        positions,
        cotangent,
    ):
        rows = hidden.shape[2]
        width = hidden.shape[3]
        total = MICRO * rows
        q_cols = w_query.shape[1]
        k_cols = w_key.shape[1]
        kv_heads = k_cols // HEAD
        group = HEADS // KV_HEADS
        rank = lax.axis_index("seq")
        own_rows = w_query.shape[0]

        gains = jnp.concatenate(
            [
                jnp.broadcast_to(norm_attn[:, None], (own_rows, 64)),
                jnp.broadcast_to(norm_ffn[:, None], (own_rows, 64)),
            ],
            axis=1,
        )
        first = jnp.concatenate([w_query, w_key, w_value, w_out.T, gains], axis=1)
        first = lax.all_gather(first, data_axes, axis=0, tiled=True)
        second = jnp.stack([w_gate, w_up, w_down.T])
        second, first = lax.optimization_barrier((second, first))
        second = lax.all_gather(second, data_axes, axis=1, tiled=True)
        tokens = hidden.reshape(total, width).astype(F32)
        inv_attn = inv_rms(tokens)
        frequency = ROPE_BASE ** (-(jnp.arange(HEAD // 2, dtype=F32) * 2.0) / HEAD)
        angles = positions.reshape(total).astype(F32)[:, None] * frequency[None, :]
        angles = jnp.concatenate([angles, angles], axis=-1)[:, None, :]
        cosine = jnp.cos(angles)
        sine = jnp.sin(angles)
        first, cosine, sine, inv_attn = lax.optimization_barrier((first, cosine, sine, inv_attn))
        qkv_cols = q_cols + 2 * k_cols
        w_qkv = first[:, :qkv_cols]
        w_out_t = first[:, qkv_cols : qkv_cols + q_cols]
        gain_attn = first[:, qkv_cols + q_cols].astype(F32)
        gain_ffn = first[:, qkv_cols + q_cols + 64].astype(F32)
        gate_full, up_full, down_t = second[0], second[1], second[2]
        gain_query = norm_query.astype(F32)
        gain_key = norm_key.astype(F32)

        cot = cotangent.reshape(total, width)

        seg_own = segments[:, 0]
        seg_pair = lax.ppermute(seg_own, "seq", pair)
        both = jnp.stack([seg_own, seg_pair])
        both_x = lax.ppermute(both, "seq", up_pairs)
        seg_keys = jnp.stack([both[0], both[1], both_x[0], both_x[1]])
        flips = jnp.arange(4, dtype=jnp.int32)
        near_enough = (seg_keys[:, :, -1] == seg_own[None, :, 0]) | (flips[:, None] == 0)
        need = (near_enough & (jnp.bitwise_xor(rank, flips)[:, None] <= rank)).astype(jnp.int32)

        normed_attn = (tokens * inv_attn * gain_attn).astype(BF16)
        raw = dot(normed_attn, w_qkv)
        query_raw = raw[:, :q_cols].reshape(total, -1, HEAD)
        key_raw = raw[:, q_cols : q_cols + k_cols].reshape(total, -1, HEAD)
        values = raw[:, q_cols + k_cols :].astype(BF16)
        query_inv = inv_rms(query_raw)
        key_inv = inv_rms(key_raw)
        queries = rotate(query_raw * query_inv * gain_query, cosine, sine).astype(BF16)
        queries = queries.reshape(total, q_cols)
        keys = rotate(key_raw * key_inv * gain_key, cosine, sine).astype(BF16)
        keys = keys.reshape(total, k_cols)
        kept = []
        middles = []
        heads_out = []
        for step in range(MICRO):
            cut = slice(step * rows, (step + 1) * rows)
            own = jnp.concatenate([keys[cut], values[cut]], axis=1)
            near = lax.ppermute(own, "seq", pair)
            far = lax.ppermute(own, "seq", up_pairs)
            far_near = lax.ppermute(far, "seq", pair)
            parts = (own, near, far, far_near)
            attn_heads, log_sum = attend(
                need[:, step],
                queries,
                step,
                parts,
                seg_own[step][:, None],
                seg_keys[:, step],
                k_cols,
                group,
                rows,
            )
            heads_out.append(attn_heads)
            kept.append((parts, log_sum))
            attn_part = rdot(attn_heads, w_out_t)
            middles.append(tokens[cut] + mp_sum(attn_part))
        middle = jnp.concatenate(middles, axis=0)
        attn_heads = jnp.concatenate(heads_out, axis=0)

        inv_ffn = inv_rms(middle)
        normed_ffn = (middle * inv_ffn * gain_ffn).astype(BF16)
        gate = dot(normed_ffn, gate_full)
        upward = dot(normed_ffn, up_full)
        sigma = jax.nn.sigmoid(gate)
        silu = gate * sigma
        act = (silu * upward).astype(BF16)
        down_grad = tdot(cot, act).astype(BF16)
        down_owned = scatter(down_grad)
        cot_late, act, down_grad = lax.optimization_barrier((cot, act, down_grad))
        grad_act = dot(cot_late, down_t)
        grad_gate_in = (grad_act * upward * sigma * (1.0 + gate * (1.0 - sigma))).astype(BF16)
        grad_up_in = (grad_act * silu).astype(BF16)
        backs = []
        for step in range(MICRO):
            cut = slice(step * rows, (step + 1) * rows)
            backs.append(
                mp_part(rdot(grad_gate_in[cut], gate_full) + rdot(grad_up_in[cut], up_full))
            )
        gate_grad = tdot(normed_ffn, grad_gate_in).astype(BF16)
        gate_owned = scatter(gate_grad)
        up_grad = tdot(normed_ffn, grad_up_in).astype(BF16)
        up_owned = scatter(up_grad)
        backs, act, gate_grad, up_grad = lax.optimization_barrier((backs, act, gate_grad, up_grad))
        backs = [mine.astype(F32) + other.astype(F32) for mine, other in backs]
        layer_out = (middle + mp_sum(rdot(act, down_t))).astype(BF16)
        grad_normed_ffn = jnp.concatenate(backs, axis=0)
        gain_ffn_grad = jnp.sum(grad_normed_ffn * middle * inv_ffn, axis=0)
        grad_middle = cot.astype(F32) + norm_back(grad_normed_ffn, middle, inv_ffn, gain_ffn)
        grad_middle_b = grad_middle.astype(BF16)
        grad_heads = dot(grad_middle_b, w_out_t).astype(BF16)
        out_owned = scatter(tdot(grad_middle_b, attn_heads).astype(BF16))

        grad_queries = []
        grad_keys = []
        grad_values = []
        for step in range(MICRO):
            cut = slice(step * rows, (step + 1) * rows)
            parts, log_sum = kept[step]
            dots = grad_heads[cut].astype(F32) * heads_out[step].astype(F32)
            dots = jnp.sum(dots.reshape(rows, kv_heads, group, HEAD), axis=-1)
            dots = dots.transpose(1, 2, 0).reshape(kv_heads, 1, group * rows)
            stats = jnp.concatenate([log_sum.reshape(kv_heads, 1, group * rows), dots], axis=1)
            grad_q, d_own, d_near, d_far, d_far_near = attend_back(
                need[:, step],
                queries,
                grad_heads,
                step,
                parts,
                seg_own[step][None],
                seg_keys[:, step].T,
                stats,
                k_cols,
                group,
                rows,
            )
            grad_queries.append(grad_q)
            got = lax.ppermute(jnp.stack([d_near, d_far_near]), "seq", pair).astype(F32)
            far = lax.ppermute((d_far + got[1]).astype(BF16), "seq", down_pairs).astype(F32)
            owned = d_own + got[0] + far
            grad_keys.append(owned[0])
            grad_values.append(owned[1])
        grad_queries, down_owned = lax.optimization_barrier((grad_queries, down_owned))
        grad_query_rot = jnp.concatenate(grad_queries, axis=0).reshape(total, -1, HEAD)
        grad_key_rot = jnp.concatenate(grad_keys, axis=0).reshape(total, -1, HEAD)
        grad_value_in = jnp.concatenate(grad_values, axis=0).astype(BF16)
        query_turn = rotate_back(grad_query_rot, cosine, sine)
        key_turn = rotate_back(grad_key_rot, cosine, sine)
        query_gain = jnp.sum(query_turn * query_raw * query_inv, axis=(0, 1))
        key_gain = jnp.sum(key_turn * key_raw * key_inv, axis=(0, 1))
        grad_query_in = norm_back(query_turn, query_raw, query_inv, gain_query)
        grad_key_in = norm_back(key_turn, key_raw, key_inv, gain_key)
        grad_qkv_in = jnp.concatenate(
            [
                grad_query_in.astype(BF16).reshape(total, -1),
                grad_key_in.astype(BF16).reshape(total, -1),
                grad_value_in,
            ],
            axis=1,
        )
        grad_qkv_in, gate_owned = lax.optimization_barrier((grad_qkv_in, gate_owned))
        qkv_owned = scatter(tdot(normed_attn, grad_qkv_in).astype(BF16))
        backs = []
        for step in range(MICRO):
            cut = slice(step * rows, (step + 1) * rows)
            backs.append(mp_sum(rdot(grad_qkv_in[cut], w_qkv)))
        grad_normed_attn = jnp.concatenate(backs, axis=0)
        gain_attn_grad = jnp.sum(grad_normed_attn * tokens * inv_attn, axis=0)
        grad_tokens = (
            grad_middle + norm_back(grad_normed_attn, tokens, inv_attn, gain_attn)
        ).astype(BF16)

        small = jnp.concatenate([gain_attn_grad, gain_ffn_grad, query_gain, key_gain])
        small = lax.all_gather(small, ("dp", "seq", "mp"), axis=0, tiled=False)
        small = small.reshape(dp_size * seq_size, mp_size, -1)
        head_sum = jnp.sum(small[:, :, 2 * width :], axis=(0, 1))
        owner = (lax.axis_index("dp") * seq_size + rank) * own_rows
        wide_sum = jnp.sum(small[:, 0, : 2 * width], axis=0).reshape(2, width)
        wide_sum = lax.dynamic_slice_in_dim(wide_sum, owner, own_rows, 1)

        qkv_owned = qkv_owned.astype(F32)
        return (
            layer_out.reshape(MICRO, 1, rows, width),
            grad_tokens.reshape(MICRO, 1, rows, width),
            qkv_owned[:, :q_cols],
            qkv_owned[:, q_cols : q_cols + k_cols],
            qkv_owned[:, q_cols + k_cols :],
            out_owned.T.astype(F32),
            gate_owned.astype(F32),
            up_owned.astype(F32),
            down_owned.T.astype(F32),
            wide_sum[0],
            wide_sum[1],
            head_sum[:HEAD],
            head_sum[HEAD:],
        )

    return local


def solution(mesh):
    return jax.shard_map(
        make_local(mesh.shape["mp"], mesh.shape["seq"], mesh.shape["dp"]),
        mesh=mesh,
        in_specs=(
            P(None, "dp", "seq", None),
            P(("dp", "seq"), "mp"),
            P(("dp", "seq"), "mp"),
            P(("dp", "seq"), "mp"),
            P("mp", ("dp", "seq")),
            P(("dp", "seq"), "mp"),
            P(("dp", "seq"), "mp"),
            P("mp", ("dp", "seq")),
            P(("dp", "seq")),
            P(("dp", "seq")),
            P(),
            P(),
            P(None, "dp", "seq"),
            P(None, "dp", "seq"),
            P(None, "dp", "seq", None),
        ),
        out_specs=(
            P(None, "dp", "seq", None),
            P(None, "dp", "seq", None),
            P(("dp", "seq"), "mp"),
            P(("dp", "seq"), "mp"),
            P(("dp", "seq"), "mp"),
            P("mp", ("dp", "seq")),
            P(("dp", "seq"), "mp"),
            P(("dp", "seq"), "mp"),
            P("mp", ("dp", "seq")),
            P(("dp", "seq")),
            P(("dp", "seq")),
            P(),
            P(),
        ),
        check_vma=False,
    )
```

```python
import functools

import jax
import jax.numpy as jnp
from jax import lax
from jax.experimental import pallas as pl
from jax.experimental.layout import Layout, with_layout_constraint
from jax.experimental.pallas import tpu as pltpu
from jax.sharding import PartitionSpec as P

HEADS = 16
KV_HEADS = 8
HEAD = 128
MICRO = 2

EPS = 1e-06
ROPE_BASE = 1000000.0
F32 = jnp.float32
BF16 = jnp.bfloat16
SCALE = HEAD ** (-0.5)
EXP2_SCALE = SCALE * 1.4426950408889634


def dot(left, right):
    return jnp.dot(left, right, preferred_element_type=F32)


def tdot(left, right):
    return lax.dot_general(left, right, (((0,), (0,)), ((), ())), preferred_element_type=F32)


def rdot(left, right):
    return lax.dot_general(left, right, (((1,), (1,)), ((), ())), preferred_element_type=F32)


def norm_back(grads, values, inverse, gain):
    scaled = grads * gain
    return inverse * scaled - values * inverse**3 * jnp.mean(
        scaled * values, axis=-1, keepdims=True
    )


def inv_rms(values):
    return lax.rsqrt(jnp.mean(values * values, axis=-1, keepdims=True) + EPS)


def forward_kernel(tile, group, need, q, k0,v0,k1,v1,k2,v2,k3,v3, seg_q, seg_k, out, log_sum, acc, den):
    rows=q.shape[0]
    tiles=[(g,t) for g in range(group) for t in range(rows//tile)]
    def run(flip, k, v):
        for g,t in tiles:
            cut=slice(t*tile,(t+1)*tile)
            n=(t+1)*tile if flip==0 else rows
            s=rdot(q[cut,g*HEAD:(g+1)*HEAD], k[:n,:])
            ok=seg_q[cut,:]==seg_k[flip:flip+1,:n]
            if flip==0:
                ok&=(lax.broadcasted_iota(jnp.int32,(tile,n),0)+t*tile)>=lax.broadcasted_iota(jnp.int32,(tile,n),1)
            e=jnp.where(ok,jnp.exp2(s*EXP2_SCALE),0.0)
            mixed=dot(e.astype(BF16),v[:n,:])
            total=jnp.sum(e,axis=1,keepdims=True)
            at=slice(g*rows+t*tile,g*rows+(t+1)*tile)
            if flip==0:
                acc[at,:]=mixed; den[at,:]=total
            else:
                acc[at,:]+=mixed; den[at,:]+=total
    run(0,k0,v0)
    for flip,(k,v) in ((1,(k1,v1)),(2,(k2,v2)),(3,(k3,v3))):
        pl.when(need[flip]>0)(functools.partial(run,flip,k,v))
    for g in range(group):
        at=slice(g*rows,(g+1)*rows)
        out[:,g*HEAD:(g+1)*HEAD]=(acc[at,:]/den[at,:]).astype(out.dtype)
    log_sum[0] = jnp.transpose(jnp.broadcast_to(jnp.log2(den[...]), (group * rows, HEAD)))[0:1]

def attend(need, queries, step, parts, seg_q, seg_k, k_cols, group, tile=256):
    rows=parts[0].shape[0]; kv=k_cols//HEAD
    kspec=pl.BlockSpec((rows,HEAD),lambda h,n:(0,h))
    vspec=pl.BlockSpec((rows,HEAD),lambda h,n:(0,h+kv))
    return pl.pallas_call(
        functools.partial(forward_kernel,tile,group),
        grid_spec=pltpu.PrefetchScalarGridSpec(
            num_scalar_prefetch=1, grid=(kv,),
            in_specs=[pl.BlockSpec((rows,group*HEAD),lambda h,n:(step,h))]+[kspec,vspec]*4+[
                pl.BlockSpec((rows,1),lambda h,n:(0,0)), pl.BlockSpec((4,rows),lambda h,n:(0,0))],
            out_specs=[pl.BlockSpec((rows,group*HEAD),lambda h,n:(0,h)), pl.BlockSpec((1,1,group*rows),lambda h,n:(h,0,0))],
            scratch_shapes=[pltpu.VMEM((group*rows,HEAD),F32),pltpu.VMEM((group*rows,1),F32)]),
        out_shape=[jax.ShapeDtypeStruct((rows,kv*group*HEAD),BF16),jax.ShapeDtypeStruct((kv,1,group*rows),F32)],
        name="attend",
    )(need,queries,*[p for part in parts for p in (part,part)],seg_q,seg_k)

def backward_kernel(tile, group, need, q, g_out, heads, k0,v0,k1,v1,k2,v2,k3,v3, seg_q, seg_k, log_sum, dq, d0,d1,d2,d3, acc, delta):
    rows=q.shape[0]
    ones=jnp.ones((8,HEAD),F32)
    for g in range(group):
        lanes=slice(g*HEAD,(g+1)*HEAD)
        product=g_out[:,lanes].astype(F32)*heads[:,lanes].astype(F32)
        delta[:,g*rows:(g+1)*rows]=lax.dot_general(ones,product,(((1,),(1,)),((),())),precision=lax.Precision.HIGHEST,preferred_element_type=F32)
    tiles=[(g,t) for g in range(group) for t in range(rows//tile)]
    def run(flip,k,v,d,dk_acc,dv_acc):
        for idx,(g,t) in enumerate(tiles):
            cut=slice(t*tile,(t+1)*tile)
            at=slice(g*rows+t*tile,g*rows+(t+1)*tile)
            n=(t+1)*tile if flip==0 else rows
            qt=q[cut,g*HEAD:(g+1)*HEAD]; dt=g_out[cut,g*HEAD:(g+1)*HEAD]
            kn=k[:n,:]
            s=rdot(kn,qt)
            ok=seg_k[:n,flip:flip+1]==seg_q[:,cut]
            if flip==0:
                ok&=(lax.broadcasted_iota(jnp.int32,(n,tile),1)+t*tile)>=lax.broadcasted_iota(jnp.int32,(n,tile),0)
            p=jnp.where(ok,jnp.exp2(s*EXP2_SCALE-log_sum[0,0:1,at]),0.0)
            dp=rdot(v[:n,:],dt)
            ds=(p*(dp-delta[0:1,at])).astype(BF16)
            dv=dot(p.astype(BF16),dt)
            dk=dot(ds,qt)
            if idx==0:
                dk_acc[...]=jnp.zeros_like(dk_acc); dv_acc[...]=jnp.zeros_like(dv_acc)
            dk_acc[:n,:]+=dk
            dv_acc[:n,:]+=dv
            back=tdot(ds,kn)*SCALE
            o=(cut,slice(g*HEAD,(g+1)*HEAD))
            if flip==0: dq[o]=back
            else: dq[o]+=back
        d[0]=(dk_acc[...]*SCALE).astype(d.dtype)
        d[1]=dv_acc[...].astype(d.dtype)
    run(0,k0,v0,d0,acc.at[0],acc.at[1])
    for flip,(k,v,d) in ((1,(k1,v1,d1)),(2,(k2,v2,d2)),(3,(k3,v3,d3))):
        pl.when(need[flip]>0)(functools.partial(run,flip,k,v,d,acc.at[0],acc.at[1]))
        def clear(d=d): d[...]=jnp.zeros_like(d)
        pl.when(need[flip]<=0)(clear)

def attend_back(need, queries, grad_heads, heads, step, parts, seg_q, seg_k, log_sum, k_cols, group, tile=256):
    rows=parts[0].shape[0]; kv=k_cols//HEAD
    kspec=pl.BlockSpec((rows,HEAD),lambda h,n:(0,h))
    vspec=pl.BlockSpec((rows,HEAD),lambda h,n:(0,h+kv))
    qspec=pl.BlockSpec((rows,group*HEAD),lambda h,n:(step,h))
    dspec=pl.BlockSpec((2,rows,HEAD),lambda h,n:(0,0,h))
    types=(F32,BF16,F32,BF16)
    return pl.pallas_call(
        functools.partial(backward_kernel,tile,group),
        grid_spec=pltpu.PrefetchScalarGridSpec(
            num_scalar_prefetch=1, grid=(kv,),
            in_specs=[qspec,qspec,pl.BlockSpec((rows,group*HEAD),lambda h,n:(0,h))]+[kspec,vspec]*4+[
                pl.BlockSpec((1,rows),lambda h,n:(0,0)), pl.BlockSpec((rows,4),lambda h,n:(0,0)),
                pl.BlockSpec((1,1,group*rows),lambda h,n:(h,0,0))],
            out_specs=[pl.BlockSpec((rows,group*HEAD),lambda h,n:(0,h))]+[dspec]*4,
            scratch_shapes=[pltpu.VMEM((2,rows,HEAD),F32),pltpu.VMEM((8,group*rows),F32)]),
        out_shape=[jax.ShapeDtypeStruct((rows,kv*group*HEAD),F32)]+[jax.ShapeDtypeStruct((2,rows,k_cols),t) for t in types],
        name="attend_back",
    )(need,queries,grad_heads,heads,*[p for part in parts for p in (part,part)],seg_q,seg_k,log_sum)


def rope_kernel(q_heads, k_heads, raw, turn, gains, queries, pairs):
    cosine, sine = turn[0], turn[1]
    for head in range(q_heads + k_heads):
        values = raw[:, head * HEAD : (head + 1) * HEAD]
        inverse = lax.rsqrt(jnp.mean(values * values, axis=-1, keepdims=True) + EPS)
        gain = gains[0:1] if head < q_heads else gains[1:2]
        scaled = values * inverse * gain
        turned = (scaled * cosine + pltpu.roll(scaled, HEAD // 2, 1) * sine).astype(BF16)
        if head < q_heads:
            queries[:, head * HEAD : (head + 1) * HEAD] = turned
        else:
            at = head - q_heads
            pairs[:, at * HEAD : (at + 1) * HEAD] = turned
    cols = (q_heads + k_heads) * HEAD
    pairs[:, k_heads * HEAD :] = raw[:, cols:].astype(BF16)


def rope(raw, turn, gains, q_cols, k_cols, block=256):
    total = raw.shape[0]
    return pl.pallas_call(
        functools.partial(rope_kernel, q_cols // HEAD, k_cols // HEAD),
        grid=(total // block,),
        in_specs=[
            pl.BlockSpec((block, raw.shape[1]), lambda i: (i, 0)),
            pl.BlockSpec((2, block, HEAD), lambda i: (0, i, 0)),
            pl.BlockSpec((2, HEAD), lambda i: (0, 0)),
        ],
        out_specs=[
            pl.BlockSpec((block, q_cols), lambda i: (i, 0)),
            pl.BlockSpec((block, 2 * k_cols), lambda i: (i, 0)),
        ],
        out_shape=[
            jax.ShapeDtypeStruct((total, q_cols), BF16),
            jax.ShapeDtypeStruct((total, 2 * k_cols), BF16),
        ],
        name="rope",
    )(raw, turn, gains)


def rope_back_kernel(q_heads, k_heads, raw, turn, gains, dq, d_own, d_near, d_far, out, sums):
    cosine, sine = turn[0], turn[1]

    @pl.when(pl.program_id(0) == 0)
    def _():
        sums[...] = jnp.zeros_like(sums)

    for head in range(q_heads + k_heads):
        lanes = slice(head * HEAD, (head + 1) * HEAD)
        which = 0 if head < q_heads else 1
        if which == 0:
            grads = dq[:, lanes]
        else:
            at = slice((head - q_heads) * HEAD, (head - q_heads + 1) * HEAD)
            grads = d_own[0, :, at] + d_near[0, :, at].astype(F32) + d_far[0, :, at].astype(F32)
        values = raw[:, lanes]
        inverse = lax.rsqrt(jnp.mean(values * values, axis=-1, keepdims=True) + EPS)
        unit = values * inverse
        turned = grads * cosine - pltpu.roll(grads, HEAD // 2, 1) * sine
        sums[which : which + 1] += jnp.sum(turned * unit, axis=0, keepdims=True)
        scaled = turned * gains[which : which + 1]
        mean = jnp.mean(scaled * unit, axis=-1, keepdims=True)
        out[:, lanes] = (inverse * (scaled - unit * mean)).astype(BF16)
    cols = (q_heads + k_heads) * HEAD
    out[:, cols:] = (d_own[1] + d_near[1].astype(F32) + d_far[1].astype(F32)).astype(BF16)


def rope_back(raw, turn, gains, dq, d_own, d_near, d_far, step, q_cols, k_cols, block=256):
    rows = dq.shape[0]
    base = step * (rows // block)
    cols = q_cols + 2 * k_cols
    dspec = pl.BlockSpec((2, block, k_cols), lambda i: (0, i, 0))
    return pl.pallas_call(
        functools.partial(rope_back_kernel, q_cols // HEAD, k_cols // HEAD),
        grid=(rows // block,),
        in_specs=[
            pl.BlockSpec((block, cols), lambda i: (base + i, 0)),
            pl.BlockSpec((2, block, HEAD), lambda i: (0, base + i, 0)),
            pl.BlockSpec((2, HEAD), lambda i: (0, 0)),
            pl.BlockSpec((block, q_cols), lambda i: (i, 0)),
            dspec,
            dspec,
            dspec,
        ],
        out_specs=[
            pl.BlockSpec((block, cols), lambda i: (i, 0)),
            pl.BlockSpec((2, HEAD), lambda i: (0, 0)),
        ],
        out_shape=[
            jax.ShapeDtypeStruct((rows, cols), BF16),
            jax.ShapeDtypeStruct((2, HEAD), F32),
        ],
        name="rope_back",
    )(raw, turn, gains, dq, d_own, d_near, d_far)


def make_local(mp_size, seq_size, dp_size):
    data_axes = ("dp", "seq")
    pair = [(i, i ^ 1) for i in range(seq_size)]
    up_pairs = [(i, i + 2) for i in range(seq_size - 2)]
    down_pairs = [(i + 2, i) for i in range(seq_size - 2)]

    def scatter(grad):
        return lax.psum_scatter(grad, data_axes, scatter_dimension=0, tiled=True)

    def mp_other(part):
        if mp_size == 2:
            return lax.ppermute(part, "mp", [(0, 1), (1, 0)])
        return (lax.psum(part.astype(F32), "mp") - part.astype(F32)).astype(BF16)

    def mp_part(part):
        part = lax.optimization_barrier(part.astype(BF16))
        return part, mp_other(part)

    def butterfly(value, axis, size):
        flip = 1
        while flip < size:
            moves = [(i, i ^ flip) for i in range(size)]
            value = value + lax.ppermute(value, axis, moves)
            flip *= 2
        return value

    def mp_sum(part):
        mine, other = mp_part(part)
        return mine.astype(F32) + other.astype(F32)

    def local(
        hidden,
        w_query,
        w_key,
        w_value,
        w_out,
        w_gate,
        w_up,
        w_down,
        norm_attn,
        norm_ffn,
        norm_query,
        norm_key,
        segments,
        positions,
        cotangent,
    ):
        rows = hidden.shape[2]
        width = hidden.shape[3]
        total = MICRO * rows
        q_cols = w_query.shape[1]
        k_cols = w_key.shape[1]
        group = HEADS // KV_HEADS
        rank = lax.axis_index("seq")
        own_rows = w_query.shape[0]

        gains = jnp.concatenate(
            [
                jnp.broadcast_to(norm_attn[:, None], (own_rows, 64)),
                jnp.broadcast_to(norm_ffn[:, None], (own_rows, 64)),
            ],
            axis=1,
        )
        first = jnp.concatenate([w_query, w_key, w_value, w_out.T, gains], axis=1)
        first = lax.all_gather(first, data_axes, axis=0, tiled=True)
        second = jnp.stack([w_gate, w_up, w_down.T])
        second, first = lax.optimization_barrier((second, first))
        second = lax.all_gather(second, data_axes, axis=1, tiled=True)
        tokens = hidden.reshape(total, width).astype(F32)
        inv_attn = inv_rms(tokens)
        frequency = ROPE_BASE ** (-(jnp.arange(HEAD // 2, dtype=F32) * 2.0) / HEAD)
        angles = positions.reshape(total).astype(F32)[:, None] * frequency[None, :]
        cosine = jnp.cos(angles)
        sine = jnp.sin(angles)
        turn = jnp.stack(
            [
                jnp.concatenate([cosine, cosine], axis=-1),
                jnp.concatenate([-sine, sine], axis=-1),
            ]
        )
        seg_own = segments[:, 0]
        seg_pair = lax.ppermute(seg_own, "seq", pair)
        both = jnp.stack([seg_own, seg_pair])
        both_x = lax.ppermute(both, "seq", up_pairs)
        seg_keys = jnp.stack([both[0], both[1], both_x[0], both_x[1]])
        flips = jnp.arange(4, dtype=jnp.int32)
        near_enough = (seg_keys[:, :, -1] == seg_own[None, :, 0]) | (flips[:, None] == 0)
        need = (near_enough & (jnp.bitwise_xor(rank, flips)[:, None] <= rank)).astype(jnp.int32)
        first, turn, inv_attn, seg_keys, need = lax.optimization_barrier(
            (first, turn, inv_attn, seg_keys, need)
        )
        qkv_cols = q_cols + 2 * k_cols
        w_qkv = first[:, :qkv_cols]
        w_out_t = first[:, qkv_cols : qkv_cols + q_cols]
        gain_attn = first[:, qkv_cols + q_cols].astype(F32)
        gain_ffn = first[:, qkv_cols + q_cols + 64].astype(F32)
        gate_full, up_full, down_t = second[0], second[1], second[2]
        gain_heads = jnp.stack([norm_query, norm_key]).astype(F32)

        cot = lax.optimization_barrier(cotangent.reshape(total, width))

        normed_attn = (tokens * inv_attn * gain_attn).astype(BF16)
        raw = dot(normed_attn, w_qkv)
        queries, pairs = rope(raw, turn, gain_heads, q_cols, k_cols)

        kept = []
        middles = []
        heads_out = []
        for step in range(MICRO):
            cut = slice(step * rows, (step + 1) * rows)
            own = pairs[cut]
            near = lax.ppermute(own, "seq", pair)
            far = lax.ppermute(own, "seq", up_pairs)
            far_near = lax.ppermute(far, "seq", pair)
            parts = (own, near, far, far_near)
            attn_heads, log_sum = attend(
                need[:, step],
                queries,
                step,
                parts,
                seg_own[step][:, None],
                seg_keys[:, step],
                k_cols,
                group,
                rows,
            )
            heads_out.append(attn_heads)
            kept.append((parts, log_sum))
            attn_part = rdot(attn_heads, w_out_t)
            middles.append(tokens[cut] + mp_sum(attn_part))
        middle = jnp.concatenate(middles, axis=0)
        attn_heads = jnp.concatenate(heads_out, axis=0)

        inv_ffn = inv_rms(middle)
        normed_ffn = (middle * inv_ffn * gain_ffn).astype(BF16)
        gate = dot(normed_ffn, gate_full)
        upward = dot(normed_ffn, up_full)
        sigma = jax.nn.sigmoid(gate)
        silu = gate * sigma
        act = (silu * upward).astype(BF16)
        down_grad = tdot(cot, act).astype(BF16)
        down_grad = with_layout_constraint(down_grad, Layout((0, 1)))
        down_owned = scatter(down_grad)
        cot_late, act, down_grad = lax.optimization_barrier((cot, act, down_grad))
        grad_act = dot(cot_late, down_t)
        grad_gate_in = (grad_act * upward * sigma * (1.0 + gate * (1.0 - sigma))).astype(BF16)
        grad_up_in = (grad_act * silu).astype(BF16)
        backs = []
        for step in range(MICRO):
            cut = slice(step * rows, (step + 1) * rows)
            backs.append(
                mp_part(rdot(grad_gate_in[cut], gate_full) + rdot(grad_up_in[cut], up_full))
            )
        gate_grad = tdot(normed_ffn, grad_gate_in).astype(BF16)
        gate_owned = scatter(gate_grad)
        up_grad = tdot(normed_ffn, grad_up_in).astype(BF16)
        up_owned = scatter(up_grad)
        down_mine = lax.optimization_barrier(rdot(act, down_t).astype(BF16))
        backs, gate_grad, up_grad, down_mine = lax.optimization_barrier(
            (backs, gate_grad, up_grad, down_mine)
        )
        down_other = mp_other(down_mine)
        gain_ffn_part = jnp.concatenate([mine for mine, _ in backs], axis=0).astype(F32)
        gain_ffn_part = jnp.sum(gain_ffn_part * middle * inv_ffn, axis=0)
        backs = [mine.astype(F32) + other.astype(F32) for mine, other in backs]
        grad_normed_ffn = jnp.concatenate(backs, axis=0)
        grad_middle = cot.astype(F32) + norm_back(grad_normed_ffn, middle, inv_ffn, gain_ffn)
        grad_middle_b = grad_middle.astype(BF16)
        grad_heads = dot(grad_middle_b, w_out_t).astype(BF16)
        out_owned = scatter(tdot(grad_middle_b, attn_heads).astype(BF16))

        grads_in = []
        head_sums = []
        sides = []
        for step in range(MICRO):
            parts, log_sum = kept[step]
            grad_q, d_own, d_near, d_far, d_far_near = attend_back(
                need[:, step],
                queries,
                grad_heads,
                heads_out[step],
                step,
                parts,
                seg_own[step][None],
                seg_keys[:, step].T,
                log_sum,
                k_cols,
                group,
                rows,
            )
            got = lax.ppermute(d_near, "seq", pair)
            got_far = lax.ppermute(d_far_near, "seq", pair)
            far = lax.ppermute(
                (d_far + got_far.astype(F32)).astype(BF16), "seq", down_pairs
            )
            sides.append((grad_q, d_own, got, far))
        for step in range(MICRO):
            if step == MICRO - 1:
                down_other, down_owned, side = lax.optimization_barrier(
                    (down_other, down_owned, sides[step])
                )
            else:
                side = sides[step]
            grad_in, sums = rope_back(raw, turn, gain_heads, *side, step, q_cols, k_cols)
            grads_in.append(grad_in)
            head_sums.append(sums)
        layer_out = (middle + (down_mine.astype(F32) + down_other.astype(F32))).astype(BF16)
        backs = [mp_part(rdot(grad_in, w_qkv)) for grad_in in grads_in]
        grad_qkv_in = jnp.concatenate(grads_in, axis=0)
        mines = [mine for mine, _ in backs]
        grad_qkv_in, gate_owned, mines = lax.optimization_barrier(
            (grad_qkv_in, gate_owned, mines)
        )
        qkv_owned = scatter(tdot(normed_attn, grad_qkv_in).astype(BF16))
        gain_attn_part = jnp.concatenate([mine for mine, _ in backs], axis=0).astype(F32)
        gain_attn_part = jnp.sum(gain_attn_part * tokens * inv_attn, axis=0)
        head_sum = (head_sums[0] + head_sums[1]).reshape(-1)
        small = jnp.concatenate([gain_attn_part, gain_ffn_part, head_sum]).reshape(-1, HEAD)
        small = butterfly(small, "seq", seq_size)
        small = butterfly(small, "dp", dp_size)
        small = butterfly(small, "mp", mp_size).reshape(-1)
        head_sum = small[2 * width :]
        owner = (lax.axis_index("dp") * seq_size + rank) * own_rows
        wide_sum = small[: 2 * width].reshape(2, width)
        wide_sum = lax.dynamic_slice_in_dim(wide_sum, owner, own_rows, 1)

        grad_normed_attn = jnp.concatenate(
            [mine.astype(F32) + other.astype(F32) for mine, other in backs], axis=0
        )
        grad_tokens = (
            grad_middle + norm_back(grad_normed_attn, tokens, inv_attn, gain_attn)
        ).astype(BF16)

        qkv_owned = qkv_owned.astype(F32)
        return (
            layer_out.reshape(MICRO, 1, rows, width),
            grad_tokens.reshape(MICRO, 1, rows, width),
            qkv_owned[:, :q_cols],
            qkv_owned[:, q_cols : q_cols + k_cols],
            qkv_owned[:, q_cols + k_cols :],
            out_owned.T.astype(F32),
            gate_owned.astype(F32),
            up_owned.astype(F32),
            down_owned.T.astype(F32),
            wide_sum[0],
            wide_sum[1],
            head_sum[:HEAD],
            head_sum[HEAD:],
        )

    return local


def solution(mesh):
    return jax.shard_map(
        make_local(mesh.shape["mp"], mesh.shape["seq"], mesh.shape["dp"]),
        mesh=mesh,
        in_specs=(
            P(None, "dp", "seq", None),
            P(("dp", "seq"), "mp"),
            P(("dp", "seq"), "mp"),
            P(("dp", "seq"), "mp"),
            P("mp", ("dp", "seq")),
            P(("dp", "seq"), "mp"),
            P(("dp", "seq"), "mp"),
            P("mp", ("dp", "seq")),
            P(("dp", "seq")),
            P(("dp", "seq")),
            P(),
            P(),
            P(None, "dp", "seq"),
            P(None, "dp", "seq"),
            P(None, "dp", "seq", None),
        ),
        out_specs=(
            P(None, "dp", "seq", None),
            P(None, "dp", "seq", None),
            P(("dp", "seq"), "mp"),
            P(("dp", "seq"), "mp"),
            P(("dp", "seq"), "mp"),
            P("mp", ("dp", "seq")),
            P(("dp", "seq"), "mp"),
            P(("dp", "seq"), "mp"),
            P("mp", ("dp", "seq")),
            P(("dp", "seq")),
            P(("dp", "seq")),
            P(),
            P(),
        ),
        check_vma=False,
    )
```

```python
import functools

import jax
import jax.numpy as jnp
from jax import lax
from jax.experimental import pallas as pl
from jax.experimental.layout import Layout, with_layout_constraint
from jax.experimental.pallas import tpu as pltpu
from jax.sharding import PartitionSpec as P

HEADS = 16
KV_HEADS = 8
HEAD = 128
MICRO = 2

EPS = 1e-06
ROPE_BASE = 1000000.0
F32 = jnp.float32
BF16 = jnp.bfloat16
SCALE = HEAD ** (-0.5)
EXP2_SCALE = SCALE * 1.4426950408889634


def dot(left, right):
    return jnp.dot(left, right, preferred_element_type=F32)


def tdot(left, right):
    return lax.dot_general(left, right, (((0,), (0,)), ((), ())), preferred_element_type=F32)


def rdot(left, right):
    return lax.dot_general(left, right, (((1,), (1,)), ((), ())), preferred_element_type=F32)


def norm_back(grads, values, inverse, gain):
    scaled = grads * gain
    return inverse * scaled - values * inverse**3 * jnp.mean(
        scaled * values, axis=-1, keepdims=True
    )


def inv_rms(values):
    return lax.rsqrt(jnp.mean(values * values, axis=-1, keepdims=True) + EPS)


def forward_kernel(tile, group, need, q, k0,v0,k1,v1,k2,v2,k3,v3, seg_q, seg_k, out, log_sum, acc, den):
    rows=q.shape[0]
    tiles=[(g,t) for g in range(group) for t in range(rows//tile)]
    def run(flip, k, v):
        for g,t in tiles:
            cut=slice(t*tile,(t+1)*tile)
            n=(t+1)*tile if flip==0 else rows
            s=rdot(q[cut,g*HEAD:(g+1)*HEAD], k[:n,:])
            ok=seg_q[cut,:]==seg_k[flip:flip+1,:n]
            if flip==0:
                ok&=(lax.broadcasted_iota(jnp.int32,(tile,n),0)+t*tile)>=lax.broadcasted_iota(jnp.int32,(tile,n),1)
            e=jnp.where(ok,jnp.exp2(s*EXP2_SCALE),0.0)
            mixed=dot(e.astype(BF16),v[:n,:])
            total=jnp.sum(e,axis=1,keepdims=True)
            at=slice(g*rows+t*tile,g*rows+(t+1)*tile)
            if flip==0:
                acc[at,:]=mixed; den[at,:]=total
            else:
                acc[at,:]+=mixed; den[at,:]+=total
    run(0,k0,v0)
    for flip,(k,v) in ((1,(k1,v1)),(2,(k2,v2)),(3,(k3,v3))):
        pl.when(need[flip]>0)(functools.partial(run,flip,k,v))
    for g in range(group):
        at=slice(g*rows,(g+1)*rows)
        out[:,g*HEAD:(g+1)*HEAD]=(acc[at,:]/den[at,:]).astype(out.dtype)
    log_sum[0] = jnp.transpose(jnp.broadcast_to(jnp.log2(den[...]), (group * rows, HEAD)))[0:1]

def attend(need, queries, step, parts, seg_q, seg_k, k_cols, group, tile=256):
    rows=parts[0].shape[0]; kv=k_cols//HEAD
    kspec=pl.BlockSpec((rows,HEAD),lambda h,n:(0,h))
    vspec=pl.BlockSpec((rows,HEAD),lambda h,n:(0,h+kv))
    return pl.pallas_call(
        functools.partial(forward_kernel,tile,group),
        grid_spec=pltpu.PrefetchScalarGridSpec(
            num_scalar_prefetch=1, grid=(kv,),
            in_specs=[pl.BlockSpec((rows,group*HEAD),lambda h,n:(step,h))]+[kspec,vspec]*4+[
                pl.BlockSpec((rows,1),lambda h,n:(0,0)), pl.BlockSpec((4,rows),lambda h,n:(0,0))],
            out_specs=[pl.BlockSpec((rows,group*HEAD),lambda h,n:(0,h)), pl.BlockSpec((1,1,group*rows),lambda h,n:(h,0,0))],
            scratch_shapes=[pltpu.VMEM((group*rows,HEAD),F32),pltpu.VMEM((group*rows,1),F32)]),
        out_shape=[jax.ShapeDtypeStruct((rows,kv*group*HEAD),BF16),jax.ShapeDtypeStruct((kv,1,group*rows),F32)],
        name="attend",
    )(need,queries,*[p for part in parts for p in (part,part)],seg_q,seg_k)

def backward_kernel(tile, group, need, q, g_out, heads, k0,v0,k1,v1,k2,v2,k3,v3, seg_q, seg_k, log_sum, dq, d0,d1,d2,d3, acc, delta):
    rows=q.shape[0]
    ones=jnp.ones((8,HEAD),F32)
    for g in range(group):
        lanes=slice(g*HEAD,(g+1)*HEAD)
        product=g_out[:,lanes].astype(F32)*heads[:,lanes].astype(F32)
        delta[:,g*rows:(g+1)*rows]=lax.dot_general(ones,product,(((1,),(1,)),((),())),precision=lax.Precision.HIGHEST,preferred_element_type=F32)
    tiles=[(g,t) for g in range(group) for t in range(rows//tile)]
    def run(flip,k,v,d,dk_acc,dv_acc):
        for idx,(g,t) in enumerate(tiles):
            cut=slice(t*tile,(t+1)*tile)
            at=slice(g*rows+t*tile,g*rows+(t+1)*tile)
            n=(t+1)*tile if flip==0 else rows
            qt=q[cut,g*HEAD:(g+1)*HEAD]; dt=g_out[cut,g*HEAD:(g+1)*HEAD]
            kn=k[:n,:]
            s=rdot(kn,qt)
            ok=seg_k[:n,flip:flip+1]==seg_q[:,cut]
            if flip==0:
                ok&=(lax.broadcasted_iota(jnp.int32,(n,tile),1)+t*tile)>=lax.broadcasted_iota(jnp.int32,(n,tile),0)
            p=jnp.where(ok,jnp.exp2(s*EXP2_SCALE-log_sum[0,0:1,at]),0.0)
            dp=rdot(v[:n,:],dt)
            ds=(p*(dp-delta[0:1,at])).astype(BF16)
            dv=dot(p.astype(BF16),dt)
            dk=dot(ds,qt)
            if idx==0:
                dk_acc[...]=jnp.zeros_like(dk_acc); dv_acc[...]=jnp.zeros_like(dv_acc)
            dk_acc[:n,:]+=dk
            dv_acc[:n,:]+=dv
            back=tdot(ds,kn)*SCALE
            o=(cut,slice(g*HEAD,(g+1)*HEAD))
            if flip==0: dq[o]=back
            else: dq[o]+=back
        d[0]=(dk_acc[...]*SCALE).astype(d.dtype)
        d[1]=dv_acc[...].astype(d.dtype)
    run(0,k0,v0,d0,acc.at[0],acc.at[1])
    for flip,(k,v,d) in ((1,(k1,v1,d1)),(2,(k2,v2,d2)),(3,(k3,v3,d3))):
        pl.when(need[flip]>0)(functools.partial(run,flip,k,v,d,acc.at[0],acc.at[1]))
        def clear(d=d): d[...]=jnp.zeros_like(d)
        pl.when(need[flip]<=0)(clear)

def attend_back(need, queries, grad_heads, heads, step, parts, seg_q, seg_k, log_sum, k_cols, group, tile=256):
    rows=parts[0].shape[0]; kv=k_cols//HEAD
    kspec=pl.BlockSpec((rows,HEAD),lambda h,n:(0,h))
    vspec=pl.BlockSpec((rows,HEAD),lambda h,n:(0,h+kv))
    qspec=pl.BlockSpec((rows,group*HEAD),lambda h,n:(step,h))
    dspec=pl.BlockSpec((2,rows,HEAD),lambda h,n:(0,0,h))
    types=(F32,BF16,F32,BF16)
    return pl.pallas_call(
        functools.partial(backward_kernel,tile,group),
        grid_spec=pltpu.PrefetchScalarGridSpec(
            num_scalar_prefetch=1, grid=(kv,),
            in_specs=[qspec,qspec,pl.BlockSpec((rows,group*HEAD),lambda h,n:(0,h))]+[kspec,vspec]*4+[
                pl.BlockSpec((1,rows),lambda h,n:(0,0)), pl.BlockSpec((rows,4),lambda h,n:(0,0)),
                pl.BlockSpec((1,1,group*rows),lambda h,n:(h,0,0))],
            out_specs=[pl.BlockSpec((rows,group*HEAD),lambda h,n:(0,h))]+[dspec]*4,
            scratch_shapes=[pltpu.VMEM((2,rows,HEAD),F32),pltpu.VMEM((8,group*rows),F32)]),
        out_shape=[jax.ShapeDtypeStruct((rows,kv*group*HEAD),F32)]+[jax.ShapeDtypeStruct((2,rows,k_cols),t) for t in types],
        name="attend_back",
    )(need,queries,grad_heads,heads,*[p for part in parts for p in (part,part)],seg_q,seg_k,log_sum)


def rope_kernel(q_heads, k_heads, raw, turn, gains, queries, pairs):
    cosine, sine = turn[0], turn[1]
    for head in range(q_heads + k_heads):
        values = raw[:, head * HEAD : (head + 1) * HEAD]
        inverse = lax.rsqrt(jnp.mean(values * values, axis=-1, keepdims=True) + EPS)
        gain = gains[0:1] if head < q_heads else gains[1:2]
        scaled = values * inverse * gain
        turned = (scaled * cosine + pltpu.roll(scaled, HEAD // 2, 1) * sine).astype(BF16)
        if head < q_heads:
            queries[:, head * HEAD : (head + 1) * HEAD] = turned
        else:
            at = head - q_heads
            pairs[:, at * HEAD : (at + 1) * HEAD] = turned
    cols = (q_heads + k_heads) * HEAD
    pairs[:, k_heads * HEAD :] = raw[:, cols:].astype(BF16)


def rope(raw, turn, gains, q_cols, k_cols, block=256):
    total = raw.shape[0]
    return pl.pallas_call(
        functools.partial(rope_kernel, q_cols // HEAD, k_cols // HEAD),
        grid=(total // block,),
        in_specs=[
            pl.BlockSpec((block, raw.shape[1]), lambda i: (i, 0)),
            pl.BlockSpec((2, block, HEAD), lambda i: (0, i, 0)),
            pl.BlockSpec((2, HEAD), lambda i: (0, 0)),
        ],
        out_specs=[
            pl.BlockSpec((block, q_cols), lambda i: (i, 0)),
            pl.BlockSpec((block, 2 * k_cols), lambda i: (i, 0)),
        ],
        out_shape=[
            jax.ShapeDtypeStruct((total, q_cols), BF16),
            jax.ShapeDtypeStruct((total, 2 * k_cols), BF16),
        ],
        name="rope",
    )(raw, turn, gains)


def rope_back_kernel(q_heads, k_heads, raw, turn, gains, dq, d_own, d_near, d_far, out, sums):
    cosine, sine = turn[0], turn[1]

    @pl.when(pl.program_id(0) == 0)
    def _():
        sums[...] = jnp.zeros_like(sums)

    for head in range(q_heads + k_heads):
        lanes = slice(head * HEAD, (head + 1) * HEAD)
        which = 0 if head < q_heads else 1
        if which == 0:
            grads = dq[:, lanes]
        else:
            at = slice((head - q_heads) * HEAD, (head - q_heads + 1) * HEAD)
            grads = d_own[0, :, at] + d_near[0, :, at].astype(F32) + d_far[0, :, at].astype(F32)
        values = raw[:, lanes]
        inverse = lax.rsqrt(jnp.mean(values * values, axis=-1, keepdims=True) + EPS)
        unit = values * inverse
        turned = grads * cosine - pltpu.roll(grads, HEAD // 2, 1) * sine
        sums[which : which + 1] += jnp.sum(turned * unit, axis=0, keepdims=True)
        scaled = turned * gains[which : which + 1]
        mean = jnp.mean(scaled * unit, axis=-1, keepdims=True)
        out[:, lanes] = (inverse * (scaled - unit * mean)).astype(BF16)
    cols = (q_heads + k_heads) * HEAD
    out[:, cols:] = (d_own[1] + d_near[1].astype(F32) + d_far[1].astype(F32)).astype(BF16)


def rope_back(raw, turn, gains, dq, d_own, d_near, d_far, step, q_cols, k_cols, block=256):
    rows = dq.shape[0]
    base = step * (rows // block)
    cols = q_cols + 2 * k_cols
    dspec = pl.BlockSpec((2, block, k_cols), lambda i: (0, i, 0))
    return pl.pallas_call(
        functools.partial(rope_back_kernel, q_cols // HEAD, k_cols // HEAD),
        grid=(rows // block,),
        in_specs=[
            pl.BlockSpec((block, cols), lambda i: (base + i, 0)),
            pl.BlockSpec((2, block, HEAD), lambda i: (0, base + i, 0)),
            pl.BlockSpec((2, HEAD), lambda i: (0, 0)),
            pl.BlockSpec((block, q_cols), lambda i: (i, 0)),
            dspec,
            dspec,
            dspec,
        ],
        out_specs=[
            pl.BlockSpec((block, cols), lambda i: (i, 0)),
            pl.BlockSpec((2, HEAD), lambda i: (0, 0)),
        ],
        out_shape=[
            jax.ShapeDtypeStruct((rows, cols), BF16),
            jax.ShapeDtypeStruct((2, HEAD), F32),
        ],
        name="rope_back",
    )(raw, turn, gains, dq, d_own, d_near, d_far)


def move_kernel(rank, source, out):
    out[...] = source[...]


def relative(values, rank, dp_size, seq_size):
    total, width = values.shape
    lanes = width // (dp_size * seq_size)

    def pick(step, rank):
        turn = step // dp_size
        flip = (turn % 2) * 2 + turn // 2
        return (0, (step % dp_size) * seq_size + jnp.bitwise_xor(rank[0], flip))

    return pl.pallas_call(
        move_kernel,
        grid_spec=pltpu.PrefetchScalarGridSpec(
            num_scalar_prefetch=1,
            grid=(dp_size * seq_size,),
            in_specs=[pl.BlockSpec((total, lanes), pick)],
            out_specs=pl.BlockSpec((total, lanes), lambda step, rank: (0, step)),
        ),
        out_shape=jax.ShapeDtypeStruct(values.shape, values.dtype),
        name="relative",
    )(rank.reshape(1).astype(jnp.int32), values)


def make_local(mp_size, seq_size, dp_size):
    data_axes = ("dp", "seq")
    pair = [(i, i ^ 1) for i in range(seq_size)]
    up_pairs = [(i, i + 2) for i in range(seq_size - 2)]
    down_pairs = [(i + 2, i) for i in range(seq_size - 2)]
    cross = [(i, i ^ 2) for i in range(seq_size)]

    def scatter(grad):
        return lax.psum_scatter(grad, data_axes, scatter_dimension=0, tiled=True)

    def mp_other(part):
        if mp_size == 2:
            return lax.ppermute(part, "mp", [(0, 1), (1, 0)])
        return (lax.psum(part.astype(F32), "mp") - part.astype(F32)).astype(BF16)

    def mp_part(part):
        part = lax.optimization_barrier(part.astype(BF16))
        return part, mp_other(part)

    def pair_stage(left, right):
        half = left.shape[1] // 2
        theirs = tdot(left[:, half:], right).astype(BF16)
        got = lax.ppermute(theirs, "seq", pair)
        return (tdot(left[:, :half], right) + got.astype(F32)).astype(BF16)

    def cross_stage(block):
        half = block.shape[0] // 2
        got = lax.ppermute(block[half:], "seq", cross)
        return (block[:half].astype(F32) + got.astype(F32)).astype(BF16)

    def line_stage(block):
        place = lax.axis_index("dp")
        blocks = block.reshape(dp_size, -1, block.shape[1])
        owned = lax.dynamic_index_in_dim(blocks, place, 0, False).astype(F32)
        for flip in range(1, dp_size):
            sent = lax.dynamic_index_in_dim(blocks, jnp.bitwise_xor(place, flip), 0, False)
            moves = [(i, i ^ flip) for i in range(dp_size)]
            owned = owned + lax.ppermute(sent, "dp", moves).astype(F32)
        return owned

    def butterfly(value, axis, size):
        flip = 1
        while flip < size:
            moves = [(i, i ^ flip) for i in range(size)]
            value = value + lax.ppermute(value, axis, moves)
            flip *= 2
        return value

    def mp_sum(part):
        mine, other = mp_part(part)
        return mine.astype(F32) + other.astype(F32)

    def local(
        hidden,
        w_query,
        w_key,
        w_value,
        w_out,
        w_gate,
        w_up,
        w_down,
        norm_attn,
        norm_ffn,
        norm_query,
        norm_key,
        segments,
        positions,
        cotangent,
    ):
        rows = hidden.shape[2]
        width = hidden.shape[3]
        total = MICRO * rows
        q_cols = w_query.shape[1]
        k_cols = w_key.shape[1]
        group = HEADS // KV_HEADS
        rank = lax.axis_index("seq")
        own_rows = w_query.shape[0]

        gains = jnp.concatenate(
            [
                jnp.broadcast_to(norm_attn[:, None], (own_rows, 64)),
                jnp.broadcast_to(norm_ffn[:, None], (own_rows, 64)),
            ],
            axis=1,
        )
        first = jnp.concatenate([w_query, w_key, w_value, w_out.T, gains], axis=1)
        first = lax.all_gather(first, data_axes, axis=0, tiled=True)
        second = jnp.stack([w_gate, w_up, w_down.T])
        second, first = lax.optimization_barrier((second, first))
        second = lax.all_gather(second, data_axes, axis=1, tiled=True)
        tokens = hidden.reshape(total, width).astype(F32)
        inv_attn = inv_rms(tokens)
        frequency = ROPE_BASE ** (-(jnp.arange(HEAD // 2, dtype=F32) * 2.0) / HEAD)
        angles = positions.reshape(total).astype(F32)[:, None] * frequency[None, :]
        cosine = jnp.cos(angles)
        sine = jnp.sin(angles)
        turn = jnp.stack(
            [
                jnp.concatenate([cosine, cosine], axis=-1),
                jnp.concatenate([-sine, sine], axis=-1),
            ]
        )
        seg_own = segments[:, 0]
        seg_pair = lax.ppermute(seg_own, "seq", pair)
        both = jnp.stack([seg_own, seg_pair])
        both_x = lax.ppermute(both, "seq", up_pairs)
        seg_keys = jnp.stack([both[0], both[1], both_x[0], both_x[1]])
        flips = jnp.arange(4, dtype=jnp.int32)
        near_enough = (seg_keys[:, :, -1] == seg_own[None, :, 0]) | (flips[:, None] == 0)
        need = (near_enough & (jnp.bitwise_xor(rank, flips)[:, None] <= rank)).astype(jnp.int32)
        first, turn, inv_attn, seg_keys, need = lax.optimization_barrier(
            (first, turn, inv_attn, seg_keys, need)
        )
        qkv_cols = q_cols + 2 * k_cols
        w_qkv = first[:, :qkv_cols]
        w_out_t = first[:, qkv_cols : qkv_cols + q_cols]
        gain_attn = first[:, qkv_cols + q_cols].astype(F32)
        gain_ffn = first[:, qkv_cols + q_cols + 64].astype(F32)
        gate_full, up_full, down_t = second[0], second[1], second[2]
        gain_heads = jnp.stack([norm_query, norm_key]).astype(F32)

        cot = lax.optimization_barrier(cotangent.reshape(total, width))

        normed_attn = (tokens * inv_attn * gain_attn).astype(BF16)
        raw = dot(normed_attn, w_qkv)
        queries, pairs = rope(raw, turn, gain_heads, q_cols, k_cols)

        kept = []
        middles = []
        heads_out = []
        for step in range(MICRO):
            cut = slice(step * rows, (step + 1) * rows)
            own = pairs[cut]
            near = lax.ppermute(own, "seq", pair)
            far = lax.ppermute(own, "seq", up_pairs)
            far_near = lax.ppermute(far, "seq", pair)
            parts = (own, near, far, far_near)
            attn_heads, log_sum = attend(
                need[:, step],
                queries,
                step,
                parts,
                seg_own[step][:, None],
                seg_keys[:, step],
                k_cols,
                group,
                rows,
            )
            heads_out.append(attn_heads)
            kept.append((parts, log_sum))
            attn_part = rdot(attn_heads, w_out_t)
            middles.append(tokens[cut] + mp_sum(attn_part))
        middle = jnp.concatenate(middles, axis=0)
        attn_heads = jnp.concatenate(heads_out, axis=0)

        inv_ffn = inv_rms(middle)
        normed_ffn = (middle * inv_ffn * gain_ffn).astype(BF16)
        gate = dot(normed_ffn, gate_full)
        upward = dot(normed_ffn, up_full)
        sigma = jax.nn.sigmoid(gate)
        silu = gate * sigma
        act = (silu * upward).astype(BF16)
        down_grad = tdot(cot, act).astype(BF16)
        down_grad = with_layout_constraint(down_grad, Layout((0, 1)))
        down_owned = scatter(down_grad)
        cot_late, act, down_grad = lax.optimization_barrier((cot, act, down_grad))
        grad_act = dot(cot_late, down_t)
        grad_gate_in = (grad_act * upward * sigma * (1.0 + gate * (1.0 - sigma))).astype(BF16)
        grad_up_in = (grad_act * silu).astype(BF16)
        backs = []
        for step in range(MICRO):
            cut = slice(step * rows, (step + 1) * rows)
            backs.append(
                mp_part(rdot(grad_gate_in[cut], gate_full) + rdot(grad_up_in[cut], up_full))
            )
        ffn_rel = relative(normed_ffn, rank, dp_size, seq_size)
        up_block = pair_stage(ffn_rel, grad_up_in)
        gate_grad = tdot(normed_ffn, grad_gate_in).astype(BF16)
        gate_owned = scatter(gate_grad)
        down_mine = lax.optimization_barrier(rdot(act, down_t).astype(BF16))
        backs, gate_grad, up_block, down_mine = lax.optimization_barrier(
            (backs, gate_grad, up_block, down_mine)
        )
        down_other = mp_other(down_mine)
        gain_ffn_part = jnp.concatenate([mine for mine, _ in backs], axis=0).astype(F32)
        gain_ffn_part = jnp.sum(gain_ffn_part * middle * inv_ffn, axis=0)
        backs = [mine.astype(F32) + other.astype(F32) for mine, other in backs]
        grad_normed_ffn = jnp.concatenate(backs, axis=0)
        grad_middle = cot.astype(F32) + norm_back(grad_normed_ffn, middle, inv_ffn, gain_ffn)
        grad_middle_b = grad_middle.astype(BF16)
        grad_heads = dot(grad_middle_b, w_out_t).astype(BF16)
        out_owned = scatter(tdot(grad_middle_b, attn_heads).astype(BF16))
        up_block = cross_stage(up_block)

        grads_in = []
        head_sums = []
        sides = []
        for step in range(MICRO):
            parts, log_sum = kept[step]
            grad_q, d_own, d_near, d_far, d_far_near = attend_back(
                need[:, step],
                queries,
                grad_heads,
                heads_out[step],
                step,
                parts,
                seg_own[step][None],
                seg_keys[:, step].T,
                log_sum,
                k_cols,
                group,
                rows,
            )
            got = lax.ppermute(d_near, "seq", pair)
            got_far = lax.ppermute(d_far_near, "seq", pair)
            far = lax.ppermute(
                (d_far + got_far.astype(F32)).astype(BF16), "seq", down_pairs
            )
            if step == 0:
                up_block, d_own = lax.optimization_barrier((up_block, d_own))
                up_owned = line_stage(up_block)
            sides.append((grad_q, d_own, got, far))
        for step in range(MICRO):
            side = sides[step]
            if step == 0:
                down_other, side = lax.optimization_barrier((down_other, side))
            else:
                down_owned, side = lax.optimization_barrier((down_owned, side))
            grad_in, sums = rope_back(raw, turn, gain_heads, *side, step, q_cols, k_cols)
            grads_in.append(grad_in)
            head_sums.append(sums)
        layer_out = (middle + (down_mine.astype(F32) + down_other.astype(F32))).astype(BF16)
        backs = [mp_part(rdot(grad_in, w_qkv)) for grad_in in grads_in]
        grad_qkv_in = jnp.concatenate(grads_in, axis=0)
        grad_qkv_in, gate_owned, up_owned, backs[0], mine = lax.optimization_barrier(
            (grad_qkv_in, gate_owned, up_owned, backs[0], backs[1][0])
        )
        backs[1] = (mine, backs[1][1])
        qkv_owned = scatter(tdot(normed_attn, grad_qkv_in).astype(BF16))
        gain_attn_part = jnp.concatenate([mine for mine, _ in backs], axis=0).astype(F32)
        gain_attn_part = jnp.sum(gain_attn_part * tokens * inv_attn, axis=0)
        head_sum = (head_sums[0] + head_sums[1]).reshape(-1)
        small = jnp.concatenate([gain_attn_part, gain_ffn_part, head_sum]).reshape(-1, HEAD)
        small = butterfly(small, "seq", seq_size)
        small = butterfly(small, "dp", dp_size)
        small = butterfly(small, "mp", mp_size).reshape(-1)
        head_sum = small[2 * width :]
        owner = (lax.axis_index("dp") * seq_size + rank) * own_rows
        wide_sum = small[: 2 * width].reshape(2, width)
        wide_sum = lax.dynamic_slice_in_dim(wide_sum, owner, own_rows, 1)

        grad_normed_attn = jnp.concatenate(
            [mine.astype(F32) + other.astype(F32) for mine, other in backs], axis=0
        )
        grad_tokens = (
            grad_middle + norm_back(grad_normed_attn, tokens, inv_attn, gain_attn)
        ).astype(BF16)

        qkv_owned = qkv_owned.astype(F32)
        return (
            layer_out.reshape(MICRO, 1, rows, width),
            grad_tokens.reshape(MICRO, 1, rows, width),
            qkv_owned[:, :q_cols],
            qkv_owned[:, q_cols : q_cols + k_cols],
            qkv_owned[:, q_cols + k_cols :],
            out_owned.T.astype(F32),
            gate_owned.astype(F32),
            up_owned.astype(F32),
            down_owned.T.astype(F32),
            wide_sum[0],
            wide_sum[1],
            head_sum[:HEAD],
            head_sum[HEAD:],
        )

    return local


def solution(mesh):
    return jax.shard_map(
        make_local(mesh.shape["mp"], mesh.shape["seq"], mesh.shape["dp"]),
        mesh=mesh,
        in_specs=(
            P(None, "dp", "seq", None),
            P(("dp", "seq"), "mp"),
            P(("dp", "seq"), "mp"),
            P(("dp", "seq"), "mp"),
            P("mp", ("dp", "seq")),
            P(("dp", "seq"), "mp"),
            P(("dp", "seq"), "mp"),
            P("mp", ("dp", "seq")),
            P(("dp", "seq")),
            P(("dp", "seq")),
            P(),
            P(),
            P(None, "dp", "seq"),
            P(None, "dp", "seq"),
            P(None, "dp", "seq", None),
        ),
        out_specs=(
            P(None, "dp", "seq", None),
            P(None, "dp", "seq", None),
            P(("dp", "seq"), "mp"),
            P(("dp", "seq"), "mp"),
            P(("dp", "seq"), "mp"),
            P("mp", ("dp", "seq")),
            P(("dp", "seq"), "mp"),
            P(("dp", "seq"), "mp"),
            P("mp", ("dp", "seq")),
            P(("dp", "seq")),
            P(("dp", "seq")),
            P(),
            P(),
        ),
        check_vma=False,
    )
```

```python
import functools

import jax
import jax.numpy as jnp
from jax import lax
from jax.experimental import pallas as pl
from jax.experimental.layout import Layout, with_layout_constraint
from jax.experimental.pallas import tpu as pltpu
from jax.sharding import PartitionSpec as P

HEADS = 16
KV_HEADS = 8
HEAD = 128
MICRO = 2

EPS = 1e-06
ROPE_BASE = 1000000.0
F32 = jnp.float32
BF16 = jnp.bfloat16
SCALE = HEAD ** (-0.5)
EXP2_SCALE = SCALE * 1.4426950408889634


def dot(left, right):
    return jnp.dot(left, right, preferred_element_type=F32)


def tdot(left, right):
    return lax.dot_general(left, right, (((0,), (0,)), ((), ())), preferred_element_type=F32)


def rdot(left, right):
    return lax.dot_general(left, right, (((1,), (1,)), ((), ())), preferred_element_type=F32)


def norm_back(grads, values, inverse, gain):
    scaled = grads * gain
    return inverse * scaled - values * inverse**3 * jnp.mean(
        scaled * values, axis=-1, keepdims=True
    )


def inv_rms(values):
    return lax.rsqrt(jnp.mean(values * values, axis=-1, keepdims=True) + EPS)


def forward_kernel(tile, group, need, q, k0,v0,k1,v1,k2,v2,k3,v3, seg_q, seg_k, out, log_sum, acc, den):
    rows=q.shape[0]
    tiles=[(g,t) for g in range(group) for t in range(rows//tile)]
    def run(flip, k, v):
        for g,t in tiles:
            cut=slice(t*tile,(t+1)*tile)
            n=(t+1)*tile if flip==0 else rows
            s=rdot(q[cut,g*HEAD:(g+1)*HEAD], k[:n,:])
            ok=seg_q[cut,:]==seg_k[flip:flip+1,:n]
            if flip==0:
                ok&=(lax.broadcasted_iota(jnp.int32,(tile,n),0)+t*tile)>=lax.broadcasted_iota(jnp.int32,(tile,n),1)
            e=jnp.where(ok,jnp.exp2(s*EXP2_SCALE),0.0)
            mixed=dot(e.astype(BF16),v[:n,:])
            total=jnp.sum(e,axis=1,keepdims=True)
            at=slice(g*rows+t*tile,g*rows+(t+1)*tile)
            if flip==0:
                acc[at,:]=mixed; den[at,:]=total
            else:
                acc[at,:]+=mixed; den[at,:]+=total
    run(0,k0,v0)
    for flip,(k,v) in ((1,(k1,v1)),(2,(k2,v2)),(3,(k3,v3))):
        pl.when(need[flip]>0)(functools.partial(run,flip,k,v))
    for g in range(group):
        at=slice(g*rows,(g+1)*rows)
        out[:,g*HEAD:(g+1)*HEAD]=(acc[at,:]/den[at,:]).astype(out.dtype)
    log_sum[0] = jnp.transpose(jnp.broadcast_to(jnp.log2(den[...]), (group * rows, HEAD)))[0:1]

def attend(need, queries, step, parts, seg_q, seg_k, k_cols, group, tile=256):
    rows=parts[0].shape[0]; kv=k_cols//HEAD
    kspec=pl.BlockSpec((rows,HEAD),lambda h,n:(0,h))
    vspec=pl.BlockSpec((rows,HEAD),lambda h,n:(0,h+kv))
    return pl.pallas_call(
        functools.partial(forward_kernel,tile,group),
        grid_spec=pltpu.PrefetchScalarGridSpec(
            num_scalar_prefetch=1, grid=(kv,),
            in_specs=[pl.BlockSpec((rows,group*HEAD),lambda h,n:(step,h))]+[kspec,vspec]*4+[
                pl.BlockSpec((rows,1),lambda h,n:(0,0)), pl.BlockSpec((4,rows),lambda h,n:(0,0))],
            out_specs=[pl.BlockSpec((rows,group*HEAD),lambda h,n:(0,h)), pl.BlockSpec((1,1,group*rows),lambda h,n:(h,0,0))],
            scratch_shapes=[pltpu.VMEM((group*rows,HEAD),F32),pltpu.VMEM((group*rows,1),F32)]),
        out_shape=[jax.ShapeDtypeStruct((rows,kv*group*HEAD),BF16),jax.ShapeDtypeStruct((kv,1,group*rows),F32)],
        name="attend",
    )(need,queries,*[p for part in parts for p in (part,part)],seg_q,seg_k)

def backward_kernel(tile, group, need, q, g_out, heads, k0,v0,k1,v1,k2,v2,k3,v3, seg_q, seg_k, log_sum, dq, d0,d1,d2,d3, acc, delta):
    rows=q.shape[0]
    ones=jnp.ones((8,HEAD),F32)
    for g in range(group):
        lanes=slice(g*HEAD,(g+1)*HEAD)
        product=g_out[:,lanes].astype(F32)*heads[:,lanes].astype(F32)
        delta[:,g*rows:(g+1)*rows]=lax.dot_general(ones,product,(((1,),(1,)),((),())),precision=lax.Precision.HIGHEST,preferred_element_type=F32)
    tiles=[(g,t) for g in range(group) for t in range(rows//tile)]
    def run(flip,k,v,d,dk_acc,dv_acc):
        for idx,(g,t) in enumerate(tiles):
            cut=slice(t*tile,(t+1)*tile)
            at=slice(g*rows+t*tile,g*rows+(t+1)*tile)
            n=(t+1)*tile if flip==0 else rows
            qt=q[cut,g*HEAD:(g+1)*HEAD]; dt=g_out[cut,g*HEAD:(g+1)*HEAD]
            kn=k[:n,:]
            s=rdot(kn,qt)
            ok=seg_k[:n,flip:flip+1]==seg_q[:,cut]
            if flip==0:
                ok&=(lax.broadcasted_iota(jnp.int32,(n,tile),1)+t*tile)>=lax.broadcasted_iota(jnp.int32,(n,tile),0)
            p=jnp.where(ok,jnp.exp2(s*EXP2_SCALE-log_sum[0,0:1,at]),0.0)
            dp=rdot(v[:n,:],dt)
            ds=(p*(dp-delta[0:1,at])).astype(BF16)
            dv=dot(p.astype(BF16),dt)
            dk=dot(ds,qt)
            if idx==0:
                dk_acc[...]=jnp.zeros_like(dk_acc); dv_acc[...]=jnp.zeros_like(dv_acc)
            dk_acc[:n,:]+=dk
            dv_acc[:n,:]+=dv
            back=tdot(ds,kn)*SCALE
            o=(cut,slice(g*HEAD,(g+1)*HEAD))
            if flip==0: dq[o]=back
            else: dq[o]+=back
        d[0]=(dk_acc[...]*SCALE).astype(d.dtype)
        d[1]=dv_acc[...].astype(d.dtype)
    run(0,k0,v0,d0,acc.at[0],acc.at[1])
    for flip,(k,v,d) in ((1,(k1,v1,d1)),(2,(k2,v2,d2)),(3,(k3,v3,d3))):
        pl.when(need[flip]>0)(functools.partial(run,flip,k,v,d,acc.at[0],acc.at[1]))
        def clear(d=d): d[...]=jnp.zeros_like(d)
        pl.when(need[flip]<=0)(clear)

def attend_back(need, queries, grad_heads, heads, step, parts, seg_q, seg_k, log_sum, k_cols, group, tile=256):
    rows=parts[0].shape[0]; kv=k_cols//HEAD
    kspec=pl.BlockSpec((rows,HEAD),lambda h,n:(0,h))
    vspec=pl.BlockSpec((rows,HEAD),lambda h,n:(0,h+kv))
    qspec=pl.BlockSpec((rows,group*HEAD),lambda h,n:(step,h))
    dspec=pl.BlockSpec((2,rows,HEAD),lambda h,n:(0,0,h))
    types=(F32,BF16,F32,BF16)
    return pl.pallas_call(
        functools.partial(backward_kernel,tile,group),
        grid_spec=pltpu.PrefetchScalarGridSpec(
            num_scalar_prefetch=1, grid=(kv,),
            in_specs=[qspec,qspec,pl.BlockSpec((rows,group*HEAD),lambda h,n:(0,h))]+[kspec,vspec]*4+[
                pl.BlockSpec((1,rows),lambda h,n:(0,0)), pl.BlockSpec((rows,4),lambda h,n:(0,0)),
                pl.BlockSpec((1,1,group*rows),lambda h,n:(h,0,0))],
            out_specs=[pl.BlockSpec((rows,group*HEAD),lambda h,n:(0,h))]+[dspec]*4,
            scratch_shapes=[pltpu.VMEM((2,rows,HEAD),F32),pltpu.VMEM((8,group*rows),F32)]),
        out_shape=[jax.ShapeDtypeStruct((rows,kv*group*HEAD),F32)]+[jax.ShapeDtypeStruct((2,rows,k_cols),t) for t in types],
        name="attend_back",
    )(need,queries,grad_heads,heads,*[p for part in parts for p in (part,part)],seg_q,seg_k,log_sum)


def rope_kernel(q_heads, k_heads, raw, turn, gains, queries, pairs):
    cosine, sine = turn[0], turn[1]
    for head in range(q_heads + k_heads):
        values = raw[:, head * HEAD : (head + 1) * HEAD]
        inverse = lax.rsqrt(jnp.mean(values * values, axis=-1, keepdims=True) + EPS)
        gain = gains[0:1] if head < q_heads else gains[1:2]
        scaled = values * inverse * gain
        turned = (scaled * cosine + pltpu.roll(scaled, HEAD // 2, 1) * sine).astype(BF16)
        if head < q_heads:
            queries[:, head * HEAD : (head + 1) * HEAD] = turned
        else:
            at = head - q_heads
            pairs[:, at * HEAD : (at + 1) * HEAD] = turned
    cols = (q_heads + k_heads) * HEAD
    pairs[:, k_heads * HEAD :] = raw[:, cols:].astype(BF16)


def rope(raw, turn, gains, q_cols, k_cols, block=256):
    total = raw.shape[0]
    return pl.pallas_call(
        functools.partial(rope_kernel, q_cols // HEAD, k_cols // HEAD),
        grid=(total // block,),
        in_specs=[
            pl.BlockSpec((block, raw.shape[1]), lambda i: (i, 0)),
            pl.BlockSpec((2, block, HEAD), lambda i: (0, i, 0)),
            pl.BlockSpec((2, HEAD), lambda i: (0, 0)),
        ],
        out_specs=[
            pl.BlockSpec((block, q_cols), lambda i: (i, 0)),
            pl.BlockSpec((block, 2 * k_cols), lambda i: (i, 0)),
        ],
        out_shape=[
            jax.ShapeDtypeStruct((total, q_cols), BF16),
            jax.ShapeDtypeStruct((total, 2 * k_cols), BF16),
        ],
        name="rope",
    )(raw, turn, gains)


def rope_back_kernel(q_heads, k_heads, raw, turn, gains, dq, d_own, d_near, d_far, out, sums):
    cosine, sine = turn[0], turn[1]

    @pl.when(pl.program_id(0) == 0)
    def _():
        sums[...] = jnp.zeros_like(sums)

    for head in range(q_heads + k_heads):
        lanes = slice(head * HEAD, (head + 1) * HEAD)
        which = 0 if head < q_heads else 1
        if which == 0:
            grads = dq[:, lanes]
        else:
            at = slice((head - q_heads) * HEAD, (head - q_heads + 1) * HEAD)
            grads = d_own[0, :, at] + d_near[0, :, at].astype(F32) + d_far[0, :, at].astype(F32)
        values = raw[:, lanes]
        inverse = lax.rsqrt(jnp.mean(values * values, axis=-1, keepdims=True) + EPS)
        unit = values * inverse
        turned = grads * cosine - pltpu.roll(grads, HEAD // 2, 1) * sine
        sums[which : which + 1] += jnp.sum(turned * unit, axis=0, keepdims=True)
        scaled = turned * gains[which : which + 1]
        mean = jnp.mean(scaled * unit, axis=-1, keepdims=True)
        out[:, lanes] = (inverse * (scaled - unit * mean)).astype(BF16)
    cols = (q_heads + k_heads) * HEAD
    out[:, cols:] = (d_own[1] + d_near[1].astype(F32) + d_far[1].astype(F32)).astype(BF16)


def rope_back(raw, turn, gains, dq, d_own, d_near, d_far, step, q_cols, k_cols, block=256):
    rows = dq.shape[0]
    base = step * (rows // block)
    cols = q_cols + 2 * k_cols
    dspec = pl.BlockSpec((2, block, k_cols), lambda i: (0, i, 0))
    return pl.pallas_call(
        functools.partial(rope_back_kernel, q_cols // HEAD, k_cols // HEAD),
        grid=(rows // block,),
        in_specs=[
            pl.BlockSpec((block, cols), lambda i: (base + i, 0)),
            pl.BlockSpec((2, block, HEAD), lambda i: (0, base + i, 0)),
            pl.BlockSpec((2, HEAD), lambda i: (0, 0)),
            pl.BlockSpec((block, q_cols), lambda i: (i, 0)),
            dspec,
            dspec,
            dspec,
        ],
        out_specs=[
            pl.BlockSpec((block, cols), lambda i: (i, 0)),
            pl.BlockSpec((2, HEAD), lambda i: (0, 0)),
        ],
        out_shape=[
            jax.ShapeDtypeStruct((rows, cols), BF16),
            jax.ShapeDtypeStruct((2, HEAD), F32),
        ],
        name="rope_back",
    )(raw, turn, gains, dq, d_own, d_near, d_far)


def move_kernel(rank, source, out):
    out[...] = source[...]


def relative(values, rank, dp_size, seq_size):
    total, width = values.shape
    lanes = width // (dp_size * seq_size)

    def pick(step, rank):
        turn = step // dp_size
        flip = (turn % 2) * 2 + turn // 2
        return (0, (step % dp_size) * seq_size + jnp.bitwise_xor(rank[0], flip))

    return pl.pallas_call(
        move_kernel,
        grid_spec=pltpu.PrefetchScalarGridSpec(
            num_scalar_prefetch=1,
            grid=(dp_size * seq_size,),
            in_specs=[pl.BlockSpec((total, lanes), pick)],
            out_specs=pl.BlockSpec((total, lanes), lambda step, rank: (0, step)),
        ),
        out_shape=jax.ShapeDtypeStruct(values.shape, values.dtype),
        name="relative",
    )(rank.reshape(1).astype(jnp.int32), values)


def make_local(mp_size, seq_size, dp_size):
    data_axes = ("dp", "seq")
    pair = [(i, i ^ 1) for i in range(seq_size)]
    up_pairs = [(i, i + 2) for i in range(seq_size - 2)]
    down_pairs = [(i + 2, i) for i in range(seq_size - 2)]
    cross = [(i, i ^ 2) for i in range(seq_size)]

    def scatter(grad):
        return lax.psum_scatter(grad, data_axes, scatter_dimension=0, tiled=True)

    def mp_other(part):
        if mp_size == 2:
            return lax.ppermute(part, "mp", [(0, 1), (1, 0)])
        return (lax.psum(part.astype(F32), "mp") - part.astype(F32)).astype(BF16)

    def mp_part(part):
        part = lax.optimization_barrier(part.astype(BF16))
        return part, mp_other(part)

    def pair_stage(left, right):
        half = left.shape[1] // 2
        theirs = tdot(left[:, half:], right).astype(BF16)
        got = lax.ppermute(theirs, "seq", pair)
        return (tdot(left[:, :half], right) + got.astype(F32)).astype(BF16)

    def cross_stage(block):
        half = block.shape[0] // 2
        got = lax.ppermute(block[half:], "seq", cross)
        return (block[:half].astype(F32) + got.astype(F32)).astype(BF16)

    def line_stage(block):
        place = lax.axis_index("dp")
        blocks = block.reshape(dp_size, -1, block.shape[1])
        pieces = [lax.dynamic_index_in_dim(blocks, place, 0, False)]
        for flip in range(1, dp_size):
            sent = lax.dynamic_index_in_dim(blocks, jnp.bitwise_xor(place, flip), 0, False)
            pieces.append(lax.ppermute(sent, "dp", [(i, i ^ flip) for i in range(dp_size)]))
        return pieces

    def butterfly(value, axis, size):
        flip = 1
        while flip < size:
            moves = [(i, i ^ flip) for i in range(size)]
            value = value + lax.ppermute(value, axis, moves)
            flip *= 2
        return value

    def mp_sum(part):
        mine, other = mp_part(part)
        return mine.astype(F32) + other.astype(F32)

    def local(
        hidden,
        w_query,
        w_key,
        w_value,
        w_out,
        w_gate,
        w_up,
        w_down,
        norm_attn,
        norm_ffn,
        norm_query,
        norm_key,
        segments,
        positions,
        cotangent,
    ):
        rows = hidden.shape[2]
        width = hidden.shape[3]
        total = MICRO * rows
        q_cols = w_query.shape[1]
        k_cols = w_key.shape[1]
        group = HEADS // KV_HEADS
        rank = lax.axis_index("seq")
        own_rows = w_query.shape[0]

        gains = jnp.concatenate(
            [
                jnp.broadcast_to(norm_attn[:, None], (own_rows, 64)),
                jnp.broadcast_to(norm_ffn[:, None], (own_rows, 64)),
            ],
            axis=1,
        )
        first = jnp.concatenate([w_query, w_key, w_value, w_out.T, gains], axis=1)
        first = lax.all_gather(first, data_axes, axis=0, tiled=True)
        second = jnp.stack([w_gate, w_up, w_down.T])
        second, first = lax.optimization_barrier((second, first))
        second = lax.all_gather(second, data_axes, axis=1, tiled=True)
        tokens = hidden.reshape(total, width).astype(F32)
        inv_attn = inv_rms(tokens)
        frequency = ROPE_BASE ** (-(jnp.arange(HEAD // 2, dtype=F32) * 2.0) / HEAD)
        angles = positions.reshape(total).astype(F32)[:, None] * frequency[None, :]
        cosine = jnp.cos(angles)
        sine = jnp.sin(angles)
        turn = jnp.stack(
            [
                jnp.concatenate([cosine, cosine], axis=-1),
                jnp.concatenate([-sine, sine], axis=-1),
            ]
        )
        seg_own = segments[:, 0]
        seg_pair = lax.ppermute(seg_own, "seq", pair)
        both = jnp.stack([seg_own, seg_pair])
        both_x = lax.ppermute(both, "seq", up_pairs)
        seg_keys = jnp.stack([both[0], both[1], both_x[0], both_x[1]])
        flips = jnp.arange(4, dtype=jnp.int32)
        near_enough = (seg_keys[:, :, -1] == seg_own[None, :, 0]) | (flips[:, None] == 0)
        need = (near_enough & (jnp.bitwise_xor(rank, flips)[:, None] <= rank)).astype(jnp.int32)
        first, turn, inv_attn, seg_keys, need = lax.optimization_barrier(
            (first, turn, inv_attn, seg_keys, need)
        )
        qkv_cols = q_cols + 2 * k_cols
        w_qkv = first[:, :qkv_cols]
        w_out_t = first[:, qkv_cols : qkv_cols + q_cols]
        gain_attn = first[:, qkv_cols + q_cols].astype(F32)
        gain_ffn = first[:, qkv_cols + q_cols + 64].astype(F32)
        gate_full, up_full, down_t = second[0], second[1], second[2]
        gain_heads = jnp.stack([norm_query, norm_key]).astype(F32)

        cot = lax.optimization_barrier(cotangent.reshape(total, width))

        normed_attn = (tokens * inv_attn * gain_attn).astype(BF16)
        raw = dot(normed_attn, w_qkv)
        queries, pairs = rope(raw, turn, gain_heads, q_cols, k_cols)

        cuts = [slice(step * rows, (step + 1) * rows) for step in range(MICRO)]
        kept = []
        middles = []
        heads_out = []
        for step in range(MICRO):
            cut = slice(step * rows, (step + 1) * rows)
            own = pairs[cut]
            near = lax.ppermute(own, "seq", pair)
            far = lax.ppermute(own, "seq", up_pairs)
            far_near = lax.ppermute(far, "seq", pair)
            parts = (own, near, far, far_near)
            attn_heads, log_sum = attend(
                need[:, step],
                queries,
                step,
                parts,
                seg_own[step][:, None],
                seg_keys[:, step],
                k_cols,
                group,
                rows,
            )
            heads_out.append(attn_heads)
            kept.append((parts, log_sum))
            attn_part = rdot(attn_heads, w_out_t)
            middles.append(tokens[cut] + mp_sum(attn_part))
        middle = jnp.concatenate(middles, axis=0)
        attn_heads = jnp.concatenate(heads_out, axis=0)

        inv_ffn = inv_rms(middle)
        normed_ffn = (middle * inv_ffn * gain_ffn).astype(BF16)
        gate = dot(normed_ffn, gate_full)
        upward = dot(normed_ffn, up_full)
        sigma = jax.nn.sigmoid(gate)
        silu = gate * sigma
        act = (silu * upward).astype(BF16)
        down_grad = tdot(cot, act).astype(BF16)
        down_grad = with_layout_constraint(down_grad, Layout((0, 1)))
        down_owned = scatter(down_grad)
        cot_late, act, down_grad = lax.optimization_barrier((cot, act, down_grad))
        grad_act = dot(cot_late, down_t)
        grad_gate_in = (grad_act * upward * sigma * (1.0 + gate * (1.0 - sigma))).astype(BF16)
        grad_up_in = (grad_act * silu).astype(BF16)
        backs = []
        for step in range(MICRO):
            cut = slice(step * rows, (step + 1) * rows)
            backs.append(
                mp_part(rdot(grad_gate_in[cut], gate_full) + rdot(grad_up_in[cut], up_full))
            )
        late, mine = lax.optimization_barrier((normed_ffn, backs[0][0]))
        backs[0] = (mine, backs[0][1])
        ffn_rel = relative(late, rank, dp_size, seq_size)
        up_block = pair_stage(ffn_rel, grad_up_in)
        gate_grad = tdot(normed_ffn, grad_gate_in).astype(BF16)
        gate_owned = scatter(gate_grad)
        down_mine = lax.optimization_barrier(rdot(act, down_t).astype(BF16))
        backs, gate_grad, up_block, down_mine = lax.optimization_barrier(
            (backs, gate_grad, up_block, down_mine)
        )
        down_other = mp_other(down_mine)
        gain_ffn_part = jnp.concatenate([mine for mine, _ in backs], axis=0).astype(F32)
        gain_ffn_part = jnp.sum(gain_ffn_part * middle * inv_ffn, axis=0)
        backs = [mine.astype(F32) + other.astype(F32) for mine, other in backs]
        grad_normed_ffn = jnp.concatenate(backs, axis=0)
        grad_middle = cot.astype(F32) + norm_back(grad_normed_ffn, middle, inv_ffn, gain_ffn)
        grad_middle_b = grad_middle.astype(BF16)
        grad_heads = dot(grad_middle_b, w_out_t).astype(BF16)
        out_owned = scatter(tdot(grad_middle_b, attn_heads).astype(BF16))
        up_block = cross_stage(up_block)

        grads_in = []
        head_sums = []
        sides = []
        for step in range(MICRO):
            parts, log_sum = kept[step]
            grad_q, d_own, d_near, d_far, d_far_near = attend_back(
                need[:, step],
                queries,
                grad_heads,
                heads_out[step],
                step,
                parts,
                seg_own[step][None],
                seg_keys[:, step].T,
                log_sum,
                k_cols,
                group,
                rows,
            )
            got = lax.ppermute(d_near, "seq", pair)
            got_far = lax.ppermute(d_far_near, "seq", pair)
            far = lax.ppermute(
                (d_far + got_far.astype(F32)).astype(BF16), "seq", down_pairs
            )
            if step == 0:
                up_block, d_own = lax.optimization_barrier((up_block, d_own))
                up_pieces = line_stage(up_block)
            sides.append((grad_q, d_own, got, far))
        for step in range(MICRO):
            side = sides[step]
            if step == 0:
                down_other, side = lax.optimization_barrier((down_other, side))
            else:
                down_owned, side = lax.optimization_barrier((down_owned, side))
            grad_in, sums = rope_back(raw, turn, gain_heads, *side, step, q_cols, k_cols)
            grads_in.append(grad_in)
            head_sums.append(sums)
        layer_out = (middle + (down_mine.astype(F32) + down_other.astype(F32))).astype(BF16)
        backs = [mp_part(rdot(grad_in, w_qkv)) for grad_in in grads_in]
        grad_qkv_in = jnp.concatenate(grads_in, axis=0)
        unit = [(tokens[cut] * inv_attn[cut]) for cut in cuts]
        gain_attn_part = sum(
            jnp.sum(back[0].astype(F32) * part, axis=0) for back, part in zip(backs, unit)
        )
        grad_qkv_in, gate_owned, layer_out, gain_attn_part, backs[0], mine = (
            lax.optimization_barrier(
                (grad_qkv_in, gate_owned, layer_out, gain_attn_part, backs[0], backs[1][0])
            )
        )
        backs[1] = (mine, backs[1][1])
        qkv_owned = scatter(tdot(normed_attn, grad_qkv_in).astype(BF16))
        head_sum = (head_sums[0] + head_sums[1]).reshape(-1)
        small = jnp.concatenate([gain_attn_part, gain_ffn_part, head_sum]).reshape(-1, HEAD)
        small = butterfly(small, "seq", seq_size)
        small = butterfly(small, "dp", dp_size)
        small = butterfly(small, "mp", mp_size)

        def finish(back, cut):
            grads = back[0].astype(F32) + back[1].astype(F32)
            return (
                grad_middle[cut] + norm_back(grads, tokens[cut], inv_attn[cut], gain_attn)
            ).astype(BF16)

        early = finish(backs[0], cuts[0])
        early, small, up_pieces, out_owned, backs[1] = lax.optimization_barrier(
            (early, small, up_pieces, out_owned, backs[1])
        )
        up_owned = sum(piece.astype(F32) for piece in up_pieces)
        grad_tokens = jnp.stack([early, finish(backs[1], cuts[1])])
        small = small.reshape(-1)
        head_sum = small[2 * width :]
        owner = (lax.axis_index("dp") * seq_size + rank) * own_rows
        wide_sum = small[: 2 * width].reshape(2, width)
        wide_sum = lax.dynamic_slice_in_dim(wide_sum, owner, own_rows, 1)

        qkv_owned = qkv_owned.astype(F32)
        return (
            layer_out.reshape(MICRO, 1, rows, width),
            grad_tokens.reshape(MICRO, 1, rows, width),
            qkv_owned[:, :q_cols],
            qkv_owned[:, q_cols : q_cols + k_cols],
            qkv_owned[:, q_cols + k_cols :],
            out_owned.T.astype(F32),
            gate_owned.astype(F32),
            up_owned.astype(F32),
            down_owned.T.astype(F32),
            wide_sum[0],
            wide_sum[1],
            head_sum[:HEAD],
            head_sum[HEAD:],
        )

    return local


def solution(mesh):
    return jax.shard_map(
        make_local(mesh.shape["mp"], mesh.shape["seq"], mesh.shape["dp"]),
        mesh=mesh,
        in_specs=(
            P(None, "dp", "seq", None),
            P(("dp", "seq"), "mp"),
            P(("dp", "seq"), "mp"),
            P(("dp", "seq"), "mp"),
            P("mp", ("dp", "seq")),
            P(("dp", "seq"), "mp"),
            P(("dp", "seq"), "mp"),
            P("mp", ("dp", "seq")),
            P(("dp", "seq")),
            P(("dp", "seq")),
            P(),
            P(),
            P(None, "dp", "seq"),
            P(None, "dp", "seq"),
            P(None, "dp", "seq", None),
        ),
        out_specs=(
            P(None, "dp", "seq", None),
            P(None, "dp", "seq", None),
            P(("dp", "seq"), "mp"),
            P(("dp", "seq"), "mp"),
            P(("dp", "seq"), "mp"),
            P("mp", ("dp", "seq")),
            P(("dp", "seq"), "mp"),
            P(("dp", "seq"), "mp"),
            P("mp", ("dp", "seq")),
            P(("dp", "seq")),
            P(("dp", "seq")),
            P(),
            P(),
        ),
        check_vma=False,
    )
```

```python
import functools

import jax
import jax.numpy as jnp
from jax import lax
from jax.experimental import pallas as pl
from jax.experimental.layout import Layout, with_layout_constraint
from jax.experimental.pallas import tpu as pltpu
from jax.sharding import PartitionSpec as P

HEADS = 16
KV_HEADS = 8
HEAD = 128
MICRO = 2

EPS = 1e-06
ROPE_BASE = 1000000.0
F32 = jnp.float32
BF16 = jnp.bfloat16
SCALE = HEAD ** (-0.5)
EXP2_SCALE = SCALE * 1.4426950408889634


def dot(left, right):
    return jnp.dot(left, right, preferred_element_type=F32)


def tdot(left, right):
    return lax.dot_general(left, right, (((0,), (0,)), ((), ())), preferred_element_type=F32)


def rdot(left, right):
    return lax.dot_general(left, right, (((1,), (1,)), ((), ())), preferred_element_type=F32)


def norm_back(grads, values, inverse, gain):
    scaled = grads * gain
    return inverse * scaled - values * inverse**3 * jnp.mean(
        scaled * values, axis=-1, keepdims=True
    )


def inv_rms(values):
    return lax.rsqrt(jnp.mean(values * values, axis=-1, keepdims=True) + EPS)


def forward_kernel(tile, group, need, q, k0,v0,k1,v1,k2,v2,k3,v3, seg_q, seg_k, out, log_sum, acc, den):
    rows=q.shape[0]
    tiles=[(g,t) for g in range(group) for t in range(rows//tile)]
    def run(flip, k, v):
        for g,t in tiles:
            cut=slice(t*tile,(t+1)*tile)
            n=(t+1)*tile if flip==0 else rows
            s=rdot(q[cut,g*HEAD:(g+1)*HEAD], k[:n,:])
            ok=seg_q[cut,:]==seg_k[flip:flip+1,:n]
            if flip==0:
                ok&=(lax.broadcasted_iota(jnp.int32,(tile,n),0)+t*tile)>=lax.broadcasted_iota(jnp.int32,(tile,n),1)
            e=jnp.where(ok,jnp.exp2(s*EXP2_SCALE),0.0)
            mixed=dot(e.astype(BF16),v[:n,:])
            total=jnp.sum(e,axis=1,keepdims=True)
            at=slice(g*rows+t*tile,g*rows+(t+1)*tile)
            if flip==0:
                acc[at,:]=mixed; den[at,:]=total
            else:
                acc[at,:]+=mixed; den[at,:]+=total
    run(0,k0,v0)
    for flip,(k,v) in ((1,(k1,v1)),(2,(k2,v2)),(3,(k3,v3))):
        pl.when(need[flip]>0)(functools.partial(run,flip,k,v))
    for g in range(group):
        at=slice(g*rows,(g+1)*rows)
        out[:,g*HEAD:(g+1)*HEAD]=(acc[at,:]/den[at,:]).astype(out.dtype)
    log_sum[0] = jnp.transpose(jnp.broadcast_to(jnp.log2(den[...]), (group * rows, HEAD)))[0:1]

def attend(need, queries, step, parts, seg_q, seg_k, k_cols, group, tile=256):
    rows=parts[0].shape[0]; kv=k_cols//HEAD
    kspec=pl.BlockSpec((rows,HEAD),lambda h,n:(0,h))
    vspec=pl.BlockSpec((rows,HEAD),lambda h,n:(0,h+kv))
    return pl.pallas_call(
        functools.partial(forward_kernel,tile,group),
        grid_spec=pltpu.PrefetchScalarGridSpec(
            num_scalar_prefetch=1, grid=(kv,),
            in_specs=[pl.BlockSpec((rows,group*HEAD),lambda h,n:(step,h))]+[kspec,vspec]*4+[
                pl.BlockSpec((rows,1),lambda h,n:(0,0)), pl.BlockSpec((4,rows),lambda h,n:(0,0))],
            out_specs=[pl.BlockSpec((rows,group*HEAD),lambda h,n:(0,h)), pl.BlockSpec((1,1,group*rows),lambda h,n:(h,0,0))],
            scratch_shapes=[pltpu.VMEM((group*rows,HEAD),F32),pltpu.VMEM((group*rows,1),F32)]),
        out_shape=[jax.ShapeDtypeStruct((rows,kv*group*HEAD),BF16),jax.ShapeDtypeStruct((kv,1,group*rows),F32)],
        name="attend",
    )(need,queries,*[p for part in parts for p in (part,part)],seg_q,seg_k)

def backward_kernel(tile, group, need, q, g_out, heads, k0,v0,k1,v1,k2,v2,k3,v3, seg_q, seg_k, log_sum, dq, d0,d1,d2,d3, acc, delta):
    rows=q.shape[0]
    ones=jnp.ones((8,HEAD),F32)
    for g in range(group):
        lanes=slice(g*HEAD,(g+1)*HEAD)
        product=g_out[:,lanes].astype(F32)*heads[:,lanes].astype(F32)
        delta[:,g*rows:(g+1)*rows]=lax.dot_general(ones,product,(((1,),(1,)),((),())),precision=lax.Precision.HIGHEST,preferred_element_type=F32)
    tiles=[(g,t) for g in range(group) for t in range(rows//tile)]
    def run(flip,k,v,d,dk_acc,dv_acc):
        for idx,(g,t) in enumerate(tiles):
            cut=slice(t*tile,(t+1)*tile)
            at=slice(g*rows+t*tile,g*rows+(t+1)*tile)
            n=(t+1)*tile if flip==0 else rows
            qt=q[cut,g*HEAD:(g+1)*HEAD]; dt=g_out[cut,g*HEAD:(g+1)*HEAD]
            kn=k[:n,:]
            s=rdot(kn,qt)
            ok=seg_k[:n,flip:flip+1]==seg_q[:,cut]
            if flip==0:
                ok&=(lax.broadcasted_iota(jnp.int32,(n,tile),1)+t*tile)>=lax.broadcasted_iota(jnp.int32,(n,tile),0)
            p=jnp.where(ok,jnp.exp2(s*EXP2_SCALE-log_sum[0,0:1,at]),0.0)
            dp=rdot(v[:n,:],dt)
            ds=(p*(dp-delta[0:1,at])).astype(BF16)
            dv=dot(p.astype(BF16),dt)
            dk=dot(ds,qt)
            if idx==0:
                dk_acc[...]=jnp.zeros_like(dk_acc); dv_acc[...]=jnp.zeros_like(dv_acc)
            dk_acc[:n,:]+=dk
            dv_acc[:n,:]+=dv
            back=tdot(ds,kn)*SCALE
            o=(cut,slice(g*HEAD,(g+1)*HEAD))
            if flip==0: dq[o]=back
            else: dq[o]+=back
        d[0]=(dk_acc[...]*SCALE).astype(d.dtype)
        d[1]=dv_acc[...].astype(d.dtype)
    run(0,k0,v0,d0,acc.at[0],acc.at[1])
    for flip,(k,v,d) in ((1,(k1,v1,d1)),(2,(k2,v2,d2)),(3,(k3,v3,d3))):
        pl.when(need[flip]>0)(functools.partial(run,flip,k,v,d,acc.at[0],acc.at[1]))
        def clear(d=d): d[...]=jnp.zeros_like(d)
        pl.when(need[flip]<=0)(clear)

def attend_back(need, queries, grad_heads, heads, step, parts, seg_q, seg_k, log_sum, k_cols, group, tile=256):
    rows=parts[0].shape[0]; kv=k_cols//HEAD
    kspec=pl.BlockSpec((rows,HEAD),lambda h,n:(0,h))
    vspec=pl.BlockSpec((rows,HEAD),lambda h,n:(0,h+kv))
    qspec=pl.BlockSpec((rows,group*HEAD),lambda h,n:(step,h))
    dspec=pl.BlockSpec((2,rows,HEAD),lambda h,n:(0,0,h))
    types=(F32,BF16,F32,BF16)
    return pl.pallas_call(
        functools.partial(backward_kernel,tile,group),
        grid_spec=pltpu.PrefetchScalarGridSpec(
            num_scalar_prefetch=1, grid=(kv,),
            in_specs=[qspec,qspec,pl.BlockSpec((rows,group*HEAD),lambda h,n:(0,h))]+[kspec,vspec]*4+[
                pl.BlockSpec((1,rows),lambda h,n:(0,0)), pl.BlockSpec((rows,4),lambda h,n:(0,0)),
                pl.BlockSpec((1,1,group*rows),lambda h,n:(h,0,0))],
            out_specs=[pl.BlockSpec((rows,group*HEAD),lambda h,n:(0,h))]+[dspec]*4,
            scratch_shapes=[pltpu.VMEM((2,rows,HEAD),F32),pltpu.VMEM((8,group*rows),F32)]),
        out_shape=[jax.ShapeDtypeStruct((rows,kv*group*HEAD),F32)]+[jax.ShapeDtypeStruct((2,rows,k_cols),t) for t in types],
        name="attend_back",
    )(need,queries,grad_heads,heads,*[p for part in parts for p in (part,part)],seg_q,seg_k,log_sum)


def rope_kernel(q_heads, k_heads, raw, turn, gains, queries, pairs):
    cosine, sine = turn[0], turn[1]
    for head in range(q_heads + k_heads):
        values = raw[:, head * HEAD : (head + 1) * HEAD]
        inverse = lax.rsqrt(jnp.mean(values * values, axis=-1, keepdims=True) + EPS)
        gain = gains[0:1] if head < q_heads else gains[1:2]
        scaled = values * inverse * gain
        turned = (scaled * cosine + pltpu.roll(scaled, HEAD // 2, 1) * sine).astype(BF16)
        if head < q_heads:
            queries[:, head * HEAD : (head + 1) * HEAD] = turned
        else:
            at = head - q_heads
            pairs[:, at * HEAD : (at + 1) * HEAD] = turned
    cols = (q_heads + k_heads) * HEAD
    pairs[:, k_heads * HEAD :] = raw[:, cols:].astype(BF16)


def rope(raw, turn, gains, q_cols, k_cols, block=256):
    total = raw.shape[0]
    return pl.pallas_call(
        functools.partial(rope_kernel, q_cols // HEAD, k_cols // HEAD),
        grid=(total // block,),
        in_specs=[
            pl.BlockSpec((block, raw.shape[1]), lambda i: (i, 0)),
            pl.BlockSpec((2, block, HEAD), lambda i: (0, i, 0)),
            pl.BlockSpec((2, HEAD), lambda i: (0, 0)),
        ],
        out_specs=[
            pl.BlockSpec((block, q_cols), lambda i: (i, 0)),
            pl.BlockSpec((block, 2 * k_cols), lambda i: (i, 0)),
        ],
        out_shape=[
            jax.ShapeDtypeStruct((total, q_cols), BF16),
            jax.ShapeDtypeStruct((total, 2 * k_cols), BF16),
        ],
        name="rope",
    )(raw, turn, gains)


def rope_back_kernel(q_heads, k_heads, raw, turn, gains, dq, d_own, d_near, d_far, out, sums):
    cosine, sine = turn[0], turn[1]

    @pl.when(pl.program_id(0) == 0)
    def _():
        sums[...] = jnp.zeros_like(sums)

    for head in range(q_heads + k_heads):
        lanes = slice(head * HEAD, (head + 1) * HEAD)
        which = 0 if head < q_heads else 1
        if which == 0:
            grads = dq[:, lanes]
        else:
            at = slice((head - q_heads) * HEAD, (head - q_heads + 1) * HEAD)
            grads = d_own[0, :, at] + d_near[0, :, at].astype(F32) + d_far[0, :, at].astype(F32)
        values = raw[:, lanes]
        inverse = lax.rsqrt(jnp.mean(values * values, axis=-1, keepdims=True) + EPS)
        unit = values * inverse
        turned = grads * cosine - pltpu.roll(grads, HEAD // 2, 1) * sine
        sums[which : which + 1] += jnp.sum(turned * unit, axis=0, keepdims=True)
        scaled = turned * gains[which : which + 1]
        mean = jnp.mean(scaled * unit, axis=-1, keepdims=True)
        out[:, lanes] = (inverse * (scaled - unit * mean)).astype(BF16)
    cols = (q_heads + k_heads) * HEAD
    out[:, cols:] = (d_own[1] + d_near[1].astype(F32) + d_far[1].astype(F32)).astype(BF16)


def rope_back(raw, turn, gains, dq, d_own, d_near, d_far, step, q_cols, k_cols, block=256):
    rows = dq.shape[0]
    base = step * (rows // block)
    cols = q_cols + 2 * k_cols
    dspec = pl.BlockSpec((2, block, k_cols), lambda i: (0, i, 0))
    return pl.pallas_call(
        functools.partial(rope_back_kernel, q_cols // HEAD, k_cols // HEAD),
        grid=(rows // block,),
        in_specs=[
            pl.BlockSpec((block, cols), lambda i: (base + i, 0)),
            pl.BlockSpec((2, block, HEAD), lambda i: (0, base + i, 0)),
            pl.BlockSpec((2, HEAD), lambda i: (0, 0)),
            pl.BlockSpec((block, q_cols), lambda i: (i, 0)),
            dspec,
            dspec,
            dspec,
        ],
        out_specs=[
            pl.BlockSpec((block, cols), lambda i: (i, 0)),
            pl.BlockSpec((2, HEAD), lambda i: (0, 0)),
        ],
        out_shape=[
            jax.ShapeDtypeStruct((rows, cols), BF16),
            jax.ShapeDtypeStruct((2, HEAD), F32),
        ],
        name="rope_back",
    )(raw, turn, gains, dq, d_own, d_near, d_far)


def move_kernel(rank, source, out):
    out[...] = source[...]


def relative(values, rank, dp_size, seq_size):
    total, width = values.shape
    lanes = width // (dp_size * seq_size)

    def pick(step, rank):
        turn = step // dp_size
        flip = (turn % 2) * 2 + turn // 2
        return (0, (step % dp_size) * seq_size + jnp.bitwise_xor(rank[0], flip))

    return pl.pallas_call(
        move_kernel,
        grid_spec=pltpu.PrefetchScalarGridSpec(
            num_scalar_prefetch=1,
            grid=(dp_size * seq_size,),
            in_specs=[pl.BlockSpec((total, lanes), pick)],
            out_specs=pl.BlockSpec((total, lanes), lambda step, rank: (0, step)),
        ),
        out_shape=jax.ShapeDtypeStruct(values.shape, values.dtype),
        name="relative",
    )(rank.reshape(1).astype(jnp.int32), values)


def make_local(mp_size, seq_size, dp_size):
    data_axes = ("dp", "seq")
    pair = [(i, i ^ 1) for i in range(seq_size)]
    up_pairs = [(i, i + 2) for i in range(seq_size - 2)]
    down_pairs = [(i + 2, i) for i in range(seq_size - 2)]
    cross = [(i, i ^ 2) for i in range(seq_size)]

    def scatter(grad):
        return lax.psum_scatter(grad, data_axes, scatter_dimension=0, tiled=True)

    def mp_other(part):
        if mp_size == 2:
            return lax.ppermute(part, "mp", [(0, 1), (1, 0)])
        return (lax.psum(part.astype(F32), "mp") - part.astype(F32)).astype(BF16)

    def mp_part(part):
        part = lax.optimization_barrier(part.astype(BF16))
        return part, mp_other(part)

    def pair_stage(left, right):
        half = left.shape[1] // 2
        theirs = tdot(left[:, half:], right).astype(BF16)
        got = lax.ppermute(theirs, "seq", pair)
        return (tdot(left[:, :half], right) + got.astype(F32)).astype(BF16)

    def cross_stage(block):
        half = block.shape[0] // 2
        got = lax.ppermute(block[half:], "seq", cross)
        return (block[:half].astype(F32) + got.astype(F32)).astype(BF16)

    def line_stage(block):
        place = lax.axis_index("dp")
        blocks = block.reshape(dp_size, -1, block.shape[1])
        pieces = [lax.dynamic_index_in_dim(blocks, place, 0, False)]
        for flip in range(1, dp_size):
            sent = lax.dynamic_index_in_dim(blocks, jnp.bitwise_xor(place, flip), 0, False)
            pieces.append(lax.ppermute(sent, "dp", [(i, i ^ flip) for i in range(dp_size)]))
        return pieces

    def butterfly(value, axis, size):
        flip = 1
        while flip < size:
            moves = [(i, i ^ flip) for i in range(size)]
            value = value + lax.ppermute(value, axis, moves)
            flip *= 2
        return value

    def mp_sum(part):
        mine, other = mp_part(part)
        return mine.astype(F32) + other.astype(F32)

    def local(
        hidden,
        w_query,
        w_key,
        w_value,
        w_out,
        w_gate,
        w_up,
        w_down,
        norm_attn,
        norm_ffn,
        norm_query,
        norm_key,
        segments,
        positions,
        cotangent,
    ):
        rows = hidden.shape[2]
        width = hidden.shape[3]
        total = MICRO * rows
        q_cols = w_query.shape[1]
        k_cols = w_key.shape[1]
        group = HEADS // KV_HEADS
        rank = lax.axis_index("seq")
        own_rows = w_query.shape[0]

        gains = jnp.concatenate(
            [
                jnp.broadcast_to(norm_attn[:, None], (own_rows, 64)),
                jnp.broadcast_to(norm_ffn[:, None], (own_rows, 64)),
            ],
            axis=1,
        )
        first = jnp.concatenate([w_query, w_key, w_value, w_out.T, gains], axis=1)
        first = lax.all_gather(first, data_axes, axis=0, tiled=True)
        second = jnp.stack([w_gate, w_up, w_down.T])
        second, first = lax.optimization_barrier((second, first))
        second = lax.all_gather(second, data_axes, axis=1, tiled=True)
        tokens = hidden.reshape(total, width).astype(F32)
        inv_attn = inv_rms(tokens)
        frequency = ROPE_BASE ** (-(jnp.arange(HEAD // 2, dtype=F32) * 2.0) / HEAD)
        angles = positions.reshape(total).astype(F32)[:, None] * frequency[None, :]
        cosine = jnp.cos(angles)
        sine = jnp.sin(angles)
        turn = jnp.stack(
            [
                jnp.concatenate([cosine, cosine], axis=-1),
                jnp.concatenate([-sine, sine], axis=-1),
            ]
        )
        seg_own = segments[:, 0]
        seg_pair = lax.ppermute(seg_own, "seq", pair)
        both = jnp.stack([seg_own, seg_pair])
        both_x = lax.ppermute(both, "seq", up_pairs)
        seg_keys = jnp.stack([both[0], both[1], both_x[0], both_x[1]])
        flips = jnp.arange(4, dtype=jnp.int32)
        near_enough = (seg_keys[:, :, -1] == seg_own[None, :, 0]) | (flips[:, None] == 0)
        need = (near_enough & (jnp.bitwise_xor(rank, flips)[:, None] <= rank)).astype(jnp.int32)
        first, turn, inv_attn, seg_keys, need = lax.optimization_barrier(
            (first, turn, inv_attn, seg_keys, need)
        )
        qkv_cols = q_cols + 2 * k_cols
        w_qkv = first[:, :qkv_cols]
        w_out_t = first[:, qkv_cols : qkv_cols + q_cols]
        gain_attn = first[:, qkv_cols + q_cols].astype(F32)
        gain_ffn = first[:, qkv_cols + q_cols + 64].astype(F32)
        gate_full, up_full, down_t = second[0], second[1], second[2]
        gain_heads = jnp.stack([norm_query, norm_key]).astype(F32)

        cot = lax.optimization_barrier(cotangent.reshape(total, width))

        normed_attn = (tokens * inv_attn * gain_attn).astype(BF16)
        raw = dot(normed_attn, w_qkv)
        queries, pairs = rope(raw, turn, gain_heads, q_cols, k_cols)

        cuts = [slice(step * rows, (step + 1) * rows) for step in range(MICRO)]
        kept = []
        middles = []
        heads_out = []
        for step in range(MICRO):
            cut = slice(step * rows, (step + 1) * rows)
            own = pairs[cut]
            near = lax.ppermute(own, "seq", pair)
            far = lax.ppermute(own, "seq", up_pairs)
            far_near = lax.ppermute(far, "seq", pair)
            parts = (own, near, far, far_near)
            attn_heads, log_sum = attend(
                need[:, step],
                queries,
                step,
                parts,
                seg_own[step][:, None],
                seg_keys[:, step],
                k_cols,
                group,
                rows,
            )
            heads_out.append(attn_heads)
            kept.append((parts, log_sum))
            attn_part = rdot(attn_heads, w_out_t)
            middles.append(tokens[cut] + mp_sum(attn_part))
        middle = jnp.concatenate(middles, axis=0)
        attn_heads = jnp.concatenate(heads_out, axis=0)

        inv_ffn = inv_rms(middle)
        normed_ffn = (middle * inv_ffn * gain_ffn).astype(BF16)
        gate = dot(normed_ffn, gate_full)
        upward = dot(normed_ffn, up_full)
        sigma = jax.nn.sigmoid(gate)
        silu = gate * sigma
        act = (silu * upward).astype(BF16)
        down_grad = tdot(cot, act).astype(BF16)
        down_grad = with_layout_constraint(down_grad, Layout((0, 1)))
        down_owned = scatter(down_grad)
        cot_late, act, down_grad = lax.optimization_barrier((cot, act, down_grad))
        grad_act = dot(cot_late, down_t)
        grad_gate_in = (grad_act * upward * sigma * (1.0 + gate * (1.0 - sigma))).astype(BF16)
        grad_up_in = (grad_act * silu).astype(BF16)
        backs = []
        for step in range(MICRO):
            cut = slice(step * rows, (step + 1) * rows)
            backs.append(
                mp_part(rdot(grad_gate_in[cut], gate_full) + rdot(grad_up_in[cut], up_full))
            )
        late, mine = lax.optimization_barrier((normed_ffn, backs[0][0]))
        backs[0] = (mine, backs[0][1])
        ffn_rel = relative(late, rank, dp_size, seq_size)
        up_block = pair_stage(ffn_rel, grad_up_in)
        gate_grad = tdot(normed_ffn, grad_gate_in).astype(BF16)
        gate_owned = scatter(gate_grad)
        down_mine = lax.optimization_barrier(rdot(act, down_t).astype(BF16))
        backs, gate_grad, up_block, down_mine = lax.optimization_barrier(
            (backs, gate_grad, up_block, down_mine)
        )
        down_other = mp_other(down_mine)
        gain_ffn_part = jnp.concatenate([mine for mine, _ in backs], axis=0).astype(F32)
        gain_ffn_part = jnp.sum(gain_ffn_part * middle * inv_ffn, axis=0)
        backs = [mine.astype(F32) + other.astype(F32) for mine, other in backs]
        grad_normed_ffn = jnp.concatenate(backs, axis=0)
        grad_middle = cot.astype(F32) + norm_back(grad_normed_ffn, middle, inv_ffn, gain_ffn)
        grad_middle_b = grad_middle.astype(BF16)
        grad_heads = dot(grad_middle_b, w_out_t).astype(BF16)
        out_owned = scatter(tdot(grad_middle_b, attn_heads).astype(BF16))
        up_block = cross_stage(up_block)

        grads_in = []
        head_sums = []
        sides = []
        for step in range(MICRO):
            parts, log_sum = kept[step]
            grad_q, d_own, d_near, d_far, d_far_near = attend_back(
                need[:, step],
                queries,
                grad_heads,
                heads_out[step],
                step,
                parts,
                seg_own[step][None],
                seg_keys[:, step].T,
                log_sum,
                k_cols,
                group,
                rows,
            )
            got = lax.ppermute(d_near, "seq", pair)
            got_far = lax.ppermute(d_far_near, "seq", pair)
            far = lax.ppermute(
                (d_far + got_far.astype(F32)).astype(BF16), "seq", down_pairs
            )
            if step == 0:
                up_block, d_own = lax.optimization_barrier((up_block, d_own))
                up_pieces = line_stage(up_block)
            sides.append((grad_q, d_own, got, far))
        for step in range(MICRO):
            side = sides[step]
            if step == 0:
                down_other, up_pieces[1], side = lax.optimization_barrier(
                    (down_other, up_pieces[1], side)
                )
            else:
                down_owned, up_pieces[2], side = lax.optimization_barrier(
                    (down_owned, up_pieces[2], side)
                )
            grad_in, sums = rope_back(raw, turn, gain_heads, *side, step, q_cols, k_cols)
            grads_in.append(grad_in)
            head_sums.append(sums)
        layer_out = (middle + (down_mine.astype(F32) + down_other.astype(F32))).astype(BF16)
        backs = [mp_part(rdot(grad_in, w_qkv)) for grad_in in grads_in]
        grad_qkv_in = jnp.concatenate(grads_in, axis=0)
        unit = [(tokens[cut] * inv_attn[cut]) for cut in cuts]
        gain_attn_part = sum(
            jnp.sum(back[0].astype(F32) * part, axis=0) for back, part in zip(backs, unit)
        )
        grad_qkv_in, gate_owned, up_pieces[3:], layer_out, gain_attn_part, backs[0], mine = (
            lax.optimization_barrier(
                (
                    grad_qkv_in,
                    gate_owned,
                    up_pieces[3:],
                    layer_out,
                    gain_attn_part,
                    backs[0],
                    backs[1][0],
                )
            )
        )
        backs[1] = (mine, backs[1][1])
        qkv_owned = scatter(tdot(normed_attn, grad_qkv_in).astype(BF16))
        head_sum = (head_sums[0] + head_sums[1]).reshape(-1)
        small = jnp.concatenate([gain_attn_part, gain_ffn_part, head_sum]).reshape(-1, HEAD)
        small = butterfly(small, "seq", seq_size)
        small = butterfly(small, "dp", dp_size)
        small = butterfly(small, "mp", mp_size)

        def finish(back, cut):
            grads = back[0].astype(F32) + back[1].astype(F32)
            return (
                grad_middle[cut] + norm_back(grads, tokens[cut], inv_attn[cut], gain_attn)
            ).astype(BF16)

        early = finish(backs[0], cuts[0])
        early, small, out_owned, backs[1] = lax.optimization_barrier(
            (early, small, out_owned, backs[1])
        )
        up_owned = sum(piece.astype(F32) for piece in up_pieces)
        grad_tokens = jnp.stack([early, finish(backs[1], cuts[1])])
        small = small.reshape(-1)
        head_sum = small[2 * width :]
        owner = (lax.axis_index("dp") * seq_size + rank) * own_rows
        wide_sum = small[: 2 * width].reshape(2, width)
        wide_sum = lax.dynamic_slice_in_dim(wide_sum, owner, own_rows, 1)

        qkv_owned = qkv_owned.astype(F32)
        return (
            layer_out.reshape(MICRO, 1, rows, width),
            grad_tokens.reshape(MICRO, 1, rows, width),
            qkv_owned[:, :q_cols],
            qkv_owned[:, q_cols : q_cols + k_cols],
            qkv_owned[:, q_cols + k_cols :],
            out_owned.T.astype(F32),
            gate_owned.astype(F32),
            up_owned.astype(F32),
            down_owned.T.astype(F32),
            wide_sum[0],
            wide_sum[1],
            head_sum[:HEAD],
            head_sum[HEAD:],
        )

    return local


def solution(mesh):
    return jax.shard_map(
        make_local(mesh.shape["mp"], mesh.shape["seq"], mesh.shape["dp"]),
        mesh=mesh,
        in_specs=(
            P(None, "dp", "seq", None),
            P(("dp", "seq"), "mp"),
            P(("dp", "seq"), "mp"),
            P(("dp", "seq"), "mp"),
            P("mp", ("dp", "seq")),
            P(("dp", "seq"), "mp"),
            P(("dp", "seq"), "mp"),
            P("mp", ("dp", "seq")),
            P(("dp", "seq")),
            P(("dp", "seq")),
            P(),
            P(),
            P(None, "dp", "seq"),
            P(None, "dp", "seq"),
            P(None, "dp", "seq", None),
        ),
        out_specs=(
            P(None, "dp", "seq", None),
            P(None, "dp", "seq", None),
            P(("dp", "seq"), "mp"),
            P(("dp", "seq"), "mp"),
            P(("dp", "seq"), "mp"),
            P("mp", ("dp", "seq")),
            P(("dp", "seq"), "mp"),
            P(("dp", "seq"), "mp"),
            P("mp", ("dp", "seq")),
            P(("dp", "seq")),
            P(("dp", "seq")),
            P(),
            P(),
        ),
        check_vma=False,
    )
```

```python
import functools

import jax
import jax.numpy as jnp
from jax import lax
from jax.experimental import pallas as pl
from jax.experimental.layout import Layout, with_layout_constraint
from jax.experimental.pallas import tpu as pltpu
from jax.sharding import PartitionSpec as P

HEADS = 16
KV_HEADS = 8
HEAD = 128
MICRO = 2

EPS = 1e-06
ROPE_BASE = 1000000.0
F32 = jnp.float32
BF16 = jnp.bfloat16
SCALE = HEAD ** (-0.5)
EXP2_SCALE = SCALE * 1.4426950408889634


def dot(left, right):
    return jnp.dot(left, right, preferred_element_type=F32)


def tdot(left, right):
    return lax.dot_general(left, right, (((0,), (0,)), ((), ())), preferred_element_type=F32)


def rdot(left, right):
    return lax.dot_general(left, right, (((1,), (1,)), ((), ())), preferred_element_type=F32)


def norm_back(grads, values, inverse, gain):
    scaled = grads * gain
    return inverse * scaled - values * inverse**3 * jnp.mean(
        scaled * values, axis=-1, keepdims=True
    )


def inv_rms(values):
    return lax.rsqrt(jnp.mean(values * values, axis=-1, keepdims=True) + EPS)


def forward_kernel(tile, group, need, q, k0,v0,k1,v1,k2,v2,k3,v3, seg_q, seg_k, out, log_sum, acc, den):
    rows=q.shape[0]
    tiles=[(g,t) for g in range(group) for t in range(rows//tile)]
    def run(flip, k, v):
        for g,t in tiles:
            cut=slice(t*tile,(t+1)*tile)
            n=(t+1)*tile if flip==0 else rows
            s=rdot(q[cut,g*HEAD:(g+1)*HEAD], k[:n,:])
            ok=seg_q[cut,:]==seg_k[flip:flip+1,:n]
            if flip==0:
                ok&=(lax.broadcasted_iota(jnp.int32,(tile,n),0)+t*tile)>=lax.broadcasted_iota(jnp.int32,(tile,n),1)
            e=jnp.where(ok,jnp.exp2(s*EXP2_SCALE),0.0)
            mixed=dot(e.astype(BF16),v[:n,:])
            total=jnp.sum(e,axis=1,keepdims=True)
            at=slice(g*rows+t*tile,g*rows+(t+1)*tile)
            if flip==0:
                acc[at,:]=mixed; den[at,:]=total
            else:
                acc[at,:]+=mixed; den[at,:]+=total
    run(0,k0,v0)
    for flip,(k,v) in ((1,(k1,v1)),(2,(k2,v2)),(3,(k3,v3))):
        pl.when(need[flip]>0)(functools.partial(run,flip,k,v))
    for g in range(group):
        at=slice(g*rows,(g+1)*rows)
        out[:,g*HEAD:(g+1)*HEAD]=(acc[at,:]/den[at,:]).astype(out.dtype)
    log_sum[0] = jnp.transpose(jnp.broadcast_to(jnp.log2(den[...]), (group * rows, HEAD)))[0:1]

def attend(need, queries, step, parts, seg_q, seg_k, k_cols, group, tile=256):
    rows=parts[0].shape[0]; kv=k_cols//HEAD
    kspec=pl.BlockSpec((rows,HEAD),lambda h,n:(0,h))
    vspec=pl.BlockSpec((rows,HEAD),lambda h,n:(0,h+kv))
    return pl.pallas_call(
        functools.partial(forward_kernel,tile,group),
        grid_spec=pltpu.PrefetchScalarGridSpec(
            num_scalar_prefetch=1, grid=(kv,),
            in_specs=[pl.BlockSpec((rows,group*HEAD),lambda h,n:(step,h))]+[kspec,vspec]*4+[
                pl.BlockSpec((rows,1),lambda h,n:(0,0)), pl.BlockSpec((4,rows),lambda h,n:(0,0))],
            out_specs=[pl.BlockSpec((rows,group*HEAD),lambda h,n:(0,h)), pl.BlockSpec((1,1,group*rows),lambda h,n:(h,0,0))],
            scratch_shapes=[pltpu.VMEM((group*rows,HEAD),F32),pltpu.VMEM((group*rows,1),F32)]),
        out_shape=[jax.ShapeDtypeStruct((rows,kv*group*HEAD),BF16),jax.ShapeDtypeStruct((kv,1,group*rows),F32)],
        name="attend",
    )(need,queries,*[p for part in parts for p in (part,part)],seg_q,seg_k)

def backward_kernel(tile, group, need, q, g_out, heads, k0,v0,k1,v1,k2,v2,k3,v3, seg_q, seg_k, log_sum, dq, d0,d1,d2,d3, acc, delta):
    rows=q.shape[0]
    ones=jnp.ones((8,HEAD),F32)
    for g in range(group):
        lanes=slice(g*HEAD,(g+1)*HEAD)
        product=g_out[:,lanes].astype(F32)*heads[:,lanes].astype(F32)
        delta[:,g*rows:(g+1)*rows]=lax.dot_general(ones,product,(((1,),(1,)),((),())),precision=lax.Precision.HIGHEST,preferred_element_type=F32)
    tiles=[(g,t) for g in range(group) for t in range(rows//tile)]
    def run(flip,k,v,d,dk_acc,dv_acc):
        for idx,(g,t) in enumerate(tiles):
            cut=slice(t*tile,(t+1)*tile)
            at=slice(g*rows+t*tile,g*rows+(t+1)*tile)
            n=(t+1)*tile if flip==0 else rows
            qt=q[cut,g*HEAD:(g+1)*HEAD]; dt=g_out[cut,g*HEAD:(g+1)*HEAD]
            kn=k[:n,:]
            s=rdot(kn,qt)
            ok=seg_k[:n,flip:flip+1]==seg_q[:,cut]
            if flip==0:
                ok&=(lax.broadcasted_iota(jnp.int32,(n,tile),1)+t*tile)>=lax.broadcasted_iota(jnp.int32,(n,tile),0)
            p=jnp.where(ok,jnp.exp2(s*EXP2_SCALE-log_sum[0,0:1,at]),0.0)
            dp=rdot(v[:n,:],dt)
            ds=(p*(dp-delta[0:1,at])).astype(BF16)
            dv=dot(p.astype(BF16),dt)
            dk=dot(ds,qt)
            if idx==0:
                dk_acc[...]=jnp.zeros_like(dk_acc); dv_acc[...]=jnp.zeros_like(dv_acc)
            dk_acc[:n,:]+=dk
            dv_acc[:n,:]+=dv
            back=tdot(ds,kn)*SCALE
            o=(cut,slice(g*HEAD,(g+1)*HEAD))
            if flip==0: dq[o]=back
            else: dq[o]+=back
        d[0]=(dk_acc[...]*SCALE).astype(d.dtype)
        d[1]=dv_acc[...].astype(d.dtype)
    run(0,k0,v0,d0,acc.at[0],acc.at[1])
    for flip,(k,v,d) in ((1,(k1,v1,d1)),(2,(k2,v2,d2)),(3,(k3,v3,d3))):
        pl.when(need[flip]>0)(functools.partial(run,flip,k,v,d,acc.at[0],acc.at[1]))
        def clear(d=d): d[...]=jnp.zeros_like(d)
        pl.when(need[flip]<=0)(clear)

def attend_back(need, queries, grad_heads, heads, step, parts, seg_q, seg_k, log_sum, k_cols, group, tile=256):
    rows=parts[0].shape[0]; kv=k_cols//HEAD
    kspec=pl.BlockSpec((rows,HEAD),lambda h,n:(0,h))
    vspec=pl.BlockSpec((rows,HEAD),lambda h,n:(0,h+kv))
    qspec=pl.BlockSpec((rows,group*HEAD),lambda h,n:(step,h))
    dspec=pl.BlockSpec((2,rows,HEAD),lambda h,n:(0,0,h))
    types=(F32,BF16,F32,BF16)
    return pl.pallas_call(
        functools.partial(backward_kernel,tile,group),
        grid_spec=pltpu.PrefetchScalarGridSpec(
            num_scalar_prefetch=1, grid=(kv,),
            in_specs=[qspec,qspec,pl.BlockSpec((rows,group*HEAD),lambda h,n:(0,h))]+[kspec,vspec]*4+[
                pl.BlockSpec((1,rows),lambda h,n:(0,0)), pl.BlockSpec((rows,4),lambda h,n:(0,0)),
                pl.BlockSpec((1,1,group*rows),lambda h,n:(h,0,0))],
            out_specs=[pl.BlockSpec((rows,group*HEAD),lambda h,n:(0,h))]+[dspec]*4,
            scratch_shapes=[pltpu.VMEM((2,rows,HEAD),F32),pltpu.VMEM((8,group*rows),F32)]),
        out_shape=[jax.ShapeDtypeStruct((rows,kv*group*HEAD),F32)]+[jax.ShapeDtypeStruct((2,rows,k_cols),t) for t in types],
        name="attend_back",
    )(need,queries,grad_heads,heads,*[p for part in parts for p in (part,part)],seg_q,seg_k,log_sum)


def rope_kernel(q_heads, k_heads, raw, turn, gains, queries, pairs):
    cosine, sine = turn[0], turn[1]
    for head in range(q_heads + k_heads):
        values = raw[:, head * HEAD : (head + 1) * HEAD]
        inverse = lax.rsqrt(jnp.mean(values * values, axis=-1, keepdims=True) + EPS)
        gain = gains[0:1] if head < q_heads else gains[1:2]
        scaled = values * inverse * gain
        turned = (scaled * cosine + pltpu.roll(scaled, HEAD // 2, 1) * sine).astype(BF16)
        if head < q_heads:
            queries[:, head * HEAD : (head + 1) * HEAD] = turned
        else:
            at = head - q_heads
            pairs[:, at * HEAD : (at + 1) * HEAD] = turned
    cols = (q_heads + k_heads) * HEAD
    pairs[:, k_heads * HEAD :] = raw[:, cols:].astype(BF16)


def rope(raw, turn, gains, q_cols, k_cols, block=256):
    total = raw.shape[0]
    return pl.pallas_call(
        functools.partial(rope_kernel, q_cols // HEAD, k_cols // HEAD),
        grid=(total // block,),
        in_specs=[
            pl.BlockSpec((block, raw.shape[1]), lambda i: (i, 0)),
            pl.BlockSpec((2, block, HEAD), lambda i: (0, i, 0)),
            pl.BlockSpec((2, HEAD), lambda i: (0, 0)),
        ],
        out_specs=[
            pl.BlockSpec((block, q_cols), lambda i: (i, 0)),
            pl.BlockSpec((block, 2 * k_cols), lambda i: (i, 0)),
        ],
        out_shape=[
            jax.ShapeDtypeStruct((total, q_cols), BF16),
            jax.ShapeDtypeStruct((total, 2 * k_cols), BF16),
        ],
        name="rope",
    )(raw, turn, gains)


def rope_back_kernel(q_heads, k_heads, raw, turn, gains, dq, d_own, d_near, d_far, out, sums):
    cosine, sine = turn[0], turn[1]

    @pl.when(pl.program_id(0) == 0)
    def _():
        sums[...] = jnp.zeros_like(sums)

    for head in range(q_heads + k_heads):
        lanes = slice(head * HEAD, (head + 1) * HEAD)
        which = 0 if head < q_heads else 1
        if which == 0:
            grads = dq[:, lanes]
        else:
            at = slice((head - q_heads) * HEAD, (head - q_heads + 1) * HEAD)
            grads = d_own[0, :, at] + d_near[0, :, at].astype(F32) + d_far[0, :, at].astype(F32)
        values = raw[:, lanes]
        inverse = lax.rsqrt(jnp.mean(values * values, axis=-1, keepdims=True) + EPS)
        unit = values * inverse
        turned = grads * cosine - pltpu.roll(grads, HEAD // 2, 1) * sine
        sums[which : which + 1] += jnp.sum(turned * unit, axis=0, keepdims=True)
        scaled = turned * gains[which : which + 1]
        mean = jnp.mean(scaled * unit, axis=-1, keepdims=True)
        out[:, lanes] = (inverse * (scaled - unit * mean)).astype(BF16)
    cols = (q_heads + k_heads) * HEAD
    out[:, cols:] = (d_own[1] + d_near[1].astype(F32) + d_far[1].astype(F32)).astype(BF16)


def rope_back(raw, turn, gains, dq, d_own, d_near, d_far, step, q_cols, k_cols, block=256):
    rows = dq.shape[0]
    base = step * (rows // block)
    cols = q_cols + 2 * k_cols
    dspec = pl.BlockSpec((2, block, k_cols), lambda i: (0, i, 0))
    return pl.pallas_call(
        functools.partial(rope_back_kernel, q_cols // HEAD, k_cols // HEAD),
        grid=(rows // block,),
        in_specs=[
            pl.BlockSpec((block, cols), lambda i: (base + i, 0)),
            pl.BlockSpec((2, block, HEAD), lambda i: (0, base + i, 0)),
            pl.BlockSpec((2, HEAD), lambda i: (0, 0)),
            pl.BlockSpec((block, q_cols), lambda i: (i, 0)),
            dspec,
            dspec,
            dspec,
        ],
        out_specs=[
            pl.BlockSpec((block, cols), lambda i: (i, 0)),
            pl.BlockSpec((2, HEAD), lambda i: (0, 0)),
        ],
        out_shape=[
            jax.ShapeDtypeStruct((rows, cols), BF16),
            jax.ShapeDtypeStruct((2, HEAD), F32),
        ],
        name="rope_back",
    )(raw, turn, gains, dq, d_own, d_near, d_far)


def move_kernel(rank, source, out):
    out[...] = source[...]


def relative(values, rank, dp_size, seq_size):
    total, width = values.shape
    lanes = width // (dp_size * seq_size)

    def pick(step, rank):
        turn = step // dp_size
        flip = (turn % 2) * 2 + turn // 2
        return (0, (step % dp_size) * seq_size + jnp.bitwise_xor(rank[0], flip))

    return pl.pallas_call(
        move_kernel,
        grid_spec=pltpu.PrefetchScalarGridSpec(
            num_scalar_prefetch=1,
            grid=(dp_size * seq_size,),
            in_specs=[pl.BlockSpec((total, lanes), pick)],
            out_specs=pl.BlockSpec((total, lanes), lambda step, rank: (0, step)),
        ),
        out_shape=jax.ShapeDtypeStruct(values.shape, values.dtype),
        name="relative",
    )(rank.reshape(1).astype(jnp.int32), values)


def make_local(mp_size, seq_size, dp_size):
    data_axes = ("dp", "seq")
    pair = [(i, i ^ 1) for i in range(seq_size)]
    up_pairs = [(i, i + 2) for i in range(seq_size - 2)]
    down_pairs = [(i + 2, i) for i in range(seq_size - 2)]
    cross = [(i, i ^ 2) for i in range(seq_size)]

    def scatter(grad):
        return lax.psum_scatter(grad, data_axes, scatter_dimension=0, tiled=True)

    def mp_other(part):
        if mp_size == 2:
            return lax.ppermute(part, "mp", [(0, 1), (1, 0)])
        return (lax.psum(part.astype(F32), "mp") - part.astype(F32)).astype(BF16)

    def mp_part(part):
        part = lax.optimization_barrier(part.astype(BF16))
        return part, mp_other(part)

    def pair_stage(left, right):
        half = left.shape[1] // 2
        theirs = tdot(left[:, half:], right).astype(BF16)
        got = lax.ppermute(theirs, "seq", pair)
        return (tdot(left[:, :half], right) + got.astype(F32)).astype(BF16)

    def cross_stage(block):
        half = block.shape[0] // 2
        got = lax.ppermute(block[half:], "seq", cross)
        return (block[:half].astype(F32) + got.astype(F32)).astype(BF16)

    def line_stage(block):
        place = lax.axis_index("dp")
        blocks = block.reshape(dp_size, -1, block.shape[1])
        pieces = [lax.dynamic_index_in_dim(blocks, place, 0, False)]
        for flip in range(1, dp_size):
            sent = lax.dynamic_index_in_dim(blocks, jnp.bitwise_xor(place, flip), 0, False)
            pieces.append(lax.ppermute(sent, "dp", [(i, i ^ flip) for i in range(dp_size)]))
        return pieces

    def butterfly(value, axis, size):
        flip = 1
        while flip < size:
            moves = [(i, i ^ flip) for i in range(size)]
            value = value + lax.ppermute(value, axis, moves)
            flip *= 2
        return value

    def mp_sum(part):
        mine, other = mp_part(part)
        return mine.astype(F32) + other.astype(F32)

    def local(
        hidden,
        w_query,
        w_key,
        w_value,
        w_out,
        w_gate,
        w_up,
        w_down,
        norm_attn,
        norm_ffn,
        norm_query,
        norm_key,
        segments,
        positions,
        cotangent,
    ):
        rows = hidden.shape[2]
        width = hidden.shape[3]
        total = MICRO * rows
        q_cols = w_query.shape[1]
        k_cols = w_key.shape[1]
        group = HEADS // KV_HEADS
        rank = lax.axis_index("seq")
        own_rows = w_query.shape[0]

        gains = jnp.concatenate(
            [
                jnp.broadcast_to(norm_attn[:, None], (own_rows, 64)),
                jnp.broadcast_to(norm_ffn[:, None], (own_rows, 64)),
            ],
            axis=1,
        )
        first = jnp.concatenate([w_query, w_key, w_value, w_out.T, gains], axis=1)
        first = lax.all_gather(first, data_axes, axis=0, tiled=True)
        second = jnp.stack([w_gate, w_up, w_down.T])
        second, first = lax.optimization_barrier((second, first))
        second = lax.all_gather(second, data_axes, axis=1, tiled=True)
        tokens = hidden.reshape(total, width).astype(F32)
        inv_attn = inv_rms(tokens)
        frequency = ROPE_BASE ** (-(jnp.arange(HEAD // 2, dtype=F32) * 2.0) / HEAD)
        angles = positions.reshape(total).astype(F32)[:, None] * frequency[None, :]
        cosine = jnp.cos(angles)
        sine = jnp.sin(angles)
        turn = jnp.stack(
            [
                jnp.concatenate([cosine, cosine], axis=-1),
                jnp.concatenate([-sine, sine], axis=-1),
            ]
        )
        seg_own = segments[:, 0]
        seg_pair = lax.ppermute(seg_own, "seq", pair)
        both = jnp.stack([seg_own, seg_pair])
        both_x = lax.ppermute(both, "seq", up_pairs)
        seg_keys = jnp.stack([both[0], both[1], both_x[0], both_x[1]])
        flips = jnp.arange(4, dtype=jnp.int32)
        near_enough = (seg_keys[:, :, -1] == seg_own[None, :, 0]) | (flips[:, None] == 0)
        need = (near_enough & (jnp.bitwise_xor(rank, flips)[:, None] <= rank)).astype(jnp.int32)
        first, turn, inv_attn, seg_keys, need = lax.optimization_barrier(
            (first, turn, inv_attn, seg_keys, need)
        )
        qkv_cols = q_cols + 2 * k_cols
        w_qkv = first[:, :qkv_cols]
        w_out_t = first[:, qkv_cols : qkv_cols + q_cols]
        gain_attn = first[:, qkv_cols + q_cols].astype(F32)
        gain_ffn = first[:, qkv_cols + q_cols + 64].astype(F32)
        gate_full, up_full, down_t = second[0], second[1], second[2]
        gain_heads = jnp.stack([norm_query, norm_key]).astype(F32)

        cot = lax.optimization_barrier(cotangent.reshape(total, width))

        normed_attn = (tokens * inv_attn * gain_attn).astype(BF16)
        raw = dot(normed_attn, w_qkv)
        queries, pairs = rope(raw, turn, gain_heads, q_cols, k_cols)

        cuts = [slice(step * rows, (step + 1) * rows) for step in range(MICRO)]
        kept = []
        middles = []
        heads_out = []
        for step in range(MICRO):
            cut = slice(step * rows, (step + 1) * rows)
            own = pairs[cut]
            near = lax.ppermute(own, "seq", pair)
            far = lax.ppermute(own, "seq", up_pairs)
            far_near = lax.ppermute(far, "seq", pair)
            parts = (own, near, far, far_near)
            attn_heads, log_sum = attend(
                need[:, step],
                queries,
                step,
                parts,
                seg_own[step][:, None],
                seg_keys[:, step],
                k_cols,
                group,
                rows,
            )
            heads_out.append(attn_heads)
            kept.append((parts, log_sum))
            attn_part = rdot(attn_heads, w_out_t)
            middles.append(tokens[cut] + mp_sum(attn_part))
        middle = jnp.concatenate(middles, axis=0)
        attn_heads = jnp.concatenate(heads_out, axis=0)

        inv_ffn = inv_rms(middle)
        normed_ffn = (middle * inv_ffn * gain_ffn).astype(BF16)
        gate = dot(normed_ffn, gate_full)
        upward = dot(normed_ffn, up_full)
        sigma = jax.nn.sigmoid(gate)
        silu = gate * sigma
        act = (silu * upward).astype(BF16)
        down_grad = tdot(cot, act).astype(BF16)
        down_grad = with_layout_constraint(down_grad, Layout((0, 1)))
        down_owned = scatter(down_grad)
        cot_late, act, down_grad = lax.optimization_barrier((cot, act, down_grad))
        grad_act = dot(cot_late, down_t)
        grad_gate_in = (grad_act * upward * sigma * (1.0 + gate * (1.0 - sigma))).astype(BF16)
        grad_up_in = (grad_act * silu).astype(BF16)
        backs = []
        for step in range(MICRO):
            cut = slice(step * rows, (step + 1) * rows)
            backs.append(
                mp_part(rdot(grad_gate_in[cut], gate_full) + rdot(grad_up_in[cut], up_full))
            )
        late, mine = lax.optimization_barrier((normed_ffn, backs[0][0]))
        backs[0] = (mine, backs[0][1])
        ffn_rel = relative(late, rank, dp_size, seq_size)
        up_block = pair_stage(ffn_rel, grad_up_in)
        gate_grad = tdot(normed_ffn, grad_gate_in).astype(BF16)
        gate_owned = scatter(gate_grad)
        down_mine = lax.optimization_barrier(rdot(act, down_t).astype(BF16))
        backs, gate_grad, _, down_mine = lax.optimization_barrier(
            (backs, gate_grad, up_block, down_mine)
        )
        down_other = mp_other(down_mine)
        gain_ffn_part = jnp.concatenate([mine for mine, _ in backs], axis=0).astype(F32)
        gain_ffn_part = jnp.sum(gain_ffn_part * middle * inv_ffn, axis=0)
        backs = [mine.astype(F32) + other.astype(F32) for mine, other in backs]
        grad_normed_ffn = jnp.concatenate(backs, axis=0)
        grad_middle = cot.astype(F32) + norm_back(grad_normed_ffn, middle, inv_ffn, gain_ffn)
        grad_middle_b = grad_middle.astype(BF16)
        grad_heads = dot(grad_middle_b, w_out_t).astype(BF16)
        out_owned = scatter(tdot(grad_middle_b, attn_heads).astype(BF16))
        up_block = cross_stage(up_block)

        grads_in = []
        head_sums = []
        sides = []
        for step in range(MICRO):
            parts, log_sum = kept[step]
            grad_q, d_own, d_near, d_far, d_far_near = attend_back(
                need[:, step],
                queries,
                grad_heads,
                heads_out[step],
                step,
                parts,
                seg_own[step][None],
                seg_keys[:, step].T,
                log_sum,
                k_cols,
                group,
                rows,
            )
            got = lax.ppermute(d_near, "seq", pair)
            got_far = lax.ppermute(d_far_near, "seq", pair)
            far = lax.ppermute(
                (d_far + got_far.astype(F32)).astype(BF16), "seq", down_pairs
            )
            if step == 0:
                up_block, d_own = lax.optimization_barrier((up_block, d_own))
                up_pieces = line_stage(up_block)
            sides.append((grad_q, d_own, got, far))
        for step in range(MICRO):
            side = sides[step]
            if step == 0:
                down_other, up_pieces[1], side = lax.optimization_barrier(
                    (down_other, up_pieces[1], side)
                )
            else:
                down_owned, up_pieces[2], side = lax.optimization_barrier(
                    (down_owned, up_pieces[2], side)
                )
            grad_in, sums = rope_back(raw, turn, gain_heads, *side, step, q_cols, k_cols)
            grads_in.append(grad_in)
            head_sums.append(sums)
        layer_out = (middle + (down_mine.astype(F32) + down_other.astype(F32))).astype(BF16)
        backs = [mp_part(rdot(grad_in, w_qkv)) for grad_in in grads_in]
        grad_qkv_in = jnp.concatenate(grads_in, axis=0)
        unit = [(tokens[cut] * inv_attn[cut]) for cut in cuts]
        gain_attn_part = sum(
            jnp.sum(back[0].astype(F32) * part, axis=0) for back, part in zip(backs, unit)
        )
        grad_qkv_in, gate_owned, up_pieces[3:], layer_out, gain_attn_part, backs[0], mine = (
            lax.optimization_barrier(
                (
                    grad_qkv_in,
                    gate_owned,
                    up_pieces[3:],
                    layer_out,
                    gain_attn_part,
                    backs[0],
                    backs[1][0],
                )
            )
        )
        backs[1] = (mine, backs[1][1])
        qkv_owned = scatter(tdot(normed_attn, grad_qkv_in).astype(BF16))
        head_sum = (head_sums[0] + head_sums[1]).reshape(-1)
        small = jnp.concatenate([gain_attn_part, gain_ffn_part, head_sum]).reshape(-1, HEAD)
        small = butterfly(small, "seq", seq_size)
        small = butterfly(small, "dp", dp_size)
        small = butterfly(small, "mp", mp_size)

        def finish(back, cut):
            grads = back[0].astype(F32) + back[1].astype(F32)
            return (
                grad_middle[cut] + norm_back(grads, tokens[cut], inv_attn[cut], gain_attn)
            ).astype(BF16)

        early = finish(backs[0], cuts[0])
        early, small, out_owned, backs[1] = lax.optimization_barrier(
            (early, small, out_owned, backs[1])
        )
        up_owned = sum(piece.astype(F32) for piece in up_pieces)
        grad_tokens = jnp.stack([early, finish(backs[1], cuts[1])])
        small = small.reshape(-1)
        head_sum = small[2 * width :]
        owner = (lax.axis_index("dp") * seq_size + rank) * own_rows
        wide_sum = small[: 2 * width].reshape(2, width)
        wide_sum = lax.dynamic_slice_in_dim(wide_sum, owner, own_rows, 1)

        qkv_owned = qkv_owned.astype(F32)
        return (
            layer_out.reshape(MICRO, 1, rows, width),
            grad_tokens.reshape(MICRO, 1, rows, width),
            qkv_owned[:, :q_cols],
            qkv_owned[:, q_cols : q_cols + k_cols],
            qkv_owned[:, q_cols + k_cols :],
            out_owned.T.astype(F32),
            gate_owned.astype(F32),
            up_owned.astype(F32),
            down_owned.T.astype(F32),
            wide_sum[0],
            wide_sum[1],
            head_sum[:HEAD],
            head_sum[HEAD:],
        )

    return local


def solution(mesh):
    return jax.shard_map(
        make_local(mesh.shape["mp"], mesh.shape["seq"], mesh.shape["dp"]),
        mesh=mesh,
        in_specs=(
            P(None, "dp", "seq", None),
            P(("dp", "seq"), "mp"),
            P(("dp", "seq"), "mp"),
            P(("dp", "seq"), "mp"),
            P("mp", ("dp", "seq")),
            P(("dp", "seq"), "mp"),
            P(("dp", "seq"), "mp"),
            P("mp", ("dp", "seq")),
            P(("dp", "seq")),
            P(("dp", "seq")),
            P(),
            P(),
            P(None, "dp", "seq"),
            P(None, "dp", "seq"),
            P(None, "dp", "seq", None),
        ),
        out_specs=(
            P(None, "dp", "seq", None),
            P(None, "dp", "seq", None),
            P(("dp", "seq"), "mp"),
            P(("dp", "seq"), "mp"),
            P(("dp", "seq"), "mp"),
            P("mp", ("dp", "seq")),
            P(("dp", "seq"), "mp"),
            P(("dp", "seq"), "mp"),
            P("mp", ("dp", "seq")),
            P(("dp", "seq")),
            P(("dp", "seq")),
            P(),
            P(),
        ),
        check_vma=False,
    )
```

```python
import functools

import jax
import jax.numpy as jnp
from jax import lax
from jax.experimental import pallas as pl
from jax.experimental.layout import Layout, with_layout_constraint
from jax.experimental.pallas import tpu as pltpu
from jax.sharding import PartitionSpec as P

HEADS = 16
KV_HEADS = 8
HEAD = 128
MICRO = 2

EPS = 1e-06
ROPE_BASE = 1000000.0
F32 = jnp.float32
BF16 = jnp.bfloat16
SCALE = HEAD ** (-0.5)
EXP2_SCALE = SCALE * 1.4426950408889634


def dot(left, right):
    return jnp.dot(left, right, preferred_element_type=F32)


def tdot(left, right):
    return lax.dot_general(left, right, (((0,), (0,)), ((), ())), preferred_element_type=F32)


def rdot(left, right):
    return lax.dot_general(left, right, (((1,), (1,)), ((), ())), preferred_element_type=F32)


def norm_back(grads, values, inverse, gain):
    scaled = grads * gain
    return inverse * scaled - values * inverse**3 * jnp.mean(
        scaled * values, axis=-1, keepdims=True
    )


def inv_rms(values):
    return lax.rsqrt(jnp.mean(values * values, axis=-1, keepdims=True) + EPS)


def forward_kernel(tile, group, need, q, k0,v0,k1,v1,k2,v2,k3,v3, seg_q, seg_k, out, log_sum, acc, den):
    rows=q.shape[0]
    tiles=[(g,t) for g in range(group) for t in range(rows//tile)]
    def run(flip, k, v):
        for g,t in tiles:
            cut=slice(t*tile,(t+1)*tile)
            n=(t+1)*tile if flip==0 else rows
            s=rdot(q[cut,g*HEAD:(g+1)*HEAD], k[:n,:])
            ok=seg_q[cut,:]==seg_k[flip:flip+1,:n]
            if flip==0:
                ok&=(lax.broadcasted_iota(jnp.int32,(tile,n),0)+t*tile)>=lax.broadcasted_iota(jnp.int32,(tile,n),1)
            e=jnp.where(ok,jnp.exp2(s*EXP2_SCALE),0.0)
            mixed=dot(e.astype(BF16),v[:n,:])
            total=jnp.sum(e,axis=1,keepdims=True)
            at=slice(g*rows+t*tile,g*rows+(t+1)*tile)
            if flip==0:
                acc[at,:]=mixed; den[at,:]=total
            else:
                acc[at,:]+=mixed; den[at,:]+=total
    run(0,k0,v0)
    for flip,(k,v) in ((1,(k1,v1)),(2,(k2,v2)),(3,(k3,v3))):
        pl.when(need[flip]>0)(functools.partial(run,flip,k,v))
    for g in range(group):
        at=slice(g*rows,(g+1)*rows)
        out[:,g*HEAD:(g+1)*HEAD]=(acc[at,:]/den[at,:]).astype(out.dtype)
    log_sum[0] = jnp.transpose(jnp.broadcast_to(jnp.log2(den[...]), (group * rows, HEAD)))[0:1]

def attend(need, queries, step, parts, seg_q, seg_k, k_cols, group, tile=256):
    rows=parts[0].shape[0]; kv=k_cols//HEAD
    kspec=pl.BlockSpec((rows,HEAD),lambda h,n:(0,h))
    vspec=pl.BlockSpec((rows,HEAD),lambda h,n:(0,h+kv))
    return pl.pallas_call(
        functools.partial(forward_kernel,tile,group),
        grid_spec=pltpu.PrefetchScalarGridSpec(
            num_scalar_prefetch=1, grid=(kv,),
            in_specs=[pl.BlockSpec((rows,group*HEAD),lambda h,n:(step,h))]+[kspec,vspec]*4+[
                pl.BlockSpec((rows,1),lambda h,n:(0,0)), pl.BlockSpec((4,rows),lambda h,n:(0,0))],
            out_specs=[pl.BlockSpec((rows,group*HEAD),lambda h,n:(0,h)), pl.BlockSpec((1,1,group*rows),lambda h,n:(h,0,0))],
            scratch_shapes=[pltpu.VMEM((group*rows,HEAD),F32),pltpu.VMEM((group*rows,1),F32)]),
        out_shape=[jax.ShapeDtypeStruct((rows,kv*group*HEAD),BF16),jax.ShapeDtypeStruct((kv,1,group*rows),F32)],
        name="attend",
    )(need,queries,*[p for part in parts for p in (part,part)],seg_q,seg_k)

def backward_kernel(tile, group, need, q, g_out, heads, k0,v0,k1,v1,k2,v2,k3,v3, seg_q, seg_k, log_sum, dq, d0,d1,d2,d3, acc, delta):
    rows=q.shape[0]
    ones=jnp.ones((8,HEAD),F32)
    for g in range(group):
        lanes=slice(g*HEAD,(g+1)*HEAD)
        product=g_out[:,lanes].astype(F32)*heads[:,lanes].astype(F32)
        delta[:,g*rows:(g+1)*rows]=lax.dot_general(ones,product,(((1,),(1,)),((),())),precision=lax.Precision.HIGHEST,preferred_element_type=F32)
    tiles=[(g,t) for g in range(group) for t in range(rows//tile)]
    def run(flip,k,v,d,dk_acc,dv_acc):
        for idx,(g,t) in enumerate(tiles):
            cut=slice(t*tile,(t+1)*tile)
            at=slice(g*rows+t*tile,g*rows+(t+1)*tile)
            n=(t+1)*tile if flip==0 else rows
            qt=q[cut,g*HEAD:(g+1)*HEAD]; dt=g_out[cut,g*HEAD:(g+1)*HEAD]
            kn=k[:n,:]
            s=rdot(kn,qt)
            ok=seg_k[:n,flip:flip+1]==seg_q[:,cut]
            if flip==0:
                ok&=(lax.broadcasted_iota(jnp.int32,(n,tile),1)+t*tile)>=lax.broadcasted_iota(jnp.int32,(n,tile),0)
            p=jnp.where(ok,jnp.exp2(s*EXP2_SCALE-log_sum[0,0:1,at]),0.0)
            dp=rdot(v[:n,:],dt)
            ds=(p*(dp-delta[0:1,at])).astype(BF16)
            dv=dot(p.astype(BF16),dt)
            dk=dot(ds,qt)
            if idx==0:
                dk_acc[...]=jnp.zeros_like(dk_acc); dv_acc[...]=jnp.zeros_like(dv_acc)
            dk_acc[:n,:]+=dk
            dv_acc[:n,:]+=dv
            back=tdot(ds,kn)*SCALE
            o=(cut,slice(g*HEAD,(g+1)*HEAD))
            if flip==0: dq[o]=back
            else: dq[o]+=back
        d[0]=(dk_acc[...]*SCALE).astype(d.dtype)
        d[1]=dv_acc[...].astype(d.dtype)
    run(0,k0,v0,d0,acc.at[0],acc.at[1])
    for flip,(k,v,d) in ((1,(k1,v1,d1)),(2,(k2,v2,d2)),(3,(k3,v3,d3))):
        pl.when(need[flip]>0)(functools.partial(run,flip,k,v,d,acc.at[0],acc.at[1]))
        def clear(d=d): d[...]=jnp.zeros_like(d)
        pl.when(need[flip]<=0)(clear)

def attend_back(need, queries, grad_heads, heads, step, parts, seg_q, seg_k, log_sum, k_cols, group, tile=256):
    rows=parts[0].shape[0]; kv=k_cols//HEAD
    kspec=pl.BlockSpec((rows,HEAD),lambda h,n:(0,h))
    vspec=pl.BlockSpec((rows,HEAD),lambda h,n:(0,h+kv))
    qspec=pl.BlockSpec((rows,group*HEAD),lambda h,n:(step,h))
    dspec=pl.BlockSpec((2,rows,HEAD),lambda h,n:(0,0,h))
    types=(F32,BF16,F32,BF16)
    return pl.pallas_call(
        functools.partial(backward_kernel,tile,group),
        grid_spec=pltpu.PrefetchScalarGridSpec(
            num_scalar_prefetch=1, grid=(kv,),
            in_specs=[qspec,qspec,pl.BlockSpec((rows,group*HEAD),lambda h,n:(0,h))]+[kspec,vspec]*4+[
                pl.BlockSpec((1,rows),lambda h,n:(0,0)), pl.BlockSpec((rows,4),lambda h,n:(0,0)),
                pl.BlockSpec((1,1,group*rows),lambda h,n:(h,0,0))],
            out_specs=[pl.BlockSpec((rows,group*HEAD),lambda h,n:(0,h))]+[dspec]*4,
            scratch_shapes=[pltpu.VMEM((2,rows,HEAD),F32),pltpu.VMEM((8,group*rows),F32)]),
        out_shape=[jax.ShapeDtypeStruct((rows,kv*group*HEAD),F32)]+[jax.ShapeDtypeStruct((2,rows,k_cols),t) for t in types],
        name="attend_back",
    )(need,queries,grad_heads,heads,*[p for part in parts for p in (part,part)],seg_q,seg_k,log_sum)


def rope_kernel(q_heads, k_heads, raw, turn, gains, queries, pairs):
    cosine, sine = turn[0], turn[1]
    for head in range(q_heads + k_heads):
        values = raw[:, head * HEAD : (head + 1) * HEAD]
        inverse = lax.rsqrt(jnp.mean(values * values, axis=-1, keepdims=True) + EPS)
        gain = gains[0:1] if head < q_heads else gains[1:2]
        scaled = values * inverse * gain
        turned = (scaled * cosine + pltpu.roll(scaled, HEAD // 2, 1) * sine).astype(BF16)
        if head < q_heads:
            queries[:, head * HEAD : (head + 1) * HEAD] = turned
        else:
            at = head - q_heads
            pairs[:, at * HEAD : (at + 1) * HEAD] = turned
    cols = (q_heads + k_heads) * HEAD
    pairs[:, k_heads * HEAD :] = raw[:, cols:].astype(BF16)


def rope(raw, turn, gains, q_cols, k_cols, block=256):
    total = raw.shape[0]
    return pl.pallas_call(
        functools.partial(rope_kernel, q_cols // HEAD, k_cols // HEAD),
        grid=(total // block,),
        in_specs=[
            pl.BlockSpec((block, raw.shape[1]), lambda i: (i, 0)),
            pl.BlockSpec((2, block, HEAD), lambda i: (0, i, 0)),
            pl.BlockSpec((2, HEAD), lambda i: (0, 0)),
        ],
        out_specs=[
            pl.BlockSpec((block, q_cols), lambda i: (i, 0)),
            pl.BlockSpec((block, 2 * k_cols), lambda i: (i, 0)),
        ],
        out_shape=[
            jax.ShapeDtypeStruct((total, q_cols), BF16),
            jax.ShapeDtypeStruct((total, 2 * k_cols), BF16),
        ],
        name="rope",
    )(raw, turn, gains)


def rope_back_kernel(q_heads, k_heads, raw, turn, gains, dq, d_own, d_near, d_far, out, sums):
    cosine, sine = turn[0], turn[1]

    @pl.when(pl.program_id(0) == 0)
    def _():
        sums[...] = jnp.zeros_like(sums)

    for head in range(q_heads + k_heads):
        lanes = slice(head * HEAD, (head + 1) * HEAD)
        which = 0 if head < q_heads else 1
        if which == 0:
            grads = dq[:, lanes]
        else:
            at = slice((head - q_heads) * HEAD, (head - q_heads + 1) * HEAD)
            grads = d_own[0, :, at] + d_near[0, :, at].astype(F32) + d_far[0, :, at].astype(F32)
        values = raw[:, lanes]
        inverse = lax.rsqrt(jnp.mean(values * values, axis=-1, keepdims=True) + EPS)
        unit = values * inverse
        turned = grads * cosine - pltpu.roll(grads, HEAD // 2, 1) * sine
        sums[which : which + 1] += jnp.sum(turned * unit, axis=0, keepdims=True)
        scaled = turned * gains[which : which + 1]
        mean = jnp.mean(scaled * unit, axis=-1, keepdims=True)
        out[:, lanes] = (inverse * (scaled - unit * mean)).astype(BF16)
    cols = (q_heads + k_heads) * HEAD
    out[:, cols:] = (d_own[1] + d_near[1].astype(F32) + d_far[1].astype(F32)).astype(BF16)


def rope_back(raw, turn, gains, dq, d_own, d_near, d_far, step, q_cols, k_cols, block=256):
    rows = dq.shape[0]
    base = step * (rows // block)
    cols = q_cols + 2 * k_cols
    dspec = pl.BlockSpec((2, block, k_cols), lambda i: (0, i, 0))
    return pl.pallas_call(
        functools.partial(rope_back_kernel, q_cols // HEAD, k_cols // HEAD),
        grid=(rows // block,),
        in_specs=[
            pl.BlockSpec((block, cols), lambda i: (base + i, 0)),
            pl.BlockSpec((2, block, HEAD), lambda i: (0, base + i, 0)),
            pl.BlockSpec((2, HEAD), lambda i: (0, 0)),
            pl.BlockSpec((block, q_cols), lambda i: (i, 0)),
            dspec,
            dspec,
            dspec,
        ],
        out_specs=[
            pl.BlockSpec((block, cols), lambda i: (i, 0)),
            pl.BlockSpec((2, HEAD), lambda i: (0, 0)),
        ],
        out_shape=[
            jax.ShapeDtypeStruct((rows, cols), BF16),
            jax.ShapeDtypeStruct((2, HEAD), F32),
        ],
        name="rope_back",
    )(raw, turn, gains, dq, d_own, d_near, d_far)


def move_kernel(rank, source, out):
    out[...] = source[...]


def relative(values, rank, dp_size, seq_size):
    total, width = values.shape
    lanes = width // (dp_size * seq_size)

    def pick(step, rank):
        turn = step // dp_size
        flip = (turn % 2) * 2 + turn // 2
        return (0, (step % dp_size) * seq_size + jnp.bitwise_xor(rank[0], flip))

    return pl.pallas_call(
        move_kernel,
        grid_spec=pltpu.PrefetchScalarGridSpec(
            num_scalar_prefetch=1,
            grid=(dp_size * seq_size,),
            in_specs=[pl.BlockSpec((total, lanes), pick)],
            out_specs=pl.BlockSpec((total, lanes), lambda step, rank: (0, step)),
        ),
        out_shape=jax.ShapeDtypeStruct(values.shape, values.dtype),
        name="relative",
    )(rank.reshape(1).astype(jnp.int32), values)


def make_local(mp_size, seq_size, dp_size):
    data_axes = ("dp", "seq")
    pair = [(i, i ^ 1) for i in range(seq_size)]
    up_pairs = [(i, i + 2) for i in range(seq_size - 2)]
    down_pairs = [(i + 2, i) for i in range(seq_size - 2)]
    cross = [(i, i ^ 2) for i in range(seq_size)]

    def scatter(grad):
        return lax.psum_scatter(grad, data_axes, scatter_dimension=0, tiled=True)

    def mp_other(part):
        if mp_size == 2:
            return lax.ppermute(part, "mp", [(0, 1), (1, 0)])
        return (lax.psum(part.astype(F32), "mp") - part.astype(F32)).astype(BF16)

    def mp_part(part):
        part = lax.optimization_barrier(part.astype(BF16))
        return part, mp_other(part)

    def pair_stage(left, right):
        half = left.shape[1] // 2
        theirs = tdot(left[:, half:], right).astype(BF16)
        got = lax.ppermute(theirs, "seq", pair)
        return (tdot(left[:, :half], right) + got.astype(F32)).astype(BF16)

    def cross_stage(block):
        half = block.shape[0] // 2
        got = lax.ppermute(block[half:], "seq", cross)
        return (block[:half].astype(F32) + got.astype(F32)).astype(BF16)

    def line_stage(block):
        place = lax.axis_index("dp")
        blocks = block.reshape(dp_size, -1, block.shape[1])
        pieces = [lax.dynamic_index_in_dim(blocks, place, 0, False)]
        for flip in range(1, dp_size):
            sent = lax.dynamic_index_in_dim(blocks, jnp.bitwise_xor(place, flip), 0, False)
            pieces.append(lax.ppermute(sent, "dp", [(i, i ^ flip) for i in range(dp_size)]))
        return pieces

    def butterfly(value, axis, size):
        flip = 1
        while flip < size:
            moves = [(i, i ^ flip) for i in range(size)]
            value = value + lax.ppermute(value, axis, moves)
            flip *= 2
        return value

    def mp_sum(part):
        mine, other = mp_part(part)
        return mine.astype(F32) + other.astype(F32)

    def local(
        hidden,
        w_query,
        w_key,
        w_value,
        w_out,
        w_gate,
        w_up,
        w_down,
        norm_attn,
        norm_ffn,
        norm_query,
        norm_key,
        segments,
        positions,
        cotangent,
    ):
        rows = hidden.shape[2]
        width = hidden.shape[3]
        total = MICRO * rows
        q_cols = w_query.shape[1]
        k_cols = w_key.shape[1]
        group = HEADS // KV_HEADS
        rank = lax.axis_index("seq")
        own_rows = w_query.shape[0]

        gains = jnp.concatenate(
            [
                jnp.broadcast_to(norm_attn[:, None], (own_rows, 64)),
                jnp.broadcast_to(norm_ffn[:, None], (own_rows, 64)),
            ],
            axis=1,
        )
        first = jnp.concatenate([w_query, w_key, w_value, w_out.T, gains], axis=1)
        first = lax.all_gather(first, data_axes, axis=0, tiled=True)
        second = jnp.stack([w_gate, w_up])
        second, first = lax.optimization_barrier((second, first))
        second = lax.all_gather(second, data_axes, axis=1, tiled=True)
        tokens = hidden.reshape(total, width).astype(F32)
        inv_attn = inv_rms(tokens)
        frequency = ROPE_BASE ** (-(jnp.arange(HEAD // 2, dtype=F32) * 2.0) / HEAD)
        angles = positions.reshape(total).astype(F32)[:, None] * frequency[None, :]
        cosine = jnp.cos(angles)
        sine = jnp.sin(angles)
        turn = jnp.stack(
            [
                jnp.concatenate([cosine, cosine], axis=-1),
                jnp.concatenate([-sine, sine], axis=-1),
            ]
        )
        seg_own = segments[:, 0]
        seg_pair = lax.ppermute(seg_own, "seq", pair)
        both = jnp.stack([seg_own, seg_pair])
        both_x = lax.ppermute(both, "seq", up_pairs)
        seg_keys = jnp.stack([both[0], both[1], both_x[0], both_x[1]])
        flips = jnp.arange(4, dtype=jnp.int32)
        near_enough = (seg_keys[:, :, -1] == seg_own[None, :, 0]) | (flips[:, None] == 0)
        need = (near_enough & (jnp.bitwise_xor(rank, flips)[:, None] <= rank)).astype(jnp.int32)
        first, turn, inv_attn, seg_keys, need = lax.optimization_barrier(
            (first, turn, inv_attn, seg_keys, need)
        )
        qkv_cols = q_cols + 2 * k_cols
        w_qkv = first[:, :qkv_cols]
        w_out_t = first[:, qkv_cols : qkv_cols + q_cols]
        gain_attn = first[:, qkv_cols + q_cols].astype(F32)
        gain_ffn = first[:, qkv_cols + q_cols + 64].astype(F32)
        gate_full, up_full = second[0], second[1]
        gain_heads = jnp.stack([norm_query, norm_key]).astype(F32)

        cot = lax.optimization_barrier(cotangent.reshape(total, width))

        normed_attn = (tokens * inv_attn * gain_attn).astype(BF16)
        raw = dot(normed_attn, w_qkv)
        down_own, raw = lax.optimization_barrier((w_down.T, raw))
        down_t = lax.all_gather(down_own, data_axes, axis=0, tiled=True)
        queries, pairs = rope(raw, turn, gain_heads, q_cols, k_cols)

        cuts = [slice(step * rows, (step + 1) * rows) for step in range(MICRO)]
        kept = []
        middles = []
        heads_out = []
        for step in range(MICRO):
            cut = slice(step * rows, (step + 1) * rows)
            own = pairs[cut]
            near = lax.ppermute(own, "seq", pair)
            far = lax.ppermute(own, "seq", up_pairs)
            far_near = lax.ppermute(far, "seq", pair)
            parts = (own, near, far, far_near)
            attn_heads, log_sum = attend(
                need[:, step],
                queries,
                step,
                parts,
                seg_own[step][:, None],
                seg_keys[:, step],
                k_cols,
                group,
                rows,
            )
            heads_out.append(attn_heads)
            kept.append((parts, log_sum))
            attn_part = rdot(attn_heads, w_out_t)
            middles.append(tokens[cut] + mp_sum(attn_part))
        middle = jnp.concatenate(middles, axis=0)
        attn_heads = jnp.concatenate(heads_out, axis=0)

        inv_ffn = inv_rms(middle)
        normed_ffn = (middle * inv_ffn * gain_ffn).astype(BF16)
        gate = dot(normed_ffn, gate_full)
        upward = dot(normed_ffn, up_full)
        sigma = jax.nn.sigmoid(gate)
        silu = gate * sigma
        act = (silu * upward).astype(BF16)
        down_grad = tdot(cot, act).astype(BF16)
        down_grad = with_layout_constraint(down_grad, Layout((0, 1)))
        down_owned = scatter(down_grad)
        cot_late, act, down_grad = lax.optimization_barrier((cot, act, down_grad))
        grad_act = dot(cot_late, down_t)
        grad_gate_in = (grad_act * upward * sigma * (1.0 + gate * (1.0 - sigma))).astype(BF16)
        grad_up_in = (grad_act * silu).astype(BF16)
        backs = []
        for step in range(MICRO):
            cut = slice(step * rows, (step + 1) * rows)
            backs.append(
                mp_part(rdot(grad_gate_in[cut], gate_full) + rdot(grad_up_in[cut], up_full))
            )
        late, mine = lax.optimization_barrier((normed_ffn, backs[0][0]))
        backs[0] = (mine, backs[0][1])
        ffn_rel = relative(late, rank, dp_size, seq_size)
        up_block = pair_stage(ffn_rel, grad_up_in)
        gate_grad = tdot(normed_ffn, grad_gate_in).astype(BF16)
        gate_owned = scatter(gate_grad)
        down_mine = lax.optimization_barrier(rdot(act, down_t).astype(BF16))
        backs, gate_grad, _, down_mine = lax.optimization_barrier(
            (backs, gate_grad, up_block, down_mine)
        )
        down_other = mp_other(down_mine)
        gain_ffn_part = jnp.concatenate([mine for mine, _ in backs], axis=0).astype(F32)
        gain_ffn_part = jnp.sum(gain_ffn_part * middle * inv_ffn, axis=0)
        backs = [mine.astype(F32) + other.astype(F32) for mine, other in backs]
        grad_normed_ffn = jnp.concatenate(backs, axis=0)
        grad_middle = cot.astype(F32) + norm_back(grad_normed_ffn, middle, inv_ffn, gain_ffn)
        grad_middle_b = grad_middle.astype(BF16)
        grad_heads = dot(grad_middle_b, w_out_t).astype(BF16)
        out_owned = scatter(tdot(grad_middle_b, attn_heads).astype(BF16))
        up_block = cross_stage(up_block)

        grads_in = []
        head_sums = []
        sides = []
        for step in range(MICRO):
            parts, log_sum = kept[step]
            grad_q, d_own, d_near, d_far, d_far_near = attend_back(
                need[:, step],
                queries,
                grad_heads,
                heads_out[step],
                step,
                parts,
                seg_own[step][None],
                seg_keys[:, step].T,
                log_sum,
                k_cols,
                group,
                rows,
            )
            got = lax.ppermute(d_near, "seq", pair)
            got_far = lax.ppermute(d_far_near, "seq", pair)
            far = lax.ppermute(
                (d_far + got_far.astype(F32)).astype(BF16), "seq", down_pairs
            )
            if step == 0:
                up_block, d_own = lax.optimization_barrier((up_block, d_own))
                up_pieces = line_stage(up_block)
            sides.append((grad_q, d_own, got, far))
        for step in range(MICRO):
            side = sides[step]
            if step == 0:
                down_other, up_pieces[1], side = lax.optimization_barrier(
                    (down_other, up_pieces[1], side)
                )
            else:
                down_owned, up_pieces[2], side = lax.optimization_barrier(
                    (down_owned, up_pieces[2], side)
                )
            grad_in, sums = rope_back(raw, turn, gain_heads, *side, step, q_cols, k_cols)
            grads_in.append(grad_in)
            head_sums.append(sums)
        layer_out = (middle + (down_mine.astype(F32) + down_other.astype(F32))).astype(BF16)
        backs = [mp_part(rdot(grad_in, w_qkv)) for grad_in in grads_in]
        grad_qkv_in = jnp.concatenate(grads_in, axis=0)
        unit = [(tokens[cut] * inv_attn[cut]) for cut in cuts]
        gain_attn_part = sum(
            jnp.sum(back[0].astype(F32) * part, axis=0) for back, part in zip(backs, unit)
        )
        grad_qkv_in, gate_owned, up_pieces[3:], layer_out, gain_attn_part, backs[0], mine = (
            lax.optimization_barrier(
                (
                    grad_qkv_in,
                    gate_owned,
                    up_pieces[3:],
                    layer_out,
                    gain_attn_part,
                    backs[0],
                    backs[1][0],
                )
            )
        )
        backs[1] = (mine, backs[1][1])
        qkv_owned = scatter(tdot(normed_attn, grad_qkv_in).astype(BF16))
        head_sum = (head_sums[0] + head_sums[1]).reshape(-1)
        small = jnp.concatenate([gain_attn_part, gain_ffn_part, head_sum]).reshape(-1, HEAD)
        small = butterfly(small, "seq", seq_size)
        small = butterfly(small, "dp", dp_size)
        small = butterfly(small, "mp", mp_size)

        def finish(back, cut):
            grads = back[0].astype(F32) + back[1].astype(F32)
            return (
                grad_middle[cut] + norm_back(grads, tokens[cut], inv_attn[cut], gain_attn)
            ).astype(BF16)

        early = finish(backs[0], cuts[0])
        early, small, out_owned, backs[1] = lax.optimization_barrier(
            (early, small, out_owned, backs[1])
        )
        up_owned = sum(piece.astype(F32) for piece in up_pieces)
        grad_tokens = jnp.stack([early, finish(backs[1], cuts[1])])
        small = small.reshape(-1)
        head_sum = small[2 * width :]
        owner = (lax.axis_index("dp") * seq_size + rank) * own_rows
        wide_sum = small[: 2 * width].reshape(2, width)
        wide_sum = lax.dynamic_slice_in_dim(wide_sum, owner, own_rows, 1)

        qkv_owned = qkv_owned.astype(F32)
        return (
            layer_out.reshape(MICRO, 1, rows, width),
            grad_tokens.reshape(MICRO, 1, rows, width),
            qkv_owned[:, :q_cols],
            qkv_owned[:, q_cols : q_cols + k_cols],
            qkv_owned[:, q_cols + k_cols :],
            out_owned.T.astype(F32),
            gate_owned.astype(F32),
            up_owned.astype(F32),
            down_owned.T.astype(F32),
            wide_sum[0],
            wide_sum[1],
            head_sum[:HEAD],
            head_sum[HEAD:],
        )

    return local


def solution(mesh):
    return jax.shard_map(
        make_local(mesh.shape["mp"], mesh.shape["seq"], mesh.shape["dp"]),
        mesh=mesh,
        in_specs=(
            P(None, "dp", "seq", None),
            P(("dp", "seq"), "mp"),
            P(("dp", "seq"), "mp"),
            P(("dp", "seq"), "mp"),
            P("mp", ("dp", "seq")),
            P(("dp", "seq"), "mp"),
            P(("dp", "seq"), "mp"),
            P("mp", ("dp", "seq")),
            P(("dp", "seq")),
            P(("dp", "seq")),
            P(),
            P(),
            P(None, "dp", "seq"),
            P(None, "dp", "seq"),
            P(None, "dp", "seq", None),
        ),
        out_specs=(
            P(None, "dp", "seq", None),
            P(None, "dp", "seq", None),
            P(("dp", "seq"), "mp"),
            P(("dp", "seq"), "mp"),
            P(("dp", "seq"), "mp"),
            P("mp", ("dp", "seq")),
            P(("dp", "seq"), "mp"),
            P(("dp", "seq"), "mp"),
            P("mp", ("dp", "seq")),
            P(("dp", "seq")),
            P(("dp", "seq")),
            P(),
            P(),
        ),
        check_vma=False,
    )
```
